32 devices in a mesh: grp: 2 (over y), sp: 4 (over z), sec: 2 (over x), mb: 2 (over core).
Axes of the slice: x: 2, y: 2, z: 4, core: 2. Of those that a mesh axis runs over, the one named last changes fastest.
Arguments:
- atmosphere: bfloat16 [8, 24, 32, 256], P(('grp', 'mb'), None, 'sp', 'sec'), parts along dimension 0, may hold values from -6 to 6
- ocean_state: bfloat16 [8, 8, 32, 128], P(('grp', 'mb'), None, 'sp'), parts along dimension 0, may hold values from -6 to 6
- fluxes: bfloat16 [8, 8, 32, 128], P(('grp', 'mb'), None, 'sp'), parts along dimension 0, may hold values from -6 to 6
- sea_mask: int32 [32, 128], P('sp'), may hold values 0 or 1
- air_entry: bfloat16 [3, 3, 32, 136], replicated, may hold values from -0.375 to 0.375
- air_middle: bfloat16 [3, 3, 136, 136], replicated, may hold values from -0.15625 to 0.15625
- air_exit: bfloat16 [3, 3, 136, 32], replicated, may hold values from -0.15625 to 0.15625
- sea_entry: bfloat16 [3, 3, 16, 136], replicated, may hold values from -0.5 to 0.5
- sea_exit: bfloat16 [3, 3, 136, 8], replicated, may hold values from -0.15625 to 0.15625
Outputs:
- air_final: bfloat16 [8, 24, 32, 256], P(('grp', 'mb'), None, 'sp', 'sec'), parts along dimension 0
- sea_final: bfloat16 [8, 8, 32, 128], P(('grp', 'mb'), None, 'sp'), parts along dimension 0
The draws below stay inside these ranges and needn't reach their ends.
There are 2 independent parts, one for each index of `grp`. The reference program is written for one: setup_inputs(seed, part) draws one part's arguments, and reference() takes and returns one part's arrays. A program takes and returns all parts, laid end to end along the dimension named above; an argument that names none is the same for every part. Nothing has to cross between parts.
All inputs are finite; a program needn't handle non-finite values. No bound on the sum of `sea_mask` on one device may be relied on, other than what follows from the above.
Results may differ from the reference program's by a relative error of at most 0.0055.
Values may be sent and summed in bfloat16 or wider, within the bound.
No kernel may reach another device: no remote copies, remote signals or barrier semaphores. Data moves between devices by JAX's collectives and lax.ppermute only.
A program may use at most 64 MiB of HBM per device.

```python
import jax
import jax.numpy as jnp
from jax import lax

FIELDS = 24
SURFACE = 8
FLUX = 8
HIDDEN_SIZE = 136
STEPS = 2
MEMBERS = 4
ROWS = 32
OCEAN_COLS = 128
AIR_COLS = 256


def touch_ends(values, own_key, least, largest):
    extent = values.shape
    index_at = [jax.random.randint(jax.random.fold_in(own_key, axis), (), 0, extent[axis]) for axis in range(len(extent))]
    values = values.at[tuple(index_at)].set(least)
    longest = extent.index(max(extent))
    index_at[longest] = (index_at[longest] + 1) % extent[longest]
    return values.at[tuple(index_at)].set(largest)


def block_scale(stream_key, shape, shards, low, top_value):
    loudness = 1.0
    for dim, shards_of in shards:
        steps = jax.random.uniform(jax.random.fold_in(jax.random.fold_in(stream_key, 6), dim), (shards_of,), jnp.float32, low / len(shards), top_value / len(shards))
        loudness = loudness * jnp.repeat(jnp.exp(steps), shape[dim] // shards_of).reshape((-1,) + (1,) * (len(shape) - 1 - dim))
    return loudness


def gaussian(rng, dims, scale, limit, cuts=(), held_as=jnp.bfloat16):
    level = block_scale(rng, dims, cuts, -0.22, 0.18) if cuts else 1.0
    drawn = jax.random.normal(rng, dims, jnp.float32) * scale * level
    return jnp.minimum(jnp.maximum(drawn, -limit), limit).astype(held_as)


def setup_inputs(seed: int = 0, part: int = 0) -> dict:
    keys = jax.random.split(jax.random.key(seed), 10)
    part_splits = jax.random.split(jax.random.fold_in(keys[9], part), 10)
    return {
        "atmosphere": gaussian(part_splits[0], (MEMBERS, FIELDS, ROWS, AIR_COLS), 1.0, 6.0, ((0, 2), (2, 4), (3, 2))),
        "ocean_state": gaussian(part_splits[1], (MEMBERS, SURFACE, ROWS, OCEAN_COLS), 1.0, 6.0, ((0, 2), (2, 4))),
        "fluxes": gaussian(part_splits[2], (MEMBERS, FLUX, ROWS, OCEAN_COLS), 1.0, 6.0, ((0, 2), (2, 4))),
        "sea_mask": touch_ends((jax.random.randint(keys[3], (ROWS, OCEAN_COLS), 0, 3) < 2).astype(jnp.int32), jax.random.fold_in(keys[3], 1), 0, 1),
        "air_entry": gaussian(keys[4], (3, 3, FIELDS + SURFACE, HIDDEN_SIZE), (9 * (FIELDS + SURFACE)) ** -0.5, 0.375),
        "air_middle": gaussian(keys[5], (3, 3, HIDDEN_SIZE, HIDDEN_SIZE), (9 * HIDDEN_SIZE) ** -0.5, 0.15625),
        "air_exit": gaussian(keys[6], (3, 3, HIDDEN_SIZE, FIELDS + FLUX), (9 * HIDDEN_SIZE) ** -0.5, 0.15625),
        "sea_entry": gaussian(keys[7], (3, 3, SURFACE + FLUX, HIDDEN_SIZE), (9 * (SURFACE + FLUX)) ** -0.5, 0.5),
        "sea_exit": gaussian(keys[8], (3, 3, HIDDEN_SIZE, SURFACE), (9 * HIDDEN_SIZE) ** -0.5, 0.15625),
    }


def wrap_rows(field, spread):
    return jnp.concatenate([field[:, -spread:], field, field[:, :spread]], axis=1)


def pad_columns(field, spread):
    return jnp.pad(field, ((0, 0), (0, 0), (spread, spread)))


def convolve(field, weight, dilation):
    wrapped = wrap_rows(field, dilation)
    produced = lax.conv_general_dilated(wrapped[None], weight.astype(jnp.float32), (1, 1), "VALID", rhs_dilation=(dilation, dilation), dimension_numbers=("NCHW", "HWIO", "NCHW"), precision=lax.Precision.HIGHEST)
    return produced[0]


def sea_member(state, flux_now, sea_weight, sea_entry, sea_exit):
    entry = jnp.concatenate([state, flux_now], axis=0).astype(jnp.float32)
    hidden = jax.nn.gelu(convolve(pad_columns(entry, 1), sea_entry, 1), approximate=True).astype(jnp.bfloat16)
    hidden = lax.optimization_barrier(hidden)
    produced = convolve(pad_columns(hidden.astype(jnp.float32), 1), sea_exit, 1)
    return (state.astype(jnp.float32) + sea_weight * produced).astype(jnp.bfloat16)


def air_member(state, surface_now, air_entry, air_middle, air_exit):
    extra_cols = AIR_COLS - OCEAN_COLS
    surface_wide = jnp.concatenate([surface_now, jnp.zeros((SURFACE, ROWS, extra_cols), surface_now.dtype)], axis=2)
    entry = jnp.concatenate([state, surface_wide], axis=0).astype(jnp.float32)
    hidden = convolve(pad_columns(entry, 1), air_entry, 1)[:, :, :OCEAN_COLS]
    hidden = jax.nn.gelu(hidden, approximate=True).astype(jnp.bfloat16)
    hidden = lax.optimization_barrier(hidden)
    hidden = jax.nn.gelu(convolve(pad_columns(hidden.astype(jnp.float32), 2), air_middle, 2), approximate=True).astype(jnp.bfloat16)
    hidden = lax.optimization_barrier(hidden)
    produced = convolve(pad_columns(hidden.astype(jnp.float32), 4), air_exit, 4)
    renewed = (state[:, :, :OCEAN_COLS].astype(jnp.float32) + produced[:FIELDS]).astype(jnp.bfloat16)
    new_state = jnp.concatenate([renewed, state[:, :, OCEAN_COLS:]], axis=2)
    return new_state, produced[FIELDS:].astype(jnp.bfloat16)


def reference(atmosphere, ocean_state, fluxes, sea_mask, air_entry, air_middle, air_exit, sea_entry, sea_exit):
    sea_weight = sea_mask.astype(jnp.float32)

    def one_member(members):
        state, sea_now, flux_now = members
        for step_index in range(STEPS):
            sea_now = sea_member(sea_now, flux_now, sea_weight, sea_entry, sea_exit)
            state, flux_now = air_member(state, sea_now, air_entry, air_middle, air_exit)
        return state, sea_now

    air_final, sea_final = lax.map(one_member, (atmosphere, ocean_state, fluxes))
    return air_final, sea_final
```

```python
import functools

import jax
import jax.numpy as jnp
from jax import lax
from jax.experimental import pallas as pl
from jax.experimental.pallas import tpu as pltpu
from jax.sharding import PartitionSpec as P

STEPS = 2


dilations = (1, 2, 4)


def with_halo(block, sides, width):
    for axis, dim in sides:
        count = lax.axis_size(axis)
        forward = [(i, i + 1) for i in range(count - 1)]
        forward.append((count - 1, 0))
        backward = [(target, source) for source, target in forward]
        low = lax.ppermute(
            lax.slice_in_dim(block, block.shape[dim] - width, None, axis=dim), axis, forward
        )
        high = lax.ppermute(lax.slice_in_dim(block, 0, width, axis=dim), axis, backward)
        block = jnp.concatenate([low, block, high], axis=dim)
    return block


def spread_2(value, axis, source):
    kept = jnp.where(lax.axis_index(axis) == source, value, 0).astype(value.dtype)
    return lax.psum(kept, axis)


def tap_sum(source, weight, dilation):
    out_rows = source.shape[2] - 2 * dilation
    out_cols = source.shape[3] - 2 * dilation
    pieces = []
    for tap_row in range(3):
        for tap_col in range(3):
            sliced = lax.slice_in_dim(
                source, tap_row * dilation, tap_row * dilation + out_rows, axis=2
            )
            sliced = lax.slice_in_dim(
                sliced, tap_col * dilation, tap_col * dilation + out_cols, axis=3
            )
            pieces.append(sliced)
    stacked = jnp.concatenate(pieces, axis=1)
    flat_weight = weight.reshape(-1, weight.shape[3])
    return jnp.einsum("mkrc,ko->morc", stacked, flat_weight, preferred_element_type=jnp.float32)


def gelu_round(values):
    return jax.nn.gelu(values, approximate=True).astype(jnp.bfloat16)


def keep_columns(block, first_column, limit):
    columns = lax.iota(jnp.int32, block.shape[3]) + first_column
    inside = (columns >= 0) & (columns < limit)
    return jnp.where(inside[None, None, None, :], block, jnp.zeros_like(block))


def shards(
    atmosphere, ocean_state, fluxes, sea_mask, air_entry, air_middle, air_exit, sea_entry, sea_exit
):
    sections = lax.axis_size("sec")
    position = lax.axis_index("sec")
    is_ocean = position == sections - 1
    band_cols = atmosphere.shape[3]
    ocean_cols = ocean_state.shape[3]
    field_count = atmosphere.shape[1]
    sea_weight = sea_mask.astype(jnp.float32)
    air_weights = (air_entry, air_middle, air_exit)
    sea_weights = (sea_entry, sea_exit)

    def air_layer(extended, layer_index):
        produced = tap_sum(extended, air_weights[layer_index], dilations[layer_index])
        if layer_index < 2:
            return gelu_round(produced)
        return produced

    def air_blank(extended, layer_index):
        spread = dilations[layer_index]
        out_shape = (
            extended.shape[0],
            air_weights[layer_index].shape[3],
            extended.shape[2] - 2 * spread,
            extended.shape[3] - 2 * spread,
        )
        return jnp.zeros(out_shape, jnp.bfloat16 if layer_index < 2 else jnp.float32)

    def sea_layer(extended, layer_index):
        padded = jnp.pad(extended, ((0, 0), (0, 0), (0, 0), (1, 1)))
        produced = tap_sum(padded, sea_weights[layer_index], 1)
        if layer_index < 1:
            return gelu_round(produced)
        return produced

    def sea_blank(extended, layer_index):
        out_shape = (
            extended.shape[0],
            sea_weights[layer_index].shape[3],
            extended.shape[2] - 2,
            ocean_cols,
        )
        return jnp.zeros(out_shape, jnp.bfloat16 if layer_index < 1 else jnp.float32)

    def air_extend(current, layer_index, margin):
        extended = with_halo(current, (("sp", 2), ("sec", 3)), dilations[layer_index])
        margin = dilations[layer_index]
        limit = band_cols * sections if layer_index == 0 else ocean_cols
        extended = keep_columns(extended, position * band_cols - margin, limit)
        return (extended, margin - dilations[layer_index])

    def sea_extend(current):
        return with_halo(current, (("sp", 2),), 1)

    def run_segment(air_job, sea_job):
        air_current = None
        sea_current = None
        margin = 0
        if air_job is not None:
            air_current = jnp.concatenate(air_job, axis=1)
        if sea_job is not None:
            sea_current = jnp.concatenate(sea_job, axis=1)
        for layer_index in range(3):
            air_ready = None
            sea_ready = None
            if air_current is not None:
                air_ready, margin = air_extend(air_current, layer_index, margin)
            if sea_current is not None and layer_index < 2:
                sea_ready = sea_extend(sea_current)
            if air_ready is None and sea_ready is None:
                continue

            def on_sea(ready):
                air_given, sea_given = ready
                air_made = None if air_given is None else air_blank(air_given, layer_index)
                sea_made = None if sea_given is None else sea_layer(sea_given, layer_index)
                return (air_made, sea_made)

            def on_air(ready):
                air_given, sea_given = ready
                air_made = None if air_given is None else air_layer(air_given, layer_index)
                sea_made = None if sea_given is None else sea_blank(sea_given, layer_index)
                return (air_made, sea_made)

            air_next, sea_next = lax.cond(is_ocean, on_sea, on_air, (air_ready, sea_ready))
            if air_ready is not None:
                air_current = air_next
            if sea_ready is not None:
                sea_current = sea_next
        air_result = None
        sea_result = None
        if air_job is not None:
            previous = air_job[0]
            renewed = (previous.astype(jnp.float32) + air_current[:, :field_count]).astype(
                jnp.bfloat16
            )
            air_result = (renewed, air_current[:, field_count:].astype(jnp.bfloat16))
        if sea_job is not None:
            previous = sea_job[0]
            sea_result = (
                previous.astype(jnp.float32) + sea_weight[None, None] * sea_current
            ).astype(jnp.bfloat16)
        return (air_result, sea_result)

    air_now, sea_now, flux_now = (atmosphere, ocean_state, fluxes)
    for step_index in range(STEPS):
        sea_now = run_segment(None, (sea_now, flux_now))[1]
        shared = spread_2(sea_now, "sec", sections - 1)
        start_col = jnp.minimum(position, sections - 2) * band_cols
        own_band = lax.dynamic_slice_in_dim(shared, start_col, band_cols, 3)
        own_band = jnp.where(is_ocean, jnp.zeros_like(own_band), own_band)
        sea_now = shared
        air_now, flux_band = run_segment((air_now, own_band), None)[0]
        if step_index + 1 < STEPS:
            collected = lax.all_gather(flux_band, "sec", axis=3, tiled=True)
            flux_now = collected[:, :, :, :ocean_cols]
    return (air_now, sea_now)


LANES = 128
SUBLANES = 8
PACKED = 16


def pad_to(count, unit):
    return -(-count // unit) * unit


def tree_add(terms):
    total = terms[0]
    for term in terms[1:]:
        total = total + term
    return total


def gelu(v):
    inner = v * (0.7978845608028654 + (0.7978845608028654 * 0.044715) * (v * v))
    half = 0.5 * v
    return half + half * jnp.tanh(inner)


def lane_ids(rows):
    return lax.broadcasted_iota(jnp.int32, (rows, LANES), 1)


def from_left(v, distance, fill=0.0):
    return jnp.where(lane_ids(v.shape[0]) < distance, fill, pltpu.roll(v, distance, 1))


def from_right(v, distance, fill=0.0):
    rolled = pltpu.roll(v, LANES - distance, 1)
    return jnp.where(lane_ids(v.shape[0]) >= LANES - distance, fill, rolled)


def vmem_specs(count):
    return [pl.BlockSpec(memory_space=pltpu.VMEM)] * count


def pack_kernel(sec_ref, air_ref, got_ref, sea_ref, flux_ref, mask_ref, out_ref, planes):
    fields = air_ref.shape[1]
    surface = sea_ref.shape[1]
    fluxes = flux_ref.shape[1]
    rows = air_ref.shape[2]
    first = sec_ref[0] == 0
    kept = fields + surface + fluxes
    got = got_ref[...].astype(jnp.float32)
    planes[0:fields] = jnp.where(first, air_ref[0].astype(jnp.float32), got)
    planes[kept : kept + fields] = jnp.where(first, got, air_ref[1].astype(jnp.float32))
    planes[fields : fields + surface] = jnp.where(
        first, sea_ref[0].astype(jnp.float32), sea_ref[1].astype(jnp.float32)
    )
    planes[fields + surface : kept] = jnp.where(
        first, flux_ref[0].astype(jnp.float32), flux_ref[1].astype(jnp.float32)
    )
    lanes = lane_ids(fields)
    edge = jnp.zeros((fields, LANES), jnp.float32)
    for row in range(rows):
        out_ref[:, row * LANES : (row + 1) * LANES] = planes[0:kept, row, :].astype(jnp.bfloat16)
        band = planes[kept : kept + fields, row, :]
        if row:
            band = pltpu.roll(band, row, 1)
        edge = jnp.where(lanes == row, band, edge)
    mask = mask_ref[...].astype(jnp.float32)
    rest = jnp.zeros((kept - fields - rows, LANES), jnp.float32)
    tail = jnp.concatenate([edge, mask, rest], axis=0)
    out_ref[:, rows * LANES : (rows + 1) * LANES] = tail.astype(jnp.bfloat16)


def weights_kernel(se_ref, sx_ref, ae_ref, am_ref, ax_ref, se_out, sx_out, ae_out, am_out, ax_out):
    for source, target in ((se_ref, se_out), (ae_ref, ae_out)):
        taps = [
            source[a, b].astype(jnp.float32).T for a in range(3) for b in range(3)
        ]
        target[...] = jnp.concatenate(taps, axis=1).astype(jnp.bfloat16)
    for source, target in ((sx_ref, sx_out), (am_ref, am_out), (ax_ref, ax_out)):
        depth, width = source.shape[2:]
        blank = jnp.zeros((width, pad_to(depth, PACKED) - depth), jnp.float32)
        groups = []
        for b in range(3):
            pieces = []
            for a in range(3):
                pieces += [source[a, b].astype(jnp.float32).T, blank]
            groups.append(jnp.concatenate(pieces, axis=1))
        target[...] = jnp.concatenate(groups, axis=0).astype(jnp.bfloat16)


def forecast_kernel(sizes, *refs):
    fields, surface, flux_count, hidden, blocks, rows = sizes
    block_refs = refs[:blocks]
    se_ref, sx_ref, ae_ref, am_ref, ax_ref, out_ref = refs[blocks : blocks + 6]
    sea_in, sea_hid, air_in, hid1, hid2, air_now, sea_now, edge_in, mask_in, planes = refs[blocks + 6 :]
    ring = blocks * rows
    kept = fields + surface + flux_count
    hidden_pad = sea_hid.shape[0] - hidden
    pads = {id(sea_in): 1, id(sea_hid): 1, id(air_in): 1, id(hid1): 2, id(hid2): 4}

    def at(buffer, row, count):
        start = row + pads.get(id(buffer), 0)
        if isinstance(row, int):
            return pl.ds(start * LANES, count * LANES)
        return pl.ds(pl.multiple_of(start * LANES, LANES), count * LANES)

    def close_ring(buffer):
        pad = pads[id(buffer)]
        buffer[:, 0 : pad * LANES] = buffer[:, ring * LANES : (ring + pad) * LANES]
        buffer[:, (ring + pad) * LANES :] = buffer[:, pad * LANES : 2 * pad * LANES]

    def store_sea_in(row, values):
        left, right = from_left(values, 1), from_right(values, 1)
        sea_in[:, at(sea_in, row, 1)] = jnp.concatenate([left, values, right], axis=0).astype(
            jnp.bfloat16
        )

    def store_air_in(row, values, edge):
        fill = jnp.concatenate([edge, jnp.zeros((surface, LANES), jnp.float32)], axis=0)
        left, right = from_left(values, 1), from_right(values, 1, fill)
        air_in[:, at(air_in, row, 1)] = jnp.concatenate([left, values, right], axis=0).astype(
            jnp.bfloat16
        )

    def gather_rows(buffer, row, count, spread):
        return jnp.concatenate(
            [buffer[:, at(buffer, row + spread * (a - 1), count)] for a in range(3)], axis=0
        )

    def product(weight_ref, inputs):
        return jnp.dot(weight_ref[...], inputs, preferred_element_type=jnp.float32)

    def store_hidden(buffer, row, count, values):
        values = gelu(values)
        if hidden_pad:
            blank = jnp.zeros((hidden_pad, values.shape[1]), jnp.float32)
            values = jnp.concatenate([values, blank], axis=0)
        buffer[:, at(buffer, row, count)] = values.astype(jnp.bfloat16)

    def side_sum(made, width, spread, index):
        piece = made[:, index * LANES : (index + 1) * LANES]
        left = from_left(piece[0:width], spread)
        right = from_right(piece[2 * width : 3 * width], spread)
        return piece[width : 2 * width] + left + right

    def over_rows(first, last, count, body):
        trips = (last - first) // count

        def step(i, carry):
            body(first + i * count)
            return carry

        lax.fori_loop(0, trips, step, 0)

    def sea_entry(row, count):
        store_hidden(sea_hid, row, count, product(se_ref, gather_rows(sea_in, row, count, 1)))

    def sea_exit(row, count):
        made = product(sx_ref, gather_rows(sea_hid, row, count, 1))
        for i in range(count):
            change = side_sum(made, surface, 1, i)
            weight = mask_in[pl.ds(row + i, 1), :]
            old = sea_now[:, at(sea_now, row + i, 1)]
            new = (old + weight * change).astype(jnp.bfloat16).astype(jnp.float32)
            sea_now[:, at(sea_now, row + i, 1)] = new
            air = air_now[:, at(air_now, row + i, 1)]
            store_air_in(row + i, jnp.concatenate([air, new], axis=0), edge_in[:, at(edge_in, row + i, 1)])

    def air_entry(row, count):
        store_hidden(hid1, row, count, product(ae_ref, gather_rows(air_in, row, count, 1)))

    def air_middle(row, count):
        made = product(am_ref, gather_rows(hid1, row, count, 2))
        sums = [side_sum(made, hidden, 2, i) for i in range(count)]
        store_hidden(hid2, row, count, jnp.concatenate(sums, axis=1))

    def air_exit(row, count, last):
        made = product(ax_ref, gather_rows(hid2, row, count, 4))
        for i in range(count):
            change = side_sum(made, fields + flux_count, 4, i)
            old = air_now[:, at(air_now, row + i, 1)]
            new = (old + change[0:fields]).astype(jnp.bfloat16).astype(jnp.float32)
            sea = sea_now[:, at(sea_now, row + i, 1)]
            if last:
                planes[:, row + i - rows, :] = jnp.concatenate([new, sea], axis=0)
            else:
                air_now[:, at(air_now, row + i, 1)] = new
                flux = change[fields:].astype(jnp.bfloat16).astype(jnp.float32)
                store_sea_in(row + i, jnp.concatenate([sea, flux], axis=0))

    for block, source in enumerate(block_refs):
        tail = source[:, rows * LANES : (rows + 1) * LANES].astype(jnp.float32)
        mask_in[block * rows : (block + 1) * rows, :] = tail[fields : fields + rows]
        for i in range(rows):
            row = block * rows + i
            values = source[:, i * LANES : (i + 1) * LANES].astype(jnp.float32)
            air_now[:, at(air_now, row, 1)] = values[0:fields]
            sea_now[:, at(sea_now, row, 1)] = values[fields : fields + surface]
            store_sea_in(row, values[fields:kept])
            edge = jnp.broadcast_to(tail[0:fields, i : i + 1], (fields, LANES))
            edge_in[:, at(edge_in, row, 1)] = edge
    close_ring(sea_in)

    over_rows(0, ring, 2, lambda r: sea_entry(r, 2))
    close_ring(sea_hid)
    over_rows(0, ring, 2, lambda r: sea_exit(r, 2))
    close_ring(air_in)
    over_rows(0, ring, 2, lambda r: air_entry(r, 2))
    close_ring(hid1)
    over_rows(0, ring, 2, lambda r: air_middle(r, 2))
    close_ring(hid2)
    over_rows(0, ring, 2, lambda r: air_exit(r, 2, False))
    close_ring(sea_in)

    over_rows(rows - 8, 2 * rows + 8, 2, lambda r: sea_entry(r, 2))
    over_rows(rows - 7, 2 * rows + 7, 2, lambda r: sea_exit(r, 2))
    over_rows(rows - 6, 2 * rows + 6, 2, lambda r: air_entry(r, 2))
    over_rows(rows - 4, 2 * rows + 4, 2, lambda r: air_middle(r, 2))
    for r in range(rows, 2 * rows, 2):
        air_exit(r, 2, True)
    out_ref[...] = planes[...].astype(jnp.bfloat16)


def belt_shards(
    atmosphere, ocean_state, fluxes, sea_mask, air_entry, air_middle, air_exit, sea_entry, sea_exit
):
    blocks = lax.axis_size("sp")
    position = lax.axis_index("sec")
    members, fields, rows, cols = atmosphere.shape
    surface, flux_count = ocean_state.shape[1], fluxes.shape[1]
    hidden = air_middle.shape[3]
    hidden_rows = pad_to(hidden, PACKED)
    kept = fields + surface + flux_count
    ring = blocks * rows
    swap = [(0, 1), (1, 0)]
    bf16, f32 = jnp.bfloat16, jnp.float32

    sent = jnp.where(position == 0, atmosphere[1], atmosphere[0])
    got = lax.ppermute(sent, "sec", swap)
    packed = pl.pallas_call(
        pack_kernel,
        out_shape=jax.ShapeDtypeStruct((kept, (rows + 1) * LANES), bf16),
        in_specs=[pl.BlockSpec(memory_space=pltpu.SMEM)] + vmem_specs(5),
        out_specs=vmem_specs(1)[0],
        scratch_shapes=[pltpu.VMEM((kept + fields, rows, LANES), f32)],
        cost_estimate=pl.CostEstimate(flops=100000, bytes_accessed=400000, transcendentals=0),
        name="pack",
    )(position.reshape(1), atmosphere, got, ocean_state, fluxes, sea_mask)

    weights = pl.pallas_call(
        weights_kernel,
        out_shape=(
            jax.ShapeDtypeStruct((hidden, 9 * sea_entry.shape[2]), bf16),
            jax.ShapeDtypeStruct((3 * surface, 3 * hidden_rows), bf16),
            jax.ShapeDtypeStruct((hidden, 9 * air_entry.shape[2]), bf16),
            jax.ShapeDtypeStruct((3 * hidden, 3 * hidden_rows), bf16),
            jax.ShapeDtypeStruct((3 * (fields + flux_count), 3 * hidden_rows), bf16),
        ),
        in_specs=vmem_specs(5),
        out_specs=tuple(vmem_specs(5)),
        cost_estimate=pl.CostEstimate(flops=1000000, bytes_accessed=4000000, transcendentals=0),
        name="weights",
    )(sea_entry, sea_exit, air_entry, air_middle, air_exit)

    frame = [None] * blocks
    for index in range(blocks):
        shift = (1 - index) % blocks
        if shift == 0:
            frame[index] = packed
        else:
            pairs = [(i, (i + shift) % blocks) for i in range(blocks)]
            frame[index] = lax.ppermute(packed, "sp", pairs)

    sizes = (fields, surface, flux_count, hidden, blocks, rows)
    made = pl.pallas_call(
        functools.partial(forecast_kernel, sizes),
        out_shape=jax.ShapeDtypeStruct((fields + surface, rows, LANES), bf16),
        in_specs=vmem_specs(blocks + 5),
        out_specs=vmem_specs(1)[0],
        scratch_shapes=[
            pltpu.VMEM((3 * (surface + flux_count), (ring + 2) * LANES), bf16),
            pltpu.VMEM((hidden_rows, (ring + 2) * LANES), bf16),
            pltpu.VMEM((3 * (fields + surface), (ring + 2) * LANES), bf16),
            pltpu.VMEM((hidden_rows, (ring + 4) * LANES), bf16),
            pltpu.VMEM((hidden_rows, (ring + 8) * LANES), bf16),
            pltpu.VMEM((fields, ring * LANES), f32),
            pltpu.VMEM((surface, ring * LANES), f32),
            pltpu.VMEM((fields, ring * LANES), f32),
            pltpu.VMEM((ring, LANES), f32),
            pltpu.VMEM((fields + surface, rows, LANES), f32),
        ],
        cost_estimate=pl.CostEstimate(
            flops=4000000000, bytes_accessed=3000000, transcendentals=1000000
        ),
        name="forecast",
    )(*frame, *weights)

    other = lax.ppermute(made, "sec", swap)
    first = position == 0
    low = jnp.where(first, made, other)
    high = jnp.where(first, other, made)
    both = jnp.stack([low, high])
    air_final = jnp.where(first, both[:, :fields], atmosphere)
    return (air_final, both[:, fields:])


def belt_fits(mesh, atmosphere, ocean_state, fluxes, sea_entry, sea_exit):
    sections, blocks = mesh.shape["sec"], mesh.shape["sp"]
    members = atmosphere.shape[0] // (mesh.shape["grp"] * mesh.shape["mb"])
    rows = atmosphere.shape[2] // blocks
    band = atmosphere.shape[3] // sections
    fields, surface, flux_count = atmosphere.shape[1], ocean_state.shape[1], fluxes.shape[1]
    halo = 9
    return (
        sections == 2
        and members == 2
        and band == LANES
        and ocean_state.shape[3] == band
        and rows % SUBLANES == 0
        and rows <= LANES
        and rows >= halo - 1
        and blocks > 1
        and 2 * rows + halo <= blocks * rows
        and blocks * rows <= 64
        and rows <= surface + flux_count
        and all(c % SUBLANES == 0 for c in (fields, surface, flux_count, sea_entry.shape[3]))
        and (surface + flux_count) % PACKED == 0
        and (fields + surface) % PACKED == 0
    )


def solution(mesh):
    placed = (
        P(("grp", "mb"), None, "sp", "sec"),
        P(("grp", "mb"), None, "sp", None),
        P(("grp", "mb"), None, "sp", None),
        P("sp", None),
        P(),
        P(),
        P(),
        P(),
        P(),
    )

    def run(atmosphere, ocean_state, fluxes, sea_mask, air_entry, air_middle, air_exit, sea_entry, sea_exit):
        fits = belt_fits(mesh, atmosphere, ocean_state, fluxes, sea_entry, sea_exit)
        return jax.shard_map(
            belt_shards if fits else shards,
            mesh=mesh,
            in_specs=placed,
            out_specs=(P(("grp", "mb"), None, "sp", "sec"), P(("grp", "mb"), None, "sp", None)),
            check_vma=False,
        )(
            atmosphere, ocean_state, fluxes, sea_mask, air_entry, air_middle, air_exit, sea_entry, sea_exit
        )

    return run
```

```python
import functools

import jax
import jax.numpy as jnp
from jax import lax
from jax.experimental import pallas as pl
from jax.experimental.pallas import tpu as pltpu
from jax.sharding import PartitionSpec as P

STEPS = 2


dilations = (1, 2, 4)


def with_halo(block, sides, width):
    for axis, dim in sides:
        count = lax.axis_size(axis)
        forward = [(i, i + 1) for i in range(count - 1)]
        forward.append((count - 1, 0))
        backward = [(target, source) for source, target in forward]
        low = lax.ppermute(
            lax.slice_in_dim(block, block.shape[dim] - width, None, axis=dim), axis, forward
        )
        high = lax.ppermute(lax.slice_in_dim(block, 0, width, axis=dim), axis, backward)
        block = jnp.concatenate([low, block, high], axis=dim)
    return block


def spread_2(value, axis, source):
    kept = jnp.where(lax.axis_index(axis) == source, value, 0).astype(value.dtype)
    return lax.psum(kept, axis)


def tap_sum(source, weight, dilation):
    out_rows = source.shape[2] - 2 * dilation
    out_cols = source.shape[3] - 2 * dilation
    pieces = []
    for tap_row in range(3):
        for tap_col in range(3):
            sliced = lax.slice_in_dim(
                source, tap_row * dilation, tap_row * dilation + out_rows, axis=2
            )
            sliced = lax.slice_in_dim(
                sliced, tap_col * dilation, tap_col * dilation + out_cols, axis=3
            )
            pieces.append(sliced)
    stacked = jnp.concatenate(pieces, axis=1)
    flat_weight = weight.reshape(-1, weight.shape[3])
    return jnp.einsum("mkrc,ko->morc", stacked, flat_weight, preferred_element_type=jnp.float32)


def gelu_round(values):
    return jax.nn.gelu(values, approximate=True).astype(jnp.bfloat16)


def keep_columns(block, first_column, limit):
    columns = lax.iota(jnp.int32, block.shape[3]) + first_column
    inside = (columns >= 0) & (columns < limit)
    return jnp.where(inside[None, None, None, :], block, jnp.zeros_like(block))


def shards(
    atmosphere, ocean_state, fluxes, sea_mask, air_entry, air_middle, air_exit, sea_entry, sea_exit
):
    sections = lax.axis_size("sec")
    position = lax.axis_index("sec")
    is_ocean = position == sections - 1
    band_cols = atmosphere.shape[3]
    ocean_cols = ocean_state.shape[3]
    field_count = atmosphere.shape[1]
    sea_weight = sea_mask.astype(jnp.float32)
    air_weights = (air_entry, air_middle, air_exit)
    sea_weights = (sea_entry, sea_exit)

    def air_layer(extended, layer_index):
        produced = tap_sum(extended, air_weights[layer_index], dilations[layer_index])
        if layer_index < 2:
            return gelu_round(produced)
        return produced

    def air_blank(extended, layer_index):
        spread = dilations[layer_index]
        out_shape = (
            extended.shape[0],
            air_weights[layer_index].shape[3],
            extended.shape[2] - 2 * spread,
            extended.shape[3] - 2 * spread,
        )
        return jnp.zeros(out_shape, jnp.bfloat16 if layer_index < 2 else jnp.float32)

    def sea_layer(extended, layer_index):
        padded = jnp.pad(extended, ((0, 0), (0, 0), (0, 0), (1, 1)))
        produced = tap_sum(padded, sea_weights[layer_index], 1)
        if layer_index < 1:
            return gelu_round(produced)
        return produced

    def sea_blank(extended, layer_index):
        out_shape = (
            extended.shape[0],
            sea_weights[layer_index].shape[3],
            extended.shape[2] - 2,
            ocean_cols,
        )
        return jnp.zeros(out_shape, jnp.bfloat16 if layer_index < 1 else jnp.float32)

    def air_extend(current, layer_index, margin):
        extended = with_halo(current, (("sp", 2), ("sec", 3)), dilations[layer_index])
        margin = dilations[layer_index]
        limit = band_cols * sections if layer_index == 0 else ocean_cols
        extended = keep_columns(extended, position * band_cols - margin, limit)
        return (extended, margin - dilations[layer_index])

    def sea_extend(current):
        return with_halo(current, (("sp", 2),), 1)

    def run_segment(air_job, sea_job):
        air_current = None
        sea_current = None
        margin = 0
        if air_job is not None:
            air_current = jnp.concatenate(air_job, axis=1)
        if sea_job is not None:
            sea_current = jnp.concatenate(sea_job, axis=1)
        for layer_index in range(3):
            air_ready = None
            sea_ready = None
            if air_current is not None:
                air_ready, margin = air_extend(air_current, layer_index, margin)
            if sea_current is not None and layer_index < 2:
                sea_ready = sea_extend(sea_current)
            if air_ready is None and sea_ready is None:
                continue

            def on_sea(ready):
                air_given, sea_given = ready
                air_made = None if air_given is None else air_blank(air_given, layer_index)
                sea_made = None if sea_given is None else sea_layer(sea_given, layer_index)
                return (air_made, sea_made)

            def on_air(ready):
                air_given, sea_given = ready
                air_made = None if air_given is None else air_layer(air_given, layer_index)
                sea_made = None if sea_given is None else sea_blank(sea_given, layer_index)
                return (air_made, sea_made)

            air_next, sea_next = lax.cond(is_ocean, on_sea, on_air, (air_ready, sea_ready))
            if air_ready is not None:
                air_current = air_next
            if sea_ready is not None:
                sea_current = sea_next
        air_result = None
        sea_result = None
        if air_job is not None:
            previous = air_job[0]
            renewed = (previous.astype(jnp.float32) + air_current[:, :field_count]).astype(
                jnp.bfloat16
            )
            air_result = (renewed, air_current[:, field_count:].astype(jnp.bfloat16))
        if sea_job is not None:
            previous = sea_job[0]
            sea_result = (
                previous.astype(jnp.float32) + sea_weight[None, None] * sea_current
            ).astype(jnp.bfloat16)
        return (air_result, sea_result)

    air_now, sea_now, flux_now = (atmosphere, ocean_state, fluxes)
    for step_index in range(STEPS):
        sea_now = run_segment(None, (sea_now, flux_now))[1]
        shared = spread_2(sea_now, "sec", sections - 1)
        start_col = jnp.minimum(position, sections - 2) * band_cols
        own_band = lax.dynamic_slice_in_dim(shared, start_col, band_cols, 3)
        own_band = jnp.where(is_ocean, jnp.zeros_like(own_band), own_band)
        sea_now = shared
        air_now, flux_band = run_segment((air_now, own_band), None)[0]
        if step_index + 1 < STEPS:
            collected = lax.all_gather(flux_band, "sec", axis=3, tiled=True)
            flux_now = collected[:, :, :, :ocean_cols]
    return (air_now, sea_now)


LANES = 128
SUBLANES = 8
PACKED = 16


def pad_to(count, unit):
    return -(-count // unit) * unit


def tree_add(terms):
    total = terms[0]
    for term in terms[1:]:
        total = total + term
    return total


def gelu(v):
    inner = v * (0.7978845608028654 + (0.7978845608028654 * 0.044715) * (v * v))
    half = 0.5 * v
    return half + half * jnp.tanh(inner)


def lane_ids(rows):
    return lax.broadcasted_iota(jnp.int32, (rows, LANES), 1)


def from_left(v, distance, fill=0.0):
    return jnp.where(lane_ids(v.shape[0]) < distance, fill, pltpu.roll(v, distance, 1))


def from_right(v, distance, fill=0.0):
    rolled = pltpu.roll(v, LANES - distance, 1)
    return jnp.where(lane_ids(v.shape[0]) >= LANES - distance, fill, rolled)


def vmem_specs(count):
    return [pl.BlockSpec(memory_space=pltpu.VMEM)] * count


def pack_kernel(sec_ref, air_ref, got_ref, sea_ref, flux_ref, mask_ref, out_ref, planes):
    fields = air_ref.shape[1]
    surface = sea_ref.shape[1]
    fluxes = flux_ref.shape[1]
    rows = air_ref.shape[2]
    first = sec_ref[0] == 0
    kept = fields + surface + fluxes
    got = got_ref[...].astype(jnp.float32)
    planes[0:fields] = jnp.where(first, air_ref[0].astype(jnp.float32), got)
    planes[kept : kept + fields] = jnp.where(first, got, air_ref[1].astype(jnp.float32))
    planes[fields : fields + surface] = jnp.where(
        first, sea_ref[0].astype(jnp.float32), sea_ref[1].astype(jnp.float32)
    )
    planes[fields + surface : kept] = jnp.where(
        first, flux_ref[0].astype(jnp.float32), flux_ref[1].astype(jnp.float32)
    )
    lanes = lane_ids(fields)
    edge = jnp.zeros((fields, LANES), jnp.float32)
    for row in range(rows):
        out_ref[:, row * LANES : (row + 1) * LANES] = planes[0:kept, row, :].astype(jnp.bfloat16)
        band = planes[kept : kept + fields, row, :]
        if row:
            band = pltpu.roll(band, row, 1)
        edge = jnp.where(lanes == row, band, edge)
    mask = mask_ref[...].astype(jnp.float32)
    rest = jnp.zeros((kept - fields - rows, LANES), jnp.float32)
    tail = jnp.concatenate([edge, mask, rest], axis=0)
    out_ref[:, rows * LANES : (rows + 1) * LANES] = tail.astype(jnp.bfloat16)


def weights_kernel(se_ref, sx_ref, ae_ref, am_ref, ax_ref, se_out, sx_out, ae_out, am_out, ax_out):
    for source, target in ((se_ref, se_out), (ae_ref, ae_out)):
        taps = [
            source[a, b].astype(jnp.float32).T for a in range(3) for b in range(3)
        ]
        target[...] = jnp.concatenate(taps, axis=1).astype(jnp.bfloat16)
    for source, target in ((sx_ref, sx_out), (am_ref, am_out), (ax_ref, ax_out)):
        depth, width = source.shape[2:]
        blank = jnp.zeros((width, pad_to(depth, PACKED) - depth), jnp.float32)
        groups = []
        for b in range(3):
            pieces = []
            for a in range(3):
                pieces += [source[a, b].astype(jnp.float32).T, blank]
            groups.append(jnp.concatenate(pieces, axis=1))
        target[...] = jnp.concatenate(groups, axis=0).astype(jnp.bfloat16)


def forecast_kernel(sizes, *refs):
    fields, surface, flux_count, hidden, blocks, rows = sizes
    block_refs = refs[:blocks]
    se_ref, sx_ref, ae_ref, am_ref, ax_ref, out_ref = refs[blocks : blocks + 6]
    sea_in, sea_hid, air_in, hid1, hid2, air_now, sea_now, edge_in, mask_in, planes = refs[blocks + 6 :]
    ring = blocks * rows
    kept = fields + surface + flux_count
    hidden_pad = sea_hid.shape[0] - hidden
    pads = {id(sea_in): 1, id(sea_hid): 1, id(air_in): 1, id(hid1): 2, id(hid2): 4}

    def at(buffer, row, count):
        start = row + pads.get(id(buffer), 0)
        if isinstance(row, int):
            return pl.ds(start * LANES, count * LANES)
        return pl.ds(pl.multiple_of(start * LANES, LANES), count * LANES)

    def close_ring(buffer):
        pad = pads[id(buffer)]
        buffer[:, 0 : pad * LANES] = buffer[:, ring * LANES : (ring + pad) * LANES]
        buffer[:, (ring + pad) * LANES :] = buffer[:, pad * LANES : 2 * pad * LANES]

    def store_sea_in(row, values):
        left, right = from_left(values, 1), from_right(values, 1)
        sea_in[:, at(sea_in, row, 1)] = jnp.concatenate([left, values, right], axis=0).astype(
            jnp.bfloat16
        )

    def store_air_in(row, values, edge):
        fill = jnp.concatenate([edge, jnp.zeros((surface, LANES), jnp.float32)], axis=0)
        left, right = from_left(values, 1), from_right(values, 1, fill)
        air_in[:, at(air_in, row, 1)] = jnp.concatenate([left, values, right], axis=0).astype(
            jnp.bfloat16
        )

    def gather_rows(buffer, row, count, spread):
        return jnp.concatenate(
            [buffer[:, at(buffer, row + spread * (a - 1), count)] for a in range(3)], axis=0
        )

    def product(weight_ref, inputs):
        return jnp.dot(weight_ref[...], inputs, preferred_element_type=jnp.float32)

    def store_hidden(buffer, row, count, values):
        values = gelu(values)
        if hidden_pad:
            blank = jnp.zeros((hidden_pad, values.shape[1]), jnp.float32)
            values = jnp.concatenate([values, blank], axis=0)
        buffer[:, at(buffer, row, count)] = values.astype(jnp.bfloat16)

    def side_sum(made, width, spread, index):
        piece = made[:, index * LANES : (index + 1) * LANES]
        left = from_left(piece[0:width], spread)
        right = from_right(piece[2 * width : 3 * width], spread)
        return piece[width : 2 * width] + left + right

    def over_rows(first, last, count, body):
        for row in range(first, last, count):
            body(row)

    def sea_entry(row, count):
        store_hidden(sea_hid, row, count, product(se_ref, gather_rows(sea_in, row, count, 1)))

    def sea_exit(row, count):
        made = product(sx_ref, gather_rows(sea_hid, row, count, 1))
        for i in range(count):
            change = side_sum(made, surface, 1, i)
            weight = mask_in[pl.ds(row + i, 1), :]
            old = sea_now[:, at(sea_now, row + i, 1)]
            new = (old + weight * change).astype(jnp.bfloat16).astype(jnp.float32)
            sea_now[:, at(sea_now, row + i, 1)] = new
            air = air_now[:, at(air_now, row + i, 1)]
            store_air_in(row + i, jnp.concatenate([air, new], axis=0), edge_in[:, at(edge_in, row + i, 1)])

    def air_entry(row, count):
        store_hidden(hid1, row, count, product(ae_ref, gather_rows(air_in, row, count, 1)))

    def air_middle(row, count):
        made = product(am_ref, gather_rows(hid1, row, count, 2))
        sums = [side_sum(made, hidden, 2, i) for i in range(count)]
        store_hidden(hid2, row, count, jnp.concatenate(sums, axis=1))

    def air_exit(row, count, last):
        made = product(ax_ref, gather_rows(hid2, row, count, 4))
        for i in range(count):
            change = side_sum(made, fields + flux_count, 4, i)
            old = air_now[:, at(air_now, row + i, 1)]
            new = (old + change[0:fields]).astype(jnp.bfloat16).astype(jnp.float32)
            sea = sea_now[:, at(sea_now, row + i, 1)]
            if last:
                planes[:, row + i - rows, :] = jnp.concatenate([new, sea], axis=0)
            else:
                air_now[:, at(air_now, row + i, 1)] = new
                flux = change[fields:].astype(jnp.bfloat16).astype(jnp.float32)
                store_sea_in(row + i, jnp.concatenate([sea, flux], axis=0))

    for block, source in enumerate(block_refs):
        tail = source[:, rows * LANES : (rows + 1) * LANES].astype(jnp.float32)
        mask_in[block * rows : (block + 1) * rows, :] = tail[fields : fields + rows]
        for i in range(rows):
            row = block * rows + i
            values = source[:, i * LANES : (i + 1) * LANES].astype(jnp.float32)
            air_now[:, at(air_now, row, 1)] = values[0:fields]
            sea_now[:, at(sea_now, row, 1)] = values[fields : fields + surface]
            store_sea_in(row, values[fields:kept])
            edge = jnp.broadcast_to(tail[0:fields, i : i + 1], (fields, LANES))
            edge_in[:, at(edge_in, row, 1)] = edge
    close_ring(sea_in)

    over_rows(0, ring, 2, lambda r: sea_entry(r, 2))
    close_ring(sea_hid)
    over_rows(0, ring, 2, lambda r: sea_exit(r, 2))
    close_ring(air_in)
    over_rows(0, ring, 2, lambda r: air_entry(r, 2))
    close_ring(hid1)
    over_rows(0, ring, 2, lambda r: air_middle(r, 2))
    close_ring(hid2)
    over_rows(0, ring, 2, lambda r: air_exit(r, 2, False))
    close_ring(sea_in)

    over_rows(rows - 8, 2 * rows + 8, 2, lambda r: sea_entry(r, 2))
    over_rows(rows - 7, 2 * rows + 7, 2, lambda r: sea_exit(r, 2))
    over_rows(rows - 6, 2 * rows + 6, 2, lambda r: air_entry(r, 2))
    over_rows(rows - 4, 2 * rows + 4, 2, lambda r: air_middle(r, 2))
    for r in range(rows, 2 * rows, 2):
        air_exit(r, 2, True)
    out_ref[...] = planes[...].astype(jnp.bfloat16)


def belt_shards(
    atmosphere, ocean_state, fluxes, sea_mask, air_entry, air_middle, air_exit, sea_entry, sea_exit
):
    blocks = lax.axis_size("sp")
    position = lax.axis_index("sec")
    members, fields, rows, cols = atmosphere.shape
    surface, flux_count = ocean_state.shape[1], fluxes.shape[1]
    hidden = air_middle.shape[3]
    hidden_rows = pad_to(hidden, PACKED)
    kept = fields + surface + flux_count
    ring = blocks * rows
    swap = [(0, 1), (1, 0)]
    bf16, f32 = jnp.bfloat16, jnp.float32

    sent = jnp.where(position == 0, atmosphere[1], atmosphere[0])
    got = lax.ppermute(sent, "sec", swap)
    packed = pl.pallas_call(
        pack_kernel,
        out_shape=jax.ShapeDtypeStruct((kept, (rows + 1) * LANES), bf16),
        in_specs=[pl.BlockSpec(memory_space=pltpu.SMEM)] + vmem_specs(5),
        out_specs=vmem_specs(1)[0],
        scratch_shapes=[pltpu.VMEM((kept + fields, rows, LANES), f32)],
        cost_estimate=pl.CostEstimate(flops=100000, bytes_accessed=400000, transcendentals=0),
        name="pack",
    )(position.reshape(1), atmosphere, got, ocean_state, fluxes, sea_mask)

    weights = pl.pallas_call(
        weights_kernel,
        out_shape=(
            jax.ShapeDtypeStruct((hidden, 9 * sea_entry.shape[2]), bf16),
            jax.ShapeDtypeStruct((3 * surface, 3 * hidden_rows), bf16),
            jax.ShapeDtypeStruct((hidden, 9 * air_entry.shape[2]), bf16),
            jax.ShapeDtypeStruct((3 * hidden, 3 * hidden_rows), bf16),
            jax.ShapeDtypeStruct((3 * (fields + flux_count), 3 * hidden_rows), bf16),
        ),
        in_specs=vmem_specs(5),
        out_specs=tuple(vmem_specs(5)),
        cost_estimate=pl.CostEstimate(flops=1000000, bytes_accessed=4000000, transcendentals=0),
        name="weights",
    )(sea_entry, sea_exit, air_entry, air_middle, air_exit)

    frame = [None] * blocks
    for index in range(blocks):
        shift = (1 - index) % blocks
        if shift == 0:
            frame[index] = packed
        else:
            pairs = [(i, (i + shift) % blocks) for i in range(blocks)]
            frame[index] = lax.ppermute(packed, "sp", pairs)

    sizes = (fields, surface, flux_count, hidden, blocks, rows)
    made = pl.pallas_call(
        functools.partial(forecast_kernel, sizes),
        out_shape=jax.ShapeDtypeStruct((fields + surface, rows, LANES), bf16),
        in_specs=vmem_specs(blocks + 5),
        out_specs=vmem_specs(1)[0],
        scratch_shapes=[
            pltpu.VMEM((3 * (surface + flux_count), (ring + 2) * LANES), bf16),
            pltpu.VMEM((hidden_rows, (ring + 2) * LANES), bf16),
            pltpu.VMEM((3 * (fields + surface), (ring + 2) * LANES), bf16),
            pltpu.VMEM((hidden_rows, (ring + 4) * LANES), bf16),
            pltpu.VMEM((hidden_rows, (ring + 8) * LANES), bf16),
            pltpu.VMEM((fields, ring * LANES), f32),
            pltpu.VMEM((surface, ring * LANES), f32),
            pltpu.VMEM((fields, ring * LANES), f32),
            pltpu.VMEM((ring, LANES), f32),
            pltpu.VMEM((fields + surface, rows, LANES), f32),
        ],
        cost_estimate=pl.CostEstimate(
            flops=4000000000, bytes_accessed=3000000, transcendentals=1000000
        ),
        name="forecast",
    )(*frame, *weights)

    other = lax.ppermute(made, "sec", swap)
    first = position == 0
    low = jnp.where(first, made, other)
    high = jnp.where(first, other, made)
    both = jnp.stack([low, high])
    air_final = jnp.where(first, both[:, :fields], atmosphere)
    return (air_final, both[:, fields:])


def belt_fits(mesh, atmosphere, ocean_state, fluxes, sea_entry, sea_exit):
    sections, blocks = mesh.shape["sec"], mesh.shape["sp"]
    members = atmosphere.shape[0] // (mesh.shape["grp"] * mesh.shape["mb"])
    rows = atmosphere.shape[2] // blocks
    band = atmosphere.shape[3] // sections
    fields, surface, flux_count = atmosphere.shape[1], ocean_state.shape[1], fluxes.shape[1]
    halo = 9
    return (
        sections == 2
        and members == 2
        and band == LANES
        and ocean_state.shape[3] == band
        and rows % SUBLANES == 0
        and rows <= LANES
        and rows >= halo - 1
        and blocks > 1
        and 2 * rows + halo <= blocks * rows
        and blocks * rows <= 64
        and rows <= surface + flux_count
        and all(c % SUBLANES == 0 for c in (fields, surface, flux_count, sea_entry.shape[3]))
        and (surface + flux_count) % PACKED == 0
        and (fields + surface) % PACKED == 0
    )


def solution(mesh):
    placed = (
        P(("grp", "mb"), None, "sp", "sec"),
        P(("grp", "mb"), None, "sp", None),
        P(("grp", "mb"), None, "sp", None),
        P("sp", None),
        P(),
        P(),
        P(),
        P(),
        P(),
    )

    def run(atmosphere, ocean_state, fluxes, sea_mask, air_entry, air_middle, air_exit, sea_entry, sea_exit):
        fits = belt_fits(mesh, atmosphere, ocean_state, fluxes, sea_entry, sea_exit)
        return jax.shard_map(
            belt_shards if fits else shards,
            mesh=mesh,
            in_specs=placed,
            out_specs=(P(("grp", "mb"), None, "sp", "sec"), P(("grp", "mb"), None, "sp", None)),
            check_vma=False,
        )(
            atmosphere, ocean_state, fluxes, sea_mask, air_entry, air_middle, air_exit, sea_entry, sea_exit
        )

    return run
```

```python
import functools

import jax
import jax.numpy as jnp
from jax import lax
from jax.experimental import pallas as pl
from jax.experimental.pallas import tpu as pltpu
from jax.sharding import PartitionSpec as P

STEPS = 2


dilations = (1, 2, 4)


def with_halo(block, sides, width):
    for axis, dim in sides:
        count = lax.axis_size(axis)
        forward = [(i, i + 1) for i in range(count - 1)]
        forward.append((count - 1, 0))
        backward = [(target, source) for source, target in forward]
        low = lax.ppermute(
            lax.slice_in_dim(block, block.shape[dim] - width, None, axis=dim), axis, forward
        )
        high = lax.ppermute(lax.slice_in_dim(block, 0, width, axis=dim), axis, backward)
        block = jnp.concatenate([low, block, high], axis=dim)
    return block


def spread_2(value, axis, source):
    kept = jnp.where(lax.axis_index(axis) == source, value, 0).astype(value.dtype)
    return lax.psum(kept, axis)


def tap_sum(source, weight, dilation):
    out_rows = source.shape[2] - 2 * dilation
    out_cols = source.shape[3] - 2 * dilation
    pieces = []
    for tap_row in range(3):
        for tap_col in range(3):
            sliced = lax.slice_in_dim(
                source, tap_row * dilation, tap_row * dilation + out_rows, axis=2
            )
            sliced = lax.slice_in_dim(
                sliced, tap_col * dilation, tap_col * dilation + out_cols, axis=3
            )
            pieces.append(sliced)
    stacked = jnp.concatenate(pieces, axis=1)
    flat_weight = weight.reshape(-1, weight.shape[3])
    return jnp.einsum("mkrc,ko->morc", stacked, flat_weight, preferred_element_type=jnp.float32)


def gelu_round(values):
    return jax.nn.gelu(values, approximate=True).astype(jnp.bfloat16)


def keep_columns(block, first_column, limit):
    columns = lax.iota(jnp.int32, block.shape[3]) + first_column
    inside = (columns >= 0) & (columns < limit)
    return jnp.where(inside[None, None, None, :], block, jnp.zeros_like(block))


def shards(
    atmosphere, ocean_state, fluxes, sea_mask, air_entry, air_middle, air_exit, sea_entry, sea_exit
):
    sections = lax.axis_size("sec")
    position = lax.axis_index("sec")
    is_ocean = position == sections - 1
    band_cols = atmosphere.shape[3]
    ocean_cols = ocean_state.shape[3]
    field_count = atmosphere.shape[1]
    sea_weight = sea_mask.astype(jnp.float32)
    air_weights = (air_entry, air_middle, air_exit)
    sea_weights = (sea_entry, sea_exit)

    def air_layer(extended, layer_index):
        produced = tap_sum(extended, air_weights[layer_index], dilations[layer_index])
        if layer_index < 2:
            return gelu_round(produced)
        return produced

    def air_blank(extended, layer_index):
        spread = dilations[layer_index]
        out_shape = (
            extended.shape[0],
            air_weights[layer_index].shape[3],
            extended.shape[2] - 2 * spread,
            extended.shape[3] - 2 * spread,
        )
        return jnp.zeros(out_shape, jnp.bfloat16 if layer_index < 2 else jnp.float32)

    def sea_layer(extended, layer_index):
        padded = jnp.pad(extended, ((0, 0), (0, 0), (0, 0), (1, 1)))
        produced = tap_sum(padded, sea_weights[layer_index], 1)
        if layer_index < 1:
            return gelu_round(produced)
        return produced

    def sea_blank(extended, layer_index):
        out_shape = (
            extended.shape[0],
            sea_weights[layer_index].shape[3],
            extended.shape[2] - 2,
            ocean_cols,
        )
        return jnp.zeros(out_shape, jnp.bfloat16 if layer_index < 1 else jnp.float32)

    def air_extend(current, layer_index, margin):
        extended = with_halo(current, (("sp", 2), ("sec", 3)), dilations[layer_index])
        margin = dilations[layer_index]
        limit = band_cols * sections if layer_index == 0 else ocean_cols
        extended = keep_columns(extended, position * band_cols - margin, limit)
        return (extended, margin - dilations[layer_index])

    def sea_extend(current):
        return with_halo(current, (("sp", 2),), 1)

    def run_segment(air_job, sea_job):
        air_current = None
        sea_current = None
        margin = 0
        if air_job is not None:
            air_current = jnp.concatenate(air_job, axis=1)
        if sea_job is not None:
            sea_current = jnp.concatenate(sea_job, axis=1)
        for layer_index in range(3):
            air_ready = None
            sea_ready = None
            if air_current is not None:
                air_ready, margin = air_extend(air_current, layer_index, margin)
            if sea_current is not None and layer_index < 2:
                sea_ready = sea_extend(sea_current)
            if air_ready is None and sea_ready is None:
                continue

            def on_sea(ready):
                air_given, sea_given = ready
                air_made = None if air_given is None else air_blank(air_given, layer_index)
                sea_made = None if sea_given is None else sea_layer(sea_given, layer_index)
                return (air_made, sea_made)

            def on_air(ready):
                air_given, sea_given = ready
                air_made = None if air_given is None else air_layer(air_given, layer_index)
                sea_made = None if sea_given is None else sea_blank(sea_given, layer_index)
                return (air_made, sea_made)

            air_next, sea_next = lax.cond(is_ocean, on_sea, on_air, (air_ready, sea_ready))
            if air_ready is not None:
                air_current = air_next
            if sea_ready is not None:
                sea_current = sea_next
        air_result = None
        sea_result = None
        if air_job is not None:
            previous = air_job[0]
            renewed = (previous.astype(jnp.float32) + air_current[:, :field_count]).astype(
                jnp.bfloat16
            )
            air_result = (renewed, air_current[:, field_count:].astype(jnp.bfloat16))
        if sea_job is not None:
            previous = sea_job[0]
            sea_result = (
                previous.astype(jnp.float32) + sea_weight[None, None] * sea_current
            ).astype(jnp.bfloat16)
        return (air_result, sea_result)

    air_now, sea_now, flux_now = (atmosphere, ocean_state, fluxes)
    for step_index in range(STEPS):
        sea_now = run_segment(None, (sea_now, flux_now))[1]
        shared = spread_2(sea_now, "sec", sections - 1)
        start_col = jnp.minimum(position, sections - 2) * band_cols
        own_band = lax.dynamic_slice_in_dim(shared, start_col, band_cols, 3)
        own_band = jnp.where(is_ocean, jnp.zeros_like(own_band), own_band)
        sea_now = shared
        air_now, flux_band = run_segment((air_now, own_band), None)[0]
        if step_index + 1 < STEPS:
            collected = lax.all_gather(flux_band, "sec", axis=3, tiled=True)
            flux_now = collected[:, :, :, :ocean_cols]
    return (air_now, sea_now)


LANES = 128
SUBLANES = 8
PACKED = 16


def pad_to(count, unit):
    return -(-count // unit) * unit


def tree_add(terms):
    total = terms[0]
    for term in terms[1:]:
        total = total + term
    return total


def gelu(v):
    inner = v * (0.7978845608028654 + (0.7978845608028654 * 0.044715) * (v * v))
    half = 0.5 * v
    return half + half * jnp.tanh(inner)


def lane_ids(rows):
    return lax.broadcasted_iota(jnp.int32, (rows, LANES), 1)


def from_left(v, distance, fill=0.0):
    return jnp.where(lane_ids(v.shape[0]) < distance, fill, pltpu.roll(v, distance, 1))


def from_right(v, distance, fill=0.0):
    rolled = pltpu.roll(v, LANES - distance, 1)
    return jnp.where(lane_ids(v.shape[0]) >= LANES - distance, fill, rolled)


def vmem_specs(count):
    return [pl.BlockSpec(memory_space=pltpu.VMEM)] * count


def in_vmem(*values):
    return tuple(pltpu.with_memory_space_constraint(value, pltpu.VMEM) for value in values)


def edge_of(bands):
    lanes = lane_ids(bands[0].shape[0])
    edge = jnp.where(lanes == 0, bands[0], 0.0)
    for row, band in enumerate(bands[1:], 1):
        edge = jnp.where(lanes == row, pltpu.roll(band, row, 1), edge)
    return edge


def pack_own_kernel(air_ref, sea_ref, flux_ref, mask_ref, out_ref, planes):
    fields = air_ref.shape[1]
    surface = sea_ref.shape[1]
    rows = air_ref.shape[2]
    kept = fields + surface + flux_ref.shape[1]
    section = lax.axis_index("sec")
    planes[0:fields] = air_ref[section].astype(jnp.float32)
    planes[fields : fields + surface] = sea_ref[section].astype(jnp.float32)
    planes[fields + surface : kept] = flux_ref[section].astype(jnp.float32)
    bands = []
    for row in range(rows):
        values = planes[:, row, :]
        out_ref[:, row * LANES : (row + 1) * LANES] = values.astype(jnp.bfloat16)
        bands.append(values[0:fields])
    mask = mask_ref[...].astype(jnp.float32)
    rest = jnp.zeros((kept - fields - rows, LANES), jnp.float32)
    tail = jnp.concatenate([edge_of(bands), mask, rest], axis=0)
    out_ref[:, rows * LANES : (rows + 1) * LANES] = tail.astype(jnp.bfloat16)


def pack_got_kernel(own_ref, got_ref, out_ref, planes):
    fields, rows = got_ref.shape[:2]
    first = lax.axis_index("sec") == 0
    planes[...] = got_ref[...].astype(jnp.float32)
    bands = [planes[:, row, :] for row in range(rows)]
    out_ref[fields:, :] = own_ref[fields:, :]

    @pl.when(first)
    def _():
        out_ref[0:fields, 0 : rows * LANES] = own_ref[0:fields, 0 : rows * LANES]
        out_ref[0:fields, rows * LANES :] = edge_of(bands).astype(jnp.bfloat16)

    @pl.when(jnp.logical_not(first))
    def _():
        out_ref[0:fields, rows * LANES :] = own_ref[0:fields, rows * LANES :]
        for row, band in enumerate(bands):
            out_ref[0:fields, row * LANES : (row + 1) * LANES] = band.astype(jnp.bfloat16)


def merge_kernel(made_ref, other_ref, air_ref, air_out, sea_out):
    fields = air_ref.shape[1]
    first = lax.axis_index("sec") == 0

    @pl.when(first)
    def _():
        air_out[0] = made_ref[0:fields]
        air_out[1] = other_ref[0:fields]
        sea_out[0] = made_ref[fields:]
        sea_out[1] = other_ref[fields:]

    @pl.when(jnp.logical_not(first))
    def _():
        air_out[...] = air_ref[...]
        sea_out[0] = other_ref[fields:]
        sea_out[1] = made_ref[fields:]


def weights_kernel(se_ref, sx_ref, ae_ref, am_ref, ax_ref, se_out, sx_out, ae_out, am_out, ax_out):
    for source, target in ((se_ref, se_out), (ae_ref, ae_out)):
        taps = [
            source[a, b].astype(jnp.float32).T for a in range(3) for b in range(3)
        ]
        target[...] = jnp.concatenate(taps, axis=1).astype(jnp.bfloat16)
    for source, target, turned in ((sx_ref, sx_out, True), (am_ref, am_out, False), (ax_ref, ax_out, True)):
        width, depth = source.shape[2:] if turned else source.shape[:1:-1]
        blank = jnp.zeros((width, pad_to(depth, PACKED) - depth), jnp.float32)
        groups = []
        for b in range(3):
            pieces = []
            for a in range(3):
                tap = source[a, b].astype(jnp.float32)
                pieces += [tap if turned else tap.T, blank]
            groups.append(jnp.concatenate(pieces, axis=1))
        target[...] = jnp.concatenate(groups, axis=0).astype(jnp.bfloat16)


def forecast_kernel(sizes, *refs):
    fields, surface, flux_count, hidden, blocks, rows = sizes
    block_refs = refs[:blocks]
    se_ref, sx_ref, ae_ref, am_ref, ax_ref, out_ref = refs[blocks : blocks + 6]
    sea_in, sea_hid, air_in, hid1, hid2, air_now, sea_now, edge_in, mask_in, planes = refs[blocks + 6 :]
    ring = blocks * rows
    kept = fields + surface + flux_count
    hidden_pad = sea_hid.shape[0] - hidden
    pads = {id(sea_in): 1, id(sea_hid): 1, id(air_in): 1, id(hid1): 2, id(hid2): 4}

    def at(buffer, row, count):
        start = row + pads.get(id(buffer), 0)
        if isinstance(row, int):
            return pl.ds(start * LANES, count * LANES)
        return pl.ds(pl.multiple_of(start * LANES, LANES), count * LANES)

    def close_ring(buffer):
        pad = pads[id(buffer)]
        buffer[:, 0 : pad * LANES] = buffer[:, ring * LANES : (ring + pad) * LANES]
        buffer[:, (ring + pad) * LANES :] = buffer[:, pad * LANES : 2 * pad * LANES]

    def store_sea_in(row, values):
        left, right = from_left(values, 1), from_right(values, 1)
        sea_in[:, at(sea_in, row, 1)] = jnp.concatenate([left, values, right], axis=0).astype(
            jnp.bfloat16
        )

    def store_air_in(row, values, edge):
        fill = jnp.concatenate([edge, jnp.zeros((surface, LANES), jnp.float32)], axis=0)
        left, right = from_left(values, 1), from_right(values, 1, fill)
        air_in[:, at(air_in, row, 1)] = jnp.concatenate([left, values, right], axis=0).astype(
            jnp.bfloat16
        )

    def gather_rows(buffer, row, count, spread):
        return jnp.concatenate(
            [buffer[:, at(buffer, row + spread * (a - 1), count)] for a in range(3)], axis=0
        )

    def product(weight_ref, inputs):
        return jnp.dot(weight_ref[...], inputs, preferred_element_type=jnp.float32)

    def store_hidden(buffer, row, count, values):
        values = gelu(values)
        if hidden_pad:
            blank = jnp.zeros((hidden_pad, values.shape[1]), jnp.float32)
            values = jnp.concatenate([values, blank], axis=0)
        buffer[:, at(buffer, row, count)] = values.astype(jnp.bfloat16)

    def side_sum(made, width, spread, index):
        piece = made[:, index * LANES : (index + 1) * LANES]
        left = from_left(piece[0:width], spread)
        right = from_right(piece[2 * width : 3 * width], spread)
        return piece[width : 2 * width] + left + right

    def over_rows(first, last, count, body):
        for row in range(first, last, count):
            body(row)

    def sea_entry(row, count):
        store_hidden(sea_hid, row, count, product(se_ref, gather_rows(sea_in, row, count, 1)))

    def sea_exit(row, count):
        made = product(sx_ref, gather_rows(sea_hid, row, count, 1))
        for i in range(count):
            change = side_sum(made, surface, 1, i)
            weight = mask_in[pl.ds(row + i, 1), :]
            old = sea_now[:, at(sea_now, row + i, 1)]
            new = (old + weight * change).astype(jnp.bfloat16).astype(jnp.float32)
            sea_now[:, at(sea_now, row + i, 1)] = new
            air = air_now[:, at(air_now, row + i, 1)]
            store_air_in(row + i, jnp.concatenate([air, new], axis=0), edge_in[:, at(edge_in, row + i, 1)])

    def air_entry(row, count):
        store_hidden(hid1, row, count, product(ae_ref, gather_rows(air_in, row, count, 1)))

    def air_middle(row, count):
        made = product(am_ref, gather_rows(hid1, row, count, 2))
        sums = [side_sum(made, hidden, 2, i) for i in range(count)]
        store_hidden(hid2, row, count, jnp.concatenate(sums, axis=1))

    def air_exit(row, count, last):
        made = product(ax_ref, gather_rows(hid2, row, count, 4))
        for i in range(count):
            change = side_sum(made, fields + flux_count, 4, i)
            old = air_now[:, at(air_now, row + i, 1)]
            new = (old + change[0:fields]).astype(jnp.bfloat16).astype(jnp.float32)
            sea = sea_now[:, at(sea_now, row + i, 1)]
            if last:
                planes[:, row + i - rows, :] = jnp.concatenate([new, sea], axis=0)
            else:
                air_now[:, at(air_now, row + i, 1)] = new
                flux = change[fields:].astype(jnp.bfloat16).astype(jnp.float32)
                store_sea_in(row + i, jnp.concatenate([sea, flux], axis=0))

    for block, source in enumerate(block_refs):
        tail = source[:, rows * LANES : (rows + 1) * LANES].astype(jnp.float32)
        mask_in[block * rows : (block + 1) * rows, :] = tail[fields : fields + rows]
        for i in range(rows):
            row = block * rows + i
            values = source[:, i * LANES : (i + 1) * LANES].astype(jnp.float32)
            air_now[:, at(air_now, row, 1)] = values[0:fields]
            sea_now[:, at(sea_now, row, 1)] = values[fields : fields + surface]
            store_sea_in(row, values[fields:kept])
            edge = jnp.broadcast_to(tail[0:fields, i : i + 1], (fields, LANES))
            edge_in[:, at(edge_in, row, 1)] = edge
    close_ring(sea_in)

    over_rows(0, ring, 2, lambda r: sea_entry(r, 2))
    close_ring(sea_hid)
    over_rows(0, ring, 2, lambda r: sea_exit(r, 2))
    close_ring(air_in)
    over_rows(0, ring, 2, lambda r: air_entry(r, 2))
    close_ring(hid1)
    over_rows(0, ring, 2, lambda r: air_middle(r, 2))
    close_ring(hid2)
    over_rows(0, ring, 2, lambda r: air_exit(r, 2, False))
    close_ring(sea_in)

    over_rows(rows - 8, 2 * rows + 8, 2, lambda r: sea_entry(r, 2))
    over_rows(rows - 7, 2 * rows + 7, 2, lambda r: sea_exit(r, 2))
    over_rows(rows - 6, 2 * rows + 6, 2, lambda r: air_entry(r, 2))
    over_rows(rows - 4, 2 * rows + 4, 2, lambda r: air_middle(r, 2))
    for r in range(rows, 2 * rows, 2):
        air_exit(r, 2, True)
    out_ref[...] = planes[...].astype(jnp.bfloat16)


def belt_shards(
    atmosphere, ocean_state, fluxes, sea_mask, air_entry, air_middle, air_exit, sea_entry, sea_exit
):
    blocks = lax.axis_size("sp")
    position = lax.axis_index("sec")
    members, fields, rows, cols = atmosphere.shape
    surface, flux_count = ocean_state.shape[1], fluxes.shape[1]
    hidden = air_middle.shape[3]
    hidden_rows = pad_to(hidden, PACKED)
    kept = fields + surface + flux_count
    ring = blocks * rows
    swap = [(0, 1), (1, 0)]
    bf16, f32 = jnp.bfloat16, jnp.float32

    sent = jnp.where(position == 0, atmosphere[1], atmosphere[0])
    got = lax.ppermute(sent, "sec", swap)
    packed_shape = pltpu.VMEM((kept, (rows + 1) * LANES), bf16)
    small = pl.CostEstimate(flops=1000000, bytes_accessed=1000000, transcendentals=0)
    own = pl.pallas_call(
        pack_own_kernel,
        out_shape=packed_shape,
        in_specs=vmem_specs(4),
        out_specs=vmem_specs(1)[0],
        scratch_shapes=[pltpu.VMEM((kept, rows, LANES), f32)],
        cost_estimate=small,
        name="pack_own",
    )(atmosphere, ocean_state, fluxes, sea_mask)
    packed = pl.pallas_call(
        pack_got_kernel,
        out_shape=packed_shape,
        in_specs=vmem_specs(2),
        out_specs=vmem_specs(1)[0],
        scratch_shapes=[pltpu.VMEM((fields, rows, LANES), f32)],
        cost_estimate=small,
        name="pack_got",
    )(*in_vmem(own, got))

    weights = pl.pallas_call(
        weights_kernel,
        out_shape=(
            pltpu.VMEM((hidden, 9 * sea_entry.shape[2]), bf16),
            pltpu.VMEM((3 * surface, 3 * hidden_rows), bf16),
            pltpu.VMEM((hidden, 9 * air_entry.shape[2]), bf16),
            pltpu.VMEM((3 * hidden, 3 * hidden_rows), bf16),
            pltpu.VMEM((3 * (fields + flux_count), 3 * hidden_rows), bf16),
        ),
        in_specs=vmem_specs(5),
        out_specs=tuple(vmem_specs(5)),
        cost_estimate=pl.CostEstimate(flops=1000000, bytes_accessed=4000000, transcendentals=0),
        name="weights",
    )(sea_entry, jnp.swapaxes(sea_exit, 2, 3), air_entry, air_middle, jnp.swapaxes(air_exit, 2, 3))

    frame = [None] * blocks
    for index in range(blocks):
        shift = (1 - index) % blocks
        if shift == 0:
            frame[index] = packed
        else:
            pairs = [(i, (i + shift) % blocks) for i in range(blocks)]
            frame[index] = lax.ppermute(packed, "sp", pairs)

    sizes = (fields, surface, flux_count, hidden, blocks, rows)
    made = pl.pallas_call(
        functools.partial(forecast_kernel, sizes),
        out_shape=pltpu.VMEM((fields + surface, rows, LANES), bf16),
        in_specs=vmem_specs(blocks + 5),
        out_specs=vmem_specs(1)[0],
        scratch_shapes=[
            pltpu.VMEM((3 * (surface + flux_count), (ring + 2) * LANES), bf16),
            pltpu.VMEM((hidden_rows, (ring + 2) * LANES), bf16),
            pltpu.VMEM((3 * (fields + surface), (ring + 2) * LANES), bf16),
            pltpu.VMEM((hidden_rows, (ring + 4) * LANES), bf16),
            pltpu.VMEM((hidden_rows, (ring + 8) * LANES), bf16),
            pltpu.VMEM((fields, ring * LANES), f32),
            pltpu.VMEM((surface, ring * LANES), f32),
            pltpu.VMEM((fields, ring * LANES), f32),
            pltpu.VMEM((ring, LANES), f32),
            pltpu.VMEM((fields + surface, rows, LANES), f32),
        ],
        cost_estimate=pl.CostEstimate(
            flops=4000000000, bytes_accessed=3000000, transcendentals=1000000
        ),
        name="forecast",
    )(*in_vmem(*frame, *weights))

    other = lax.ppermute(made, "sec", swap)
    return pl.pallas_call(
        merge_kernel,
        out_shape=(
            jax.ShapeDtypeStruct(atmosphere.shape, bf16),
            jax.ShapeDtypeStruct(ocean_state.shape, bf16),
        ),
        in_specs=vmem_specs(3),
        out_specs=tuple(vmem_specs(2)),
        cost_estimate=small,
        name="merge",
    )(*in_vmem(made, other, atmosphere))


def belt_fits(mesh, atmosphere, ocean_state, fluxes, sea_entry, sea_exit):
    sections, blocks = mesh.shape["sec"], mesh.shape["sp"]
    members = atmosphere.shape[0] // (mesh.shape["grp"] * mesh.shape["mb"])
    rows = atmosphere.shape[2] // blocks
    band = atmosphere.shape[3] // sections
    fields, surface, flux_count = atmosphere.shape[1], ocean_state.shape[1], fluxes.shape[1]
    halo = 9
    return (
        sections == 2
        and members == 2
        and band == LANES
        and ocean_state.shape[3] == band
        and rows % SUBLANES == 0
        and rows <= LANES
        and rows >= halo - 1
        and blocks > 1
        and 2 * rows + halo <= blocks * rows
        and blocks * rows <= 64
        and rows <= surface + flux_count
        and all(c % SUBLANES == 0 for c in (fields, surface, flux_count, sea_entry.shape[3]))
        and (surface + flux_count) % PACKED == 0
        and (fields + surface) % PACKED == 0
    )


def solution(mesh):
    placed = (
        P(("grp", "mb"), None, "sp", "sec"),
        P(("grp", "mb"), None, "sp", None),
        P(("grp", "mb"), None, "sp", None),
        P("sp", None),
        P(),
        P(),
        P(),
        P(),
        P(),
    )

    def run(atmosphere, ocean_state, fluxes, sea_mask, air_entry, air_middle, air_exit, sea_entry, sea_exit):
        fits = belt_fits(mesh, atmosphere, ocean_state, fluxes, sea_entry, sea_exit)
        return jax.shard_map(
            belt_shards if fits else shards,
            mesh=mesh,
            in_specs=placed,
            out_specs=(P(("grp", "mb"), None, "sp", "sec"), P(("grp", "mb"), None, "sp", None)),
            check_vma=False,
        )(
            atmosphere, ocean_state, fluxes, sea_mask, air_entry, air_middle, air_exit, sea_entry, sea_exit
        )

    return run
```

```python
import functools

import jax
import jax.numpy as jnp
from jax import lax
from jax.experimental import pallas as pl
from jax.experimental.pallas import tpu as pltpu
from jax.sharding import PartitionSpec as P

STEPS = 2


dilations = (1, 2, 4)


def with_halo(block, sides, width):
    for axis, dim in sides:
        count = lax.axis_size(axis)
        forward = [(i, i + 1) for i in range(count - 1)]
        forward.append((count - 1, 0))
        backward = [(target, source) for source, target in forward]
        low = lax.ppermute(
            lax.slice_in_dim(block, block.shape[dim] - width, None, axis=dim), axis, forward
        )
        high = lax.ppermute(lax.slice_in_dim(block, 0, width, axis=dim), axis, backward)
        block = jnp.concatenate([low, block, high], axis=dim)
    return block


def spread_2(value, axis, source):
    kept = jnp.where(lax.axis_index(axis) == source, value, 0).astype(value.dtype)
    return lax.psum(kept, axis)


def tap_sum(source, weight, dilation):
    out_rows = source.shape[2] - 2 * dilation
    out_cols = source.shape[3] - 2 * dilation
    pieces = []
    for tap_row in range(3):
        for tap_col in range(3):
            sliced = lax.slice_in_dim(
                source, tap_row * dilation, tap_row * dilation + out_rows, axis=2
            )
            sliced = lax.slice_in_dim(
                sliced, tap_col * dilation, tap_col * dilation + out_cols, axis=3
            )
            pieces.append(sliced)
    stacked = jnp.concatenate(pieces, axis=1)
    flat_weight = weight.reshape(-1, weight.shape[3])
    return jnp.einsum("mkrc,ko->morc", stacked, flat_weight, preferred_element_type=jnp.float32)


def gelu_round(values):
    return jax.nn.gelu(values, approximate=True).astype(jnp.bfloat16)


def keep_columns(block, first_column, limit):
    columns = lax.iota(jnp.int32, block.shape[3]) + first_column
    inside = (columns >= 0) & (columns < limit)
    return jnp.where(inside[None, None, None, :], block, jnp.zeros_like(block))


def shards(
    atmosphere, ocean_state, fluxes, sea_mask, air_entry, air_middle, air_exit, sea_entry, sea_exit
):
    sections = lax.axis_size("sec")
    position = lax.axis_index("sec")
    is_ocean = position == sections - 1
    band_cols = atmosphere.shape[3]
    ocean_cols = ocean_state.shape[3]
    field_count = atmosphere.shape[1]
    sea_weight = sea_mask.astype(jnp.float32)
    air_weights = (air_entry, air_middle, air_exit)
    sea_weights = (sea_entry, sea_exit)

    def air_layer(extended, layer_index):
        produced = tap_sum(extended, air_weights[layer_index], dilations[layer_index])
        if layer_index < 2:
            return gelu_round(produced)
        return produced

    def air_blank(extended, layer_index):
        spread = dilations[layer_index]
        out_shape = (
            extended.shape[0],
            air_weights[layer_index].shape[3],
            extended.shape[2] - 2 * spread,
            extended.shape[3] - 2 * spread,
        )
        return jnp.zeros(out_shape, jnp.bfloat16 if layer_index < 2 else jnp.float32)

    def sea_layer(extended, layer_index):
        padded = jnp.pad(extended, ((0, 0), (0, 0), (0, 0), (1, 1)))
        produced = tap_sum(padded, sea_weights[layer_index], 1)
        if layer_index < 1:
            return gelu_round(produced)
        return produced

    def sea_blank(extended, layer_index):
        out_shape = (
            extended.shape[0],
            sea_weights[layer_index].shape[3],
            extended.shape[2] - 2,
            ocean_cols,
        )
        return jnp.zeros(out_shape, jnp.bfloat16 if layer_index < 1 else jnp.float32)

    def air_extend(current, layer_index, margin):
        extended = with_halo(current, (("sp", 2), ("sec", 3)), dilations[layer_index])
        margin = dilations[layer_index]
        limit = band_cols * sections if layer_index == 0 else ocean_cols
        extended = keep_columns(extended, position * band_cols - margin, limit)
        return (extended, margin - dilations[layer_index])

    def sea_extend(current):
        return with_halo(current, (("sp", 2),), 1)

    def run_segment(air_job, sea_job):
        air_current = None
        sea_current = None
        margin = 0
        if air_job is not None:
            air_current = jnp.concatenate(air_job, axis=1)
        if sea_job is not None:
            sea_current = jnp.concatenate(sea_job, axis=1)
        for layer_index in range(3):
            air_ready = None
            sea_ready = None
            if air_current is not None:
                air_ready, margin = air_extend(air_current, layer_index, margin)
            if sea_current is not None and layer_index < 2:
                sea_ready = sea_extend(sea_current)
            if air_ready is None and sea_ready is None:
                continue

            def on_sea(ready):
                air_given, sea_given = ready
                air_made = None if air_given is None else air_blank(air_given, layer_index)
                sea_made = None if sea_given is None else sea_layer(sea_given, layer_index)
                return (air_made, sea_made)

            def on_air(ready):
                air_given, sea_given = ready
                air_made = None if air_given is None else air_layer(air_given, layer_index)
                sea_made = None if sea_given is None else sea_blank(sea_given, layer_index)
                return (air_made, sea_made)

            air_next, sea_next = lax.cond(is_ocean, on_sea, on_air, (air_ready, sea_ready))
            if air_ready is not None:
                air_current = air_next
            if sea_ready is not None:
                sea_current = sea_next
        air_result = None
        sea_result = None
        if air_job is not None:
            previous = air_job[0]
            renewed = (previous.astype(jnp.float32) + air_current[:, :field_count]).astype(
                jnp.bfloat16
            )
            air_result = (renewed, air_current[:, field_count:].astype(jnp.bfloat16))
        if sea_job is not None:
            previous = sea_job[0]
            sea_result = (
                previous.astype(jnp.float32) + sea_weight[None, None] * sea_current
            ).astype(jnp.bfloat16)
        return (air_result, sea_result)

    air_now, sea_now, flux_now = (atmosphere, ocean_state, fluxes)
    for step_index in range(STEPS):
        sea_now = run_segment(None, (sea_now, flux_now))[1]
        shared = spread_2(sea_now, "sec", sections - 1)
        start_col = jnp.minimum(position, sections - 2) * band_cols
        own_band = lax.dynamic_slice_in_dim(shared, start_col, band_cols, 3)
        own_band = jnp.where(is_ocean, jnp.zeros_like(own_band), own_band)
        sea_now = shared
        air_now, flux_band = run_segment((air_now, own_band), None)[0]
        if step_index + 1 < STEPS:
            collected = lax.all_gather(flux_band, "sec", axis=3, tiled=True)
            flux_now = collected[:, :, :, :ocean_cols]
    return (air_now, sea_now)


LANES = 128
SUBLANES = 8
PACKED = 16


def pad_to(count, unit):
    return -(-count // unit) * unit


def tree_add(terms):
    total = terms[0]
    for term in terms[1:]:
        total = total + term
    return total


def twice_gelu(v):
    inner = v * (0.7978845608028654 + (0.7978845608028654 * 0.044715) * (v * v))
    return v + v * jnp.tanh(inner)


def lane_ids(rows):
    return lax.broadcasted_iota(jnp.int32, (rows, LANES), 1)


def from_left(v, distance, fill=0.0):
    return jnp.where(lane_ids(v.shape[0]) < distance, fill, pltpu.roll(v, distance, 1))


def from_right(v, distance, fill=0.0):
    rolled = pltpu.roll(v, LANES - distance, 1)
    return jnp.where(lane_ids(v.shape[0]) >= LANES - distance, fill, rolled)


def vmem_specs(count):
    return [pl.BlockSpec(memory_space=pltpu.VMEM)] * count


def in_vmem(*values):
    return tuple(pltpu.with_memory_space_constraint(value, pltpu.VMEM) for value in values)


def edge_of(bands):
    lanes = lane_ids(bands[0].shape[0])
    edge = jnp.where(lanes == 0, bands[0], 0.0)
    for row, band in enumerate(bands[1:], 1):
        edge = jnp.where(lanes == row, pltpu.roll(band, row, 1), edge)
    return edge


def pack_own_kernel(air_ref, sea_ref, flux_ref, mask_ref, out_ref, planes):
    fields = air_ref.shape[1]
    surface = sea_ref.shape[1]
    rows = air_ref.shape[2]
    kept = fields + surface + flux_ref.shape[1]
    section = lax.axis_index("sec")
    planes[0:fields] = air_ref[section].astype(jnp.float32)
    planes[fields : fields + surface] = sea_ref[section].astype(jnp.float32)
    planes[fields + surface : kept] = flux_ref[section].astype(jnp.float32)
    bands = []
    for row in range(rows):
        values = planes[:, row, :]
        out_ref[:, row * LANES : (row + 1) * LANES] = values.astype(jnp.bfloat16)
        bands.append(values[0:fields])
    mask = mask_ref[...].astype(jnp.float32)
    rest = jnp.zeros((kept - fields - rows, LANES), jnp.float32)
    tail = jnp.concatenate([edge_of(bands), mask, rest], axis=0)
    out_ref[:, rows * LANES : (rows + 1) * LANES] = tail.astype(jnp.bfloat16)


def pack_got_kernel(own_ref, got_ref, out_ref, planes):
    fields, rows = got_ref.shape[:2]
    first = lax.axis_index("sec") == 0
    planes[...] = got_ref[...].astype(jnp.float32)
    bands = [planes[:, row, :] for row in range(rows)]
    out_ref[fields:, :] = own_ref[fields:, :]

    @pl.when(first)
    def _():
        out_ref[0:fields, 0 : rows * LANES] = own_ref[0:fields, 0 : rows * LANES]
        out_ref[0:fields, rows * LANES :] = edge_of(bands).astype(jnp.bfloat16)

    @pl.when(jnp.logical_not(first))
    def _():
        out_ref[0:fields, rows * LANES :] = own_ref[0:fields, rows * LANES :]
        for row, band in enumerate(bands):
            out_ref[0:fields, row * LANES : (row + 1) * LANES] = band.astype(jnp.bfloat16)


def merge_kernel(made_ref, other_ref, air_ref, air_out, sea_out):
    fields = air_ref.shape[1]
    first = lax.axis_index("sec") == 0

    @pl.when(first)
    def _():
        air_out[0] = made_ref[0:fields]
        air_out[1] = other_ref[0:fields]
        sea_out[0] = made_ref[fields:]
        sea_out[1] = other_ref[fields:]

    @pl.when(jnp.logical_not(first))
    def _():
        air_out[...] = air_ref[...]
        sea_out[0] = other_ref[fields:]
        sea_out[1] = made_ref[fields:]


def weights_kernel(se_ref, sx_ref, ae_ref, am_ref, ax_ref, se_out, sx_out, ae_out, am_out, ax_out):
    for source, target in ((se_ref, se_out), (ae_ref, ae_out)):
        taps = [
            source[a, b].astype(jnp.float32).T for a in range(3) for b in range(3)
        ]
        target[...] = jnp.concatenate(taps, axis=1).astype(jnp.bfloat16)
    for source, target, turned in ((sx_ref, sx_out, True), (am_ref, am_out, False), (ax_ref, ax_out, True)):
        width, depth = source.shape[2:] if turned else source.shape[:1:-1]
        blank = jnp.zeros((width, pad_to(depth, PACKED) - depth), jnp.float32)
        groups = []
        for b in range(3):
            pieces = []
            for a in range(3):
                tap = 0.5 * source[a, b].astype(jnp.float32)
                pieces += [tap if turned else tap.T, blank]
            groups.append(jnp.concatenate(pieces, axis=1))
        target[...] = jnp.concatenate(groups, axis=0).astype(jnp.bfloat16)


def ordered(tasks, ring, lag, stage):
    depends = []
    late = []
    writer, readers = {}, {}
    for index, (_, reads, writes, _) in enumerate(tasks):
        needed = set()
        reads = [(name, row % ring) for name, row in reads]
        writes = [(name, row % ring) for name, row in writes]
        for cell in reads:
            if cell in writer:
                needed.add(writer[cell])
        for cell in writes:
            needed.update(readers.pop(cell, ()))
            if cell in writer:
                needed.add(writer[cell])
        for cell in reads:
            readers.setdefault(cell, set()).add(index)
        for cell in writes:
            writer[cell] = index
        needed.discard(index)
        depends.append(needed)
        late.append(tasks[index][0] == FAR_LOAD or any(late[i] for i in needed))
    chosen_stage = [i for i in range(len(tasks)) if late[i] == bool(stage)]
    placed = {i: -lag for i in range(len(tasks)) if stage and not late[i]}
    order = []
    while len(order) < len(chosen_stage):
        ready = [i for i in chosen_stage if i not in placed and all(j in placed for j in depends[i])]
        rested = [i for i in ready if all(placed[j] + lag <= len(order) for j in depends[i])]
        if rested:
            chosen = max(rested, key=lambda i: (tasks[i][0], -i))
        else:
            chosen = min(ready, key=lambda i: max((placed[j] for j in depends[i]), default=-1))
        placed[chosen] = len(order)
        order.append(chosen)
    return [tasks[i][3] for i in order]


CHUNK = 2
LAG = 20
NEAR = 3
NEAR_LOAD = 0
FAR_LOAD = -1
HELD = 9
VMEM_GRANT = 24 * 1024 * 1024
PADS = {"sea_in": 2, "sea_hid": 2, "air_in": 2, "hid1": 2, "hid2": 4}


def forecast_kernel(sizes, stage, *refs):
    fields, surface, flux_count, hidden, blocks, rows = sizes
    loaded = range(NEAR, blocks) if stage else range(NEAR)
    block_refs = dict(zip(loaded, refs, strict=False))
    se_ref, sx_ref, ae_ref, am_ref, ax_ref = refs[len(loaded) : len(loaded) + 5]
    rest = refs[len(loaded) + 5 :]
    if stage:
        out_ref, planes = rest[HELD], rest[-1]
        rest = rest[HELD + 1 : -1]
    held = dict(zip(("sea_in", "sea_hid", "air_in", "hid1", "hid2"), rest, strict=False))
    air_now, sea_now, edge_in, mask_in = rest[5:]
    ring = blocks * rows
    kept = fields + surface + flux_count
    hidden_pad = held["sea_hid"].shape[0] - hidden

    def span(row, count):
        return pl.ds(row * LANES, count * LANES)

    def put(name, row, count, values):
        row %= ring
        pad = PADS[name]
        places = [row]
        if row < pad:
            places.append(row + ring)
        if row + count > ring - pad:
            places.append(row - ring)
        for place in places:
            low, high = max(place, -pad), min(place + count, ring + pad)
            piece = values[:, (low - place) * LANES : (high - place) * LANES]
            held[name][:, span(low + pad, high - low)] = piece

    def gather_rows(name, row, count, spread):
        start = row % ring + PADS[name]
        return jnp.concatenate(
            [held[name][:, span(start + spread * (a - 1), count)] for a in range(3)], axis=0
        )

    def put_sea_in(row, values):
        left, right = from_left(values, 1), from_right(values, 1)
        stacked = jnp.concatenate([left, values, right], axis=0).astype(jnp.bfloat16)
        put("sea_in", row, 1, stacked)

    def put_air_in(row, values, edge):
        fill = jnp.concatenate([edge, jnp.zeros((surface, LANES), jnp.float32)], axis=0)
        left, right = from_left(values, 1), from_right(values, 1, fill)
        stacked = jnp.concatenate([left, values, right], axis=0).astype(jnp.bfloat16)
        put("air_in", row, 1, stacked)

    def product(weight_ref, inputs):
        return jnp.dot(weight_ref[...], inputs, preferred_element_type=jnp.float32)

    def put_hidden(name, row, count, values):
        values = twice_gelu(values)
        if hidden_pad:
            blank = jnp.zeros((hidden_pad, values.shape[1]), jnp.float32)
            values = jnp.concatenate([values, blank], axis=0)
        put(name, row, count, values.astype(jnp.bfloat16))

    def side_sum(made, width, spread, index):
        piece = made[:, index * LANES : (index + 1) * LANES]
        left = from_left(piece[0:width], spread)
        right = from_right(piece[2 * width : 3 * width], spread)
        return piece[width : 2 * width] + left + right

    def sea_entry(row, count):
        put_hidden("sea_hid", row, count, product(se_ref, gather_rows("sea_in", row, count, 1)))

    def sea_exit(row, count):
        made = product(sx_ref, gather_rows("sea_hid", row, count, 1))
        for i in range(count):
            at = (row + i) % ring
            change = side_sum(made, surface, 1, i)
            old = sea_now[:, span(at, 1)]
            new = (old + mask_in[at : at + 1, :] * change).astype(jnp.bfloat16).astype(jnp.float32)
            sea_now[:, span(at, 1)] = new
            values = jnp.concatenate([air_now[:, span(at, 1)], new], axis=0)
            put_air_in(at, values, edge_in[:, span(at, 1)])

    def air_entry(row, count):
        put_hidden("hid1", row, count, product(ae_ref, gather_rows("air_in", row, count, 1)))

    def air_middle(row, count):
        made = product(am_ref, gather_rows("hid1", row, count, 2))
        sums = [side_sum(made, hidden, 2, i) for i in range(count)]
        put_hidden("hid2", row, count, jnp.concatenate(sums, axis=1))

    def air_exit(row, count, last):
        made = product(ax_ref, gather_rows("hid2", row, count, 4))
        for i in range(count):
            at = (row + i) % ring
            change = side_sum(made, fields + flux_count, 4, i)
            old = air_now[:, span(at, 1)]
            new = (old + change[0:fields]).astype(jnp.bfloat16).astype(jnp.float32)
            sea = sea_now[:, span(at, 1)]
            if last:
                planes[:, at - rows, :] = jnp.concatenate([new, sea], axis=0)
            else:
                air_now[:, span(at, 1)] = new
                flux = change[fields:].astype(jnp.bfloat16).astype(jnp.float32)
                put_sea_in(at, jnp.concatenate([sea, flux], axis=0))

    def load_rows(block, row, count):
        source = block_refs[block]
        for i in range(row, row + count):
            values = source[:, i * LANES : (i + 1) * LANES].astype(jnp.float32)
            at = block * rows + i
            air_now[:, span(at, 1)] = values[0:fields]
            sea_now[:, span(at, 1)] = values[fields : fields + surface]
            put_sea_in(at, values[fields:kept])
            tail = source[0:fields, rows * LANES : (rows + 1) * LANES].astype(jnp.float32)
            edge_in[:, span(at, 1)] = jnp.broadcast_to(tail[:, i : i + 1], (fields, LANES))

    for block, source in block_refs.items():
        tail = source[fields : fields + rows, rows * LANES : (rows + 1) * LANES]
        mask_in[block * rows : (block + 1) * rows, :] = tail.astype(jnp.float32)

    tasks = []

    def add(depth, first, last, body, reads, writes, spread):
        for row in range(first, last, CHUNK):
            seen = range(row - spread, row + CHUNK + spread)
            near = range(row, row + CHUNK)
            tasks.append(
                (
                    depth,
                    [(name, r) for name in reads for r in (near if name.endswith("now") else seen)],
                    [(name, r) for name in writes for r in near],
                    functools.partial(body, row, CHUNK),
                )
            )

    for block in range(blocks):
        for row in range(0, rows, CHUNK):
            near = range(block * rows + row, block * rows + row + CHUNK)
            writes = [(name, r) for name in ("sea_in", "air_now", "sea_now") for r in near]
            depth = NEAR_LOAD if block < NEAR else FAR_LOAD
            tasks.append((depth, [], writes, functools.partial(load_rows, block, row, CHUNK)))
    for step in range(STEPS):
        last = step == STEPS - 1
        base = 10 * step

        def reach(halo, last=last):
            return (rows - halo, 2 * rows + halo) if last else (0, ring)

        add(base + 1, *reach(8), sea_entry, ("sea_in",), ("sea_hid",), 1)
        add(base + 2, *reach(7), sea_exit, ("sea_hid", "sea_now", "air_now"), ("sea_now", "air_in"), 1)
        add(base + 3, *reach(6), air_entry, ("air_in",), ("hid1",), 1)
        add(base + 4, *reach(4), air_middle, ("hid1",), ("hid2",), 2)
        low, high = (rows, 2 * rows) if last else (rows - 10, 2 * rows + 10)
        writes = ("planes",) if last else ("air_now", "sea_in")
        body = functools.partial(air_exit, last=last)
        add(base + 5, low, high, body, ("hid2", "air_now", "sea_now"), writes, 4)
    for task in ordered(tasks, ring, LAG, stage):
        task()
    if stage:
        out_ref[...] = planes[...].astype(jnp.bfloat16)


def forecast(sizes, frame, weights):
    fields, surface, flux_count, hidden, blocks, rows = sizes
    ring = blocks * rows
    hidden_rows = pad_to(hidden, PACKED)
    held = []
    for name, depth in (
        ("sea_in", 3 * (surface + flux_count)),
        ("sea_hid", hidden_rows),
        ("air_in", 3 * (fields + surface)),
        ("hid1", hidden_rows),
        ("hid2", hidden_rows),
    ):
        held.append(pltpu.VMEM((depth, (ring + 2 * PADS[name]) * LANES), jnp.bfloat16))
    for depth in (fields, surface, fields):
        held.append(pltpu.VMEM((depth, ring * LANES), jnp.float32))
    held.append(pltpu.VMEM((ring, LANES), jnp.float32))
    cost = pl.CostEstimate(flops=2000000000, bytes_accessed=3000000, transcendentals=1000000)
    state = pl.pallas_call(
        functools.partial(forecast_kernel, sizes, 0),
        out_shape=tuple(held),
        in_specs=vmem_specs(NEAR + 5),
        out_specs=tuple(vmem_specs(HELD)),
        cost_estimate=pl.CostEstimate(flops=1000, bytes_accessed=1000, transcendentals=0),
        compiler_params=pltpu.CompilerParams(vmem_limit_bytes=VMEM_GRANT),
        name="forecast_near",
    )(*in_vmem(*frame[:NEAR], *weights))
    far = blocks - NEAR
    return pl.pallas_call(
        functools.partial(forecast_kernel, sizes, 1),
        out_shape=(pltpu.VMEM((fields + surface, rows, LANES), jnp.bfloat16), *held),
        in_specs=vmem_specs(far + 5 + HELD),
        out_specs=tuple(vmem_specs(1 + HELD)),
        scratch_shapes=[pltpu.VMEM((fields + surface, rows, LANES), jnp.float32)],
        input_output_aliases={far + 5 + i: 1 + i for i in range(HELD)},
        cost_estimate=cost,
        compiler_params=pltpu.CompilerParams(vmem_limit_bytes=VMEM_GRANT),
        name="forecast_far",
    )(*in_vmem(*frame[NEAR:], *weights, *state))[0]


def belt_shards(
    atmosphere, ocean_state, fluxes, sea_mask, air_entry, air_middle, air_exit, sea_entry, sea_exit
):
    blocks = lax.axis_size("sp")
    position = lax.axis_index("sec")
    members, fields, rows, cols = atmosphere.shape
    surface, flux_count = ocean_state.shape[1], fluxes.shape[1]
    hidden = air_middle.shape[3]
    hidden_rows = pad_to(hidden, PACKED)
    kept = fields + surface + flux_count
    swap = [(0, 1), (1, 0)]
    bf16, f32 = jnp.bfloat16, jnp.float32

    sent = jnp.where(position == 0, atmosphere[1], atmosphere[0])
    got = lax.ppermute(sent, "sec", swap)
    packed_shape = pltpu.VMEM((kept, (rows + 1) * LANES), bf16)
    small = pl.CostEstimate(flops=1000000, bytes_accessed=1000000, transcendentals=0)
    own = pl.pallas_call(
        pack_own_kernel,
        out_shape=packed_shape,
        in_specs=vmem_specs(4),
        out_specs=vmem_specs(1)[0],
        scratch_shapes=[pltpu.VMEM((kept, rows, LANES), f32)],
        cost_estimate=small,
        name="pack_own",
    )(atmosphere, ocean_state, fluxes, sea_mask)
    packed = pl.pallas_call(
        pack_got_kernel,
        out_shape=packed_shape,
        in_specs=vmem_specs(2),
        out_specs=vmem_specs(1)[0],
        scratch_shapes=[pltpu.VMEM((fields, rows, LANES), f32)],
        cost_estimate=small,
        name="pack_got",
    )(*in_vmem(own, got))

    weights = pl.pallas_call(
        weights_kernel,
        out_shape=(
            pltpu.VMEM((hidden, 9 * sea_entry.shape[2]), bf16),
            pltpu.VMEM((3 * surface, 3 * hidden_rows), bf16),
            pltpu.VMEM((hidden, 9 * air_entry.shape[2]), bf16),
            pltpu.VMEM((3 * hidden, 3 * hidden_rows), bf16),
            pltpu.VMEM((3 * (fields + flux_count), 3 * hidden_rows), bf16),
        ),
        in_specs=vmem_specs(5),
        out_specs=tuple(vmem_specs(5)),
        cost_estimate=pl.CostEstimate(flops=1000000, bytes_accessed=4000000, transcendentals=0),
        name="weights",
    )(sea_entry, jnp.swapaxes(sea_exit, 2, 3), air_entry, air_middle, jnp.swapaxes(air_exit, 2, 3))

    frame = [None] * blocks
    for index in range(blocks):
        shift = (1 - index) % blocks
        if shift == 0:
            frame[index] = packed
        else:
            pairs = [(i, (i + shift) % blocks) for i in range(blocks)]
            frame[index] = lax.ppermute(packed, "sp", pairs)

    sizes = (fields, surface, flux_count, hidden, blocks, rows)
    made = forecast(sizes, frame, weights)
    other = lax.ppermute(made, "sec", swap)
    return pl.pallas_call(
        merge_kernel,
        out_shape=(
            jax.ShapeDtypeStruct(atmosphere.shape, bf16),
            jax.ShapeDtypeStruct(ocean_state.shape, bf16),
        ),
        in_specs=vmem_specs(3),
        out_specs=tuple(vmem_specs(2)),
        cost_estimate=small,
        name="merge",
    )(*in_vmem(made, other, atmosphere))


def belt_fits(mesh, atmosphere, ocean_state, fluxes, sea_entry, sea_exit):
    sections, blocks = mesh.shape["sec"], mesh.shape["sp"]
    members = atmosphere.shape[0] // (mesh.shape["grp"] * mesh.shape["mb"])
    rows = atmosphere.shape[2] // blocks
    band = atmosphere.shape[3] // sections
    fields, surface, flux_count = atmosphere.shape[1], ocean_state.shape[1], fluxes.shape[1]
    return (
        sections == 2
        and members == 2
        and band == LANES
        and ocean_state.shape[3] == band
        and rows % SUBLANES == 0
        and rows <= LANES
        and rows >= 8
        and blocks > NEAR
        and 2 * rows + 10 <= blocks * rows
        and blocks * rows <= 64
        and rows <= surface + flux_count
        and all(c % SUBLANES == 0 for c in (fields, surface, flux_count, sea_entry.shape[3]))
        and (surface + flux_count) % PACKED == 0
        and (fields + surface) % PACKED == 0
    )


def solution(mesh):
    placed = (
        P(("grp", "mb"), None, "sp", "sec"),
        P(("grp", "mb"), None, "sp", None),
        P(("grp", "mb"), None, "sp", None),
        P("sp", None),
        P(),
        P(),
        P(),
        P(),
        P(),
    )

    def run(atmosphere, ocean_state, fluxes, sea_mask, air_entry, air_middle, air_exit, sea_entry, sea_exit):
        fits = belt_fits(mesh, atmosphere, ocean_state, fluxes, sea_entry, sea_exit)
        return jax.shard_map(
            belt_shards if fits else shards,
            mesh=mesh,
            in_specs=placed,
            out_specs=(P(("grp", "mb"), None, "sp", "sec"), P(("grp", "mb"), None, "sp", None)),
            check_vma=False,
        )(
            atmosphere, ocean_state, fluxes, sea_mask, air_entry, air_middle, air_exit, sea_entry, sea_exit
        )

    return run
```

```python
import functools

import jax
import jax.numpy as jnp
from jax import lax
from jax.experimental import pallas as pl
from jax.experimental.pallas import tpu as pltpu
from jax.sharding import PartitionSpec as P

STEPS = 2


dilations = (1, 2, 4)


def with_halo(block, sides, width):
    for axis, dim in sides:
        count = lax.axis_size(axis)
        forward = [(i, i + 1) for i in range(count - 1)]
        forward.append((count - 1, 0))
        backward = [(target, source) for source, target in forward]
        low = lax.ppermute(
            lax.slice_in_dim(block, block.shape[dim] - width, None, axis=dim), axis, forward
        )
        high = lax.ppermute(lax.slice_in_dim(block, 0, width, axis=dim), axis, backward)
        block = jnp.concatenate([low, block, high], axis=dim)
    return block


def spread_2(value, axis, source):
    kept = jnp.where(lax.axis_index(axis) == source, value, 0).astype(value.dtype)
    return lax.psum(kept, axis)


def tap_sum(source, weight, dilation):
    out_rows = source.shape[2] - 2 * dilation
    out_cols = source.shape[3] - 2 * dilation
    pieces = []
    for tap_row in range(3):
        for tap_col in range(3):
            sliced = lax.slice_in_dim(
                source, tap_row * dilation, tap_row * dilation + out_rows, axis=2
            )
            sliced = lax.slice_in_dim(
                sliced, tap_col * dilation, tap_col * dilation + out_cols, axis=3
            )
            pieces.append(sliced)
    stacked = jnp.concatenate(pieces, axis=1)
    flat_weight = weight.reshape(-1, weight.shape[3])
    return jnp.einsum("mkrc,ko->morc", stacked, flat_weight, preferred_element_type=jnp.float32)


def gelu_round(values):
    return jax.nn.gelu(values, approximate=True).astype(jnp.bfloat16)


def keep_columns(block, first_column, limit):
    columns = lax.iota(jnp.int32, block.shape[3]) + first_column
    inside = (columns >= 0) & (columns < limit)
    return jnp.where(inside[None, None, None, :], block, jnp.zeros_like(block))


def shards(
    atmosphere, ocean_state, fluxes, sea_mask, air_entry, air_middle, air_exit, sea_entry, sea_exit
):
    sections = lax.axis_size("sec")
    position = lax.axis_index("sec")
    is_ocean = position == sections - 1
    band_cols = atmosphere.shape[3]
    ocean_cols = ocean_state.shape[3]
    field_count = atmosphere.shape[1]
    sea_weight = sea_mask.astype(jnp.float32)
    air_weights = (air_entry, air_middle, air_exit)
    sea_weights = (sea_entry, sea_exit)

    def air_layer(extended, layer_index):
        produced = tap_sum(extended, air_weights[layer_index], dilations[layer_index])
        if layer_index < 2:
            return gelu_round(produced)
        return produced

    def air_blank(extended, layer_index):
        spread = dilations[layer_index]
        out_shape = (
            extended.shape[0],
            air_weights[layer_index].shape[3],
            extended.shape[2] - 2 * spread,
            extended.shape[3] - 2 * spread,
        )
        return jnp.zeros(out_shape, jnp.bfloat16 if layer_index < 2 else jnp.float32)

    def sea_layer(extended, layer_index):
        padded = jnp.pad(extended, ((0, 0), (0, 0), (0, 0), (1, 1)))
        produced = tap_sum(padded, sea_weights[layer_index], 1)
        if layer_index < 1:
            return gelu_round(produced)
        return produced

    def sea_blank(extended, layer_index):
        out_shape = (
            extended.shape[0],
            sea_weights[layer_index].shape[3],
            extended.shape[2] - 2,
            ocean_cols,
        )
        return jnp.zeros(out_shape, jnp.bfloat16 if layer_index < 1 else jnp.float32)

    def air_extend(current, layer_index, margin):
        extended = with_halo(current, (("sp", 2), ("sec", 3)), dilations[layer_index])
        margin = dilations[layer_index]
        limit = band_cols * sections if layer_index == 0 else ocean_cols
        extended = keep_columns(extended, position * band_cols - margin, limit)
        return (extended, margin - dilations[layer_index])

    def sea_extend(current):
        return with_halo(current, (("sp", 2),), 1)

    def run_segment(air_job, sea_job):
        air_current = None
        sea_current = None
        margin = 0
        if air_job is not None:
            air_current = jnp.concatenate(air_job, axis=1)
        if sea_job is not None:
            sea_current = jnp.concatenate(sea_job, axis=1)
        for layer_index in range(3):
            air_ready = None
            sea_ready = None
            if air_current is not None:
                air_ready, margin = air_extend(air_current, layer_index, margin)
            if sea_current is not None and layer_index < 2:
                sea_ready = sea_extend(sea_current)
            if air_ready is None and sea_ready is None:
                continue

            def on_sea(ready):
                air_given, sea_given = ready
                air_made = None if air_given is None else air_blank(air_given, layer_index)
                sea_made = None if sea_given is None else sea_layer(sea_given, layer_index)
                return (air_made, sea_made)

            def on_air(ready):
                air_given, sea_given = ready
                air_made = None if air_given is None else air_layer(air_given, layer_index)
                sea_made = None if sea_given is None else sea_blank(sea_given, layer_index)
                return (air_made, sea_made)

            air_next, sea_next = lax.cond(is_ocean, on_sea, on_air, (air_ready, sea_ready))
            if air_ready is not None:
                air_current = air_next
            if sea_ready is not None:
                sea_current = sea_next
        air_result = None
        sea_result = None
        if air_job is not None:
            previous = air_job[0]
            renewed = (previous.astype(jnp.float32) + air_current[:, :field_count]).astype(
                jnp.bfloat16
            )
            air_result = (renewed, air_current[:, field_count:].astype(jnp.bfloat16))
        if sea_job is not None:
            previous = sea_job[0]
            sea_result = (
                previous.astype(jnp.float32) + sea_weight[None, None] * sea_current
            ).astype(jnp.bfloat16)
        return (air_result, sea_result)

    air_now, sea_now, flux_now = (atmosphere, ocean_state, fluxes)
    for step_index in range(STEPS):
        sea_now = run_segment(None, (sea_now, flux_now))[1]
        shared = spread_2(sea_now, "sec", sections - 1)
        start_col = jnp.minimum(position, sections - 2) * band_cols
        own_band = lax.dynamic_slice_in_dim(shared, start_col, band_cols, 3)
        own_band = jnp.where(is_ocean, jnp.zeros_like(own_band), own_band)
        sea_now = shared
        air_now, flux_band = run_segment((air_now, own_band), None)[0]
        if step_index + 1 < STEPS:
            collected = lax.all_gather(flux_band, "sec", axis=3, tiled=True)
            flux_now = collected[:, :, :, :ocean_cols]
    return (air_now, sea_now)


LANES = 128
SUBLANES = 8
PACKED = 16


def pad_to(count, unit):
    return -(-count // unit) * unit


def tree_add(terms):
    total = terms[0]
    for term in terms[1:]:
        total = total + term
    return total


def twice_gelu(v):
    inner = v * (0.7978845608028654 + (0.7978845608028654 * 0.044715) * (v * v))
    return v + v * jnp.tanh(inner)


def lane_ids(rows):
    return lax.broadcasted_iota(jnp.int32, (rows, LANES), 1)


def from_left(v, distance, fill=0.0):
    return jnp.where(lane_ids(v.shape[0]) < distance, fill, pltpu.roll(v, distance, 1))


def from_right(v, distance, fill=0.0):
    rolled = pltpu.roll(v, LANES - distance, 1)
    return jnp.where(lane_ids(v.shape[0]) >= LANES - distance, fill, rolled)


def vmem_specs(count):
    return [pl.BlockSpec(memory_space=pltpu.VMEM)] * count


def in_vmem(*values):
    return tuple(pltpu.with_memory_space_constraint(value, pltpu.VMEM) for value in values)


def edge_of(bands):
    lanes = lane_ids(bands[0].shape[0])
    edge = jnp.where(lanes == 0, bands[0], 0.0)
    for row, band in enumerate(bands[1:], 1):
        edge = jnp.where(lanes == row, pltpu.roll(band, row, 1), edge)
    return edge


def pack_own_kernel(air_ref, sea_ref, flux_ref, mask_ref, out_ref, planes):
    fields = air_ref.shape[1]
    surface = sea_ref.shape[1]
    rows = air_ref.shape[2]
    kept = fields + surface + flux_ref.shape[1]
    section = lax.axis_index("sec")
    planes[0:fields] = air_ref[section].astype(jnp.float32)
    planes[fields : fields + surface] = sea_ref[section].astype(jnp.float32)
    planes[fields + surface : kept] = flux_ref[section].astype(jnp.float32)
    bands = []
    for row in range(rows):
        values = planes[:, row, :]
        out_ref[:, row * LANES : (row + 1) * LANES] = values.astype(jnp.bfloat16)
        bands.append(values[0:fields])
    mask = mask_ref[...].astype(jnp.float32)
    rest = jnp.zeros((kept - fields - rows, LANES), jnp.float32)
    tail = jnp.concatenate([edge_of(bands), mask, rest], axis=0)
    out_ref[:, rows * LANES : (rows + 1) * LANES] = tail.astype(jnp.bfloat16)


def pack_got_kernel(own_ref, got_ref, out_ref, planes):
    fields, rows = got_ref.shape[:2]
    first = lax.axis_index("sec") == 0
    planes[...] = got_ref[...].astype(jnp.float32)
    bands = [planes[:, row, :] for row in range(rows)]
    out_ref[fields:, :] = own_ref[fields:, :]

    @pl.when(first)
    def _():
        out_ref[0:fields, 0 : rows * LANES] = own_ref[0:fields, 0 : rows * LANES]
        out_ref[0:fields, rows * LANES :] = edge_of(bands).astype(jnp.bfloat16)

    @pl.when(jnp.logical_not(first))
    def _():
        out_ref[0:fields, rows * LANES :] = own_ref[0:fields, rows * LANES :]
        for row, band in enumerate(bands):
            out_ref[0:fields, row * LANES : (row + 1) * LANES] = band.astype(jnp.bfloat16)


def merge_kernel(made_ref, other_ref, air_ref, air_out, sea_out):
    fields = air_ref.shape[1]
    first = lax.axis_index("sec") == 0

    @pl.when(first)
    def _():
        air_out[0] = made_ref[0:fields]
        air_out[1] = other_ref[0:fields]
        sea_out[0] = made_ref[fields:]
        sea_out[1] = other_ref[fields:]

    @pl.when(jnp.logical_not(first))
    def _():
        air_out[...] = air_ref[...]
        sea_out[0] = other_ref[fields:]
        sea_out[1] = made_ref[fields:]


def weights_kernel(se_ref, sx_ref, ae_ref, am_ref, ax_ref, se_out, sx_out, ae_out, am_out, ax_out):
    for source, target in ((se_ref, se_out), (ae_ref, ae_out)):
        taps = [
            source[a, b].astype(jnp.float32).T for a in range(3) for b in range(3)
        ]
        target[...] = jnp.concatenate(taps, axis=1).astype(jnp.bfloat16)
    for source, target, turned in ((sx_ref, sx_out, True), (am_ref, am_out, False), (ax_ref, ax_out, True)):
        width, depth = source.shape[2:] if turned else source.shape[:1:-1]
        blank = jnp.zeros((width, pad_to(depth, PACKED) - depth), jnp.float32)
        groups = []
        for b in range(3):
            pieces = []
            for a in range(3):
                tap = 0.5 * source[a, b].astype(jnp.float32)
                pieces += [tap if turned else tap.T, blank]
            groups.append(jnp.concatenate(pieces, axis=1))
        target[...] = jnp.concatenate(groups, axis=0).astype(jnp.bfloat16)


def ordered(tasks, ring, lag, stage):
    depends = []
    late = []
    writer, readers = {}, {}
    for index, (_, reads, writes, _) in enumerate(tasks):
        needed = set()
        reads = [(name, row % ring) for name, row in reads]
        writes = [(name, row % ring) for name, row in writes]
        for cell in reads:
            if cell in writer:
                needed.add(writer[cell])
        for cell in writes:
            needed.update(readers.pop(cell, ()))
            if cell in writer:
                needed.add(writer[cell])
        for cell in reads:
            readers.setdefault(cell, set()).add(index)
        for cell in writes:
            writer[cell] = index
        needed.discard(index)
        depends.append(needed)
        late.append(tasks[index][0] == LATE_LOAD or any(late[i] for i in needed))
    chosen_stage = [i for i in range(len(tasks)) if late[i] == bool(stage)]
    placed = {i: -lag for i in range(len(tasks)) if stage and not late[i]}
    order = []
    while len(order) < len(chosen_stage):
        ready = [i for i in chosen_stage if i not in placed and all(j in placed for j in depends[i])]
        rested = [i for i in ready if all(placed[j] + lag <= len(order) for j in depends[i])]
        if rested:
            chosen = max(rested, key=lambda i: (tasks[i][0], -i))
        else:
            chosen = min(ready, key=lambda i: max((placed[j] for j in depends[i]), default=-1))
        placed[chosen] = len(order)
        order.append(chosen)
    return [tasks[i][3] for i in order]


CHUNK = 2
LAG = 20
LOAD = 0
LATE_LOAD = -1
HELD = 9
VMEM_GRANT = 24 * 1024 * 1024
PADS = {"sea_in": 2, "sea_hid": 2, "air_in": 2, "hid1": 2, "hid2": 4}


def forecast_kernel(sizes, stage, *refs):
    fields, surface, flux_count, hidden, blocks, rows = sizes
    loaded = range(1) if stage else range(1, blocks)
    block_refs = dict(zip(loaded, refs, strict=False))
    se_ref, sx_ref, ae_ref, am_ref, ax_ref = refs[len(loaded) : len(loaded) + 5]
    rest = refs[len(loaded) + 5 :]
    if stage:
        out_ref, planes = rest[HELD], rest[-1]
        rest = rest[HELD + 1 : -1]
    held = dict(zip(("sea_in", "sea_hid", "air_in", "hid1", "hid2"), rest, strict=False))
    air_now, sea_now, edge_in, mask_in = rest[5:]
    ring = blocks * rows
    kept = fields + surface + flux_count
    hidden_pad = held["sea_hid"].shape[0] - hidden

    def span(row, count):
        return pl.ds(row * LANES, count * LANES)

    def put(name, row, count, values):
        row %= ring
        pad = PADS[name]
        places = [row]
        if row < pad:
            places.append(row + ring)
        if row + count > ring - pad:
            places.append(row - ring)
        for place in places:
            low, high = max(place, -pad), min(place + count, ring + pad)
            piece = values[:, (low - place) * LANES : (high - place) * LANES]
            held[name][:, span(low + pad, high - low)] = piece

    def gather_rows(name, row, count, spread):
        start = row % ring + PADS[name]
        return jnp.concatenate(
            [held[name][:, span(start + spread * (a - 1), count)] for a in range(3)], axis=0
        )

    def put_sea_in(row, values):
        left, right = from_left(values, 1), from_right(values, 1)
        stacked = jnp.concatenate([left, values, right], axis=0).astype(jnp.bfloat16)
        put("sea_in", row, 1, stacked)

    def put_air_in(row, values, edge):
        fill = jnp.concatenate([edge, jnp.zeros((surface, LANES), jnp.float32)], axis=0)
        left, right = from_left(values, 1), from_right(values, 1, fill)
        stacked = jnp.concatenate([left, values, right], axis=0).astype(jnp.bfloat16)
        put("air_in", row, 1, stacked)

    def product(weight_ref, inputs):
        return jnp.dot(weight_ref[...], inputs, preferred_element_type=jnp.float32)

    def put_hidden(name, row, count, values):
        values = twice_gelu(values)
        if hidden_pad:
            blank = jnp.zeros((hidden_pad, values.shape[1]), jnp.float32)
            values = jnp.concatenate([values, blank], axis=0)
        put(name, row, count, values.astype(jnp.bfloat16))

    def side_sum(made, width, spread, index):
        piece = made[:, index * LANES : (index + 1) * LANES]
        left = from_left(piece[0:width], spread)
        right = from_right(piece[2 * width : 3 * width], spread)
        return piece[width : 2 * width] + left + right

    def sea_entry(row, count):
        put_hidden("sea_hid", row, count, product(se_ref, gather_rows("sea_in", row, count, 1)))

    def sea_exit(row, count):
        made = product(sx_ref, gather_rows("sea_hid", row, count, 1))
        for i in range(count):
            at = (row + i) % ring
            change = side_sum(made, surface, 1, i)
            old = sea_now[:, span(at, 1)]
            new = (old + mask_in[at : at + 1, :] * change).astype(jnp.bfloat16).astype(jnp.float32)
            sea_now[:, span(at, 1)] = new
            values = jnp.concatenate([air_now[:, span(at, 1)], new], axis=0)
            put_air_in(at, values, edge_in[:, span(at, 1)])

    def air_entry(row, count):
        put_hidden("hid1", row, count, product(ae_ref, gather_rows("air_in", row, count, 1)))

    def air_middle(row, count):
        made = product(am_ref, gather_rows("hid1", row, count, 2))
        sums = [side_sum(made, hidden, 2, i) for i in range(count)]
        put_hidden("hid2", row, count, jnp.concatenate(sums, axis=1))

    def air_exit(row, count, last):
        made = product(ax_ref, gather_rows("hid2", row, count, 4))
        for i in range(count):
            at = (row + i) % ring
            change = side_sum(made, fields + flux_count, 4, i)
            old = air_now[:, span(at, 1)]
            new = (old + change[0:fields]).astype(jnp.bfloat16).astype(jnp.float32)
            sea = sea_now[:, span(at, 1)]
            if last:
                planes[:, at - rows, :] = jnp.concatenate([new, sea], axis=0)
            else:
                air_now[:, span(at, 1)] = new
                flux = change[fields:].astype(jnp.bfloat16).astype(jnp.float32)
                put_sea_in(at, jnp.concatenate([sea, flux], axis=0))

    def load_rows(block, row, count):
        source = block_refs[block]
        for i in range(row, row + count):
            values = source[:, i * LANES : (i + 1) * LANES].astype(jnp.float32)
            at = block * rows + i
            air_now[:, span(at, 1)] = values[0:fields]
            sea_now[:, span(at, 1)] = values[fields : fields + surface]
            put_sea_in(at, values[fields:kept])
            tail = source[0:fields, rows * LANES : (rows + 1) * LANES].astype(jnp.float32)
            edge_in[:, span(at, 1)] = jnp.broadcast_to(tail[:, i : i + 1], (fields, LANES))

    for block, source in block_refs.items():
        tail = source[fields : fields + rows, rows * LANES : (rows + 1) * LANES]
        mask_in[block * rows : (block + 1) * rows, :] = tail.astype(jnp.float32)

    tasks = []

    def add(depth, first, last, body, reads, writes, spread):
        for row in range(first, last, CHUNK):
            seen = range(row - spread, row + CHUNK + spread)
            near = range(row, row + CHUNK)
            tasks.append(
                (
                    depth,
                    [(name, r) for name in reads for r in (near if name.endswith("now") else seen)],
                    [(name, r) for name in writes for r in near],
                    functools.partial(body, row, CHUNK),
                )
            )

    for block in range(blocks):
        for row in range(0, rows, CHUNK):
            near = range(block * rows + row, block * rows + row + CHUNK)
            writes = [(name, r) for name in ("sea_in", "air_now", "sea_now") for r in near]
            depth = LATE_LOAD if block == 0 else LOAD
            tasks.append((depth, [], writes, functools.partial(load_rows, block, row, CHUNK)))
    for step in range(STEPS):
        last = step == STEPS - 1
        base = 10 * step

        def reach(halo, last=last):
            return (rows - halo, 2 * rows + halo) if last else (0, ring)

        add(base + 1, *reach(8), sea_entry, ("sea_in",), ("sea_hid",), 1)
        add(base + 2, *reach(7), sea_exit, ("sea_hid", "sea_now", "air_now"), ("sea_now", "air_in"), 1)
        add(base + 3, *reach(6), air_entry, ("air_in",), ("hid1",), 1)
        add(base + 4, *reach(4), air_middle, ("hid1",), ("hid2",), 2)
        low, high = (rows, 2 * rows) if last else (rows - 10, 2 * rows + 10)
        writes = ("planes",) if last else ("air_now", "sea_in")
        body = functools.partial(air_exit, last=last)
        add(base + 5, low, high, body, ("hid2", "air_now", "sea_now"), writes, 4)
    for task in ordered(tasks, ring, LAG, stage):
        task()
    if stage:
        out_ref[...] = planes[...].astype(jnp.bfloat16)


def forecast(sizes, frame, weights):
    fields, surface, flux_count, hidden, blocks, rows = sizes
    ring = blocks * rows
    hidden_rows = pad_to(hidden, PACKED)
    held = []
    for name, depth in (
        ("sea_in", 3 * (surface + flux_count)),
        ("sea_hid", hidden_rows),
        ("air_in", 3 * (fields + surface)),
        ("hid1", hidden_rows),
        ("hid2", hidden_rows),
    ):
        held.append(pltpu.VMEM((depth, (ring + 2 * PADS[name]) * LANES), jnp.bfloat16))
    for depth in (fields, surface, fields):
        held.append(pltpu.VMEM((depth, ring * LANES), jnp.float32))
    held.append(pltpu.VMEM((ring, LANES), jnp.float32))
    cost = pl.CostEstimate(flops=2000000000, bytes_accessed=3000000, transcendentals=1000000)
    state = pl.pallas_call(
        functools.partial(forecast_kernel, sizes, 0),
        out_shape=tuple(held),
        in_specs=vmem_specs(blocks - 1 + 5),
        out_specs=tuple(vmem_specs(HELD)),
        cost_estimate=pl.CostEstimate(flops=1000, bytes_accessed=1000, transcendentals=0),
        compiler_params=pltpu.CompilerParams(vmem_limit_bytes=VMEM_GRANT),
        name="forecast_early",
    )(*in_vmem(*frame[1:], *weights))
    return pl.pallas_call(
        functools.partial(forecast_kernel, sizes, 1),
        out_shape=(pltpu.VMEM((fields + surface, rows, LANES), jnp.bfloat16), *held),
        in_specs=vmem_specs(1 + 5 + HELD),
        out_specs=tuple(vmem_specs(1 + HELD)),
        scratch_shapes=[pltpu.VMEM((fields + surface, rows, LANES), jnp.float32)],
        input_output_aliases={1 + 5 + i: 1 + i for i in range(HELD)},
        cost_estimate=cost,
        compiler_params=pltpu.CompilerParams(vmem_limit_bytes=VMEM_GRANT),
        name="forecast_late",
    )(*in_vmem(frame[0], *weights, *state))[0]


def belt_shards(
    atmosphere, ocean_state, fluxes, sea_mask, air_entry, air_middle, air_exit, sea_entry, sea_exit
):
    blocks = lax.axis_size("sp")
    position = lax.axis_index("sec")
    members, fields, rows, cols = atmosphere.shape
    surface, flux_count = ocean_state.shape[1], fluxes.shape[1]
    hidden = air_middle.shape[3]
    hidden_rows = pad_to(hidden, PACKED)
    kept = fields + surface + flux_count
    swap = [(0, 1), (1, 0)]
    bf16, f32 = jnp.bfloat16, jnp.float32

    sent = jnp.where(position == 0, atmosphere[1], atmosphere[0])
    got = lax.ppermute(sent, "sec", swap)
    packed_shape = pltpu.VMEM((kept, (rows + 1) * LANES), bf16)
    small = pl.CostEstimate(flops=1000000, bytes_accessed=1000000, transcendentals=0)
    own = pl.pallas_call(
        pack_own_kernel,
        out_shape=packed_shape,
        in_specs=vmem_specs(4),
        out_specs=vmem_specs(1)[0],
        scratch_shapes=[pltpu.VMEM((kept, rows, LANES), f32)],
        cost_estimate=small,
        name="pack_own",
    )(atmosphere, ocean_state, fluxes, sea_mask)
    packed = pl.pallas_call(
        pack_got_kernel,
        out_shape=packed_shape,
        in_specs=vmem_specs(2),
        out_specs=vmem_specs(1)[0],
        scratch_shapes=[pltpu.VMEM((fields, rows, LANES), f32)],
        cost_estimate=small,
        name="pack_got",
    )(*in_vmem(own, got))

    weights = pl.pallas_call(
        weights_kernel,
        out_shape=(
            pltpu.VMEM((hidden, 9 * sea_entry.shape[2]), bf16),
            pltpu.VMEM((3 * surface, 3 * hidden_rows), bf16),
            pltpu.VMEM((hidden, 9 * air_entry.shape[2]), bf16),
            pltpu.VMEM((3 * hidden, 3 * hidden_rows), bf16),
            pltpu.VMEM((3 * (fields + flux_count), 3 * hidden_rows), bf16),
        ),
        in_specs=vmem_specs(5),
        out_specs=tuple(vmem_specs(5)),
        cost_estimate=pl.CostEstimate(flops=1000000, bytes_accessed=4000000, transcendentals=0),
        name="weights",
    )(sea_entry, jnp.swapaxes(sea_exit, 2, 3), air_entry, air_middle, jnp.swapaxes(air_exit, 2, 3))

    frame = [None] * blocks
    for index in range(blocks):
        shift = (1 - index) % blocks
        if shift == 0:
            frame[index] = packed
        else:
            pairs = [(i, (i + shift) % blocks) for i in range(blocks)]
            frame[index] = lax.ppermute(packed, "sp", pairs)

    sizes = (fields, surface, flux_count, hidden, blocks, rows)
    made = forecast(sizes, frame, weights)
    other = lax.ppermute(made, "sec", swap)
    return pl.pallas_call(
        merge_kernel,
        out_shape=(
            jax.ShapeDtypeStruct(atmosphere.shape, bf16),
            jax.ShapeDtypeStruct(ocean_state.shape, bf16),
        ),
        in_specs=vmem_specs(3),
        out_specs=tuple(vmem_specs(2)),
        cost_estimate=small,
        name="merge",
    )(*in_vmem(made, other, atmosphere))


def belt_fits(mesh, atmosphere, ocean_state, fluxes, sea_entry, sea_exit):
    sections, blocks = mesh.shape["sec"], mesh.shape["sp"]
    members = atmosphere.shape[0] // (mesh.shape["grp"] * mesh.shape["mb"])
    rows = atmosphere.shape[2] // blocks
    band = atmosphere.shape[3] // sections
    fields, surface, flux_count = atmosphere.shape[1], ocean_state.shape[1], fluxes.shape[1]
    return (
        sections == 2
        and members == 2
        and band == LANES
        and ocean_state.shape[3] == band
        and rows % SUBLANES == 0
        and rows <= LANES
        and rows >= 8
        and 2 * rows + 10 <= blocks * rows
        and blocks * rows <= 64
        and rows <= surface + flux_count
        and all(c % SUBLANES == 0 for c in (fields, surface, flux_count, sea_entry.shape[3]))
        and (surface + flux_count) % PACKED == 0
        and (fields + surface) % PACKED == 0
    )


def solution(mesh):
    placed = (
        P(("grp", "mb"), None, "sp", "sec"),
        P(("grp", "mb"), None, "sp", None),
        P(("grp", "mb"), None, "sp", None),
        P("sp", None),
        P(),
        P(),
        P(),
        P(),
        P(),
    )

    def run(atmosphere, ocean_state, fluxes, sea_mask, air_entry, air_middle, air_exit, sea_entry, sea_exit):
        fits = belt_fits(mesh, atmosphere, ocean_state, fluxes, sea_entry, sea_exit)
        return jax.shard_map(
            belt_shards if fits else shards,
            mesh=mesh,
            in_specs=placed,
            out_specs=(P(("grp", "mb"), None, "sp", "sec"), P(("grp", "mb"), None, "sp", None)),
            check_vma=False,
        )(
            atmosphere, ocean_state, fluxes, sea_mask, air_entry, air_middle, air_exit, sea_entry, sea_exit
        )

    return run
```

```python
import functools

import jax
import jax.numpy as jnp
from jax import lax
from jax.experimental import pallas as pl
from jax.experimental.pallas import tpu as pltpu
from jax.sharding import PartitionSpec as P

STEPS = 2


dilations = (1, 2, 4)


def with_halo(block, sides, width):
    for axis, dim in sides:
        count = lax.axis_size(axis)
        forward = [(i, i + 1) for i in range(count - 1)]
        forward.append((count - 1, 0))
        backward = [(target, source) for source, target in forward]
        low = lax.ppermute(
            lax.slice_in_dim(block, block.shape[dim] - width, None, axis=dim), axis, forward
        )
        high = lax.ppermute(lax.slice_in_dim(block, 0, width, axis=dim), axis, backward)
        block = jnp.concatenate([low, block, high], axis=dim)
    return block


def spread_2(value, axis, source):
    kept = jnp.where(lax.axis_index(axis) == source, value, 0).astype(value.dtype)
    return lax.psum(kept, axis)


def tap_sum(source, weight, dilation):
    out_rows = source.shape[2] - 2 * dilation
    out_cols = source.shape[3] - 2 * dilation
    pieces = []
    for tap_row in range(3):
        for tap_col in range(3):
            sliced = lax.slice_in_dim(
                source, tap_row * dilation, tap_row * dilation + out_rows, axis=2
            )
            sliced = lax.slice_in_dim(
                sliced, tap_col * dilation, tap_col * dilation + out_cols, axis=3
            )
            pieces.append(sliced)
    stacked = jnp.concatenate(pieces, axis=1)
    flat_weight = weight.reshape(-1, weight.shape[3])
    return jnp.einsum("mkrc,ko->morc", stacked, flat_weight, preferred_element_type=jnp.float32)


def gelu_round(values):
    return jax.nn.gelu(values, approximate=True).astype(jnp.bfloat16)


def keep_columns(block, first_column, limit):
    columns = lax.iota(jnp.int32, block.shape[3]) + first_column
    inside = (columns >= 0) & (columns < limit)
    return jnp.where(inside[None, None, None, :], block, jnp.zeros_like(block))


def shards(
    atmosphere, ocean_state, fluxes, sea_mask, air_entry, air_middle, air_exit, sea_entry, sea_exit
):
    sections = lax.axis_size("sec")
    position = lax.axis_index("sec")
    is_ocean = position == sections - 1
    band_cols = atmosphere.shape[3]
    ocean_cols = ocean_state.shape[3]
    field_count = atmosphere.shape[1]
    sea_weight = sea_mask.astype(jnp.float32)
    air_weights = (air_entry, air_middle, air_exit)
    sea_weights = (sea_entry, sea_exit)

    def air_layer(extended, layer_index):
        produced = tap_sum(extended, air_weights[layer_index], dilations[layer_index])
        if layer_index < 2:
            return gelu_round(produced)
        return produced

    def air_blank(extended, layer_index):
        spread = dilations[layer_index]
        out_shape = (
            extended.shape[0],
            air_weights[layer_index].shape[3],
            extended.shape[2] - 2 * spread,
            extended.shape[3] - 2 * spread,
        )
        return jnp.zeros(out_shape, jnp.bfloat16 if layer_index < 2 else jnp.float32)

    def sea_layer(extended, layer_index):
        padded = jnp.pad(extended, ((0, 0), (0, 0), (0, 0), (1, 1)))
        produced = tap_sum(padded, sea_weights[layer_index], 1)
        if layer_index < 1:
            return gelu_round(produced)
        return produced

    def sea_blank(extended, layer_index):
        out_shape = (
            extended.shape[0],
            sea_weights[layer_index].shape[3],
            extended.shape[2] - 2,
            ocean_cols,
        )
        return jnp.zeros(out_shape, jnp.bfloat16 if layer_index < 1 else jnp.float32)

    def air_extend(current, layer_index, margin):
        extended = with_halo(current, (("sp", 2), ("sec", 3)), dilations[layer_index])
        margin = dilations[layer_index]
        limit = band_cols * sections if layer_index == 0 else ocean_cols
        extended = keep_columns(extended, position * band_cols - margin, limit)
        return (extended, margin - dilations[layer_index])

    def sea_extend(current):
        return with_halo(current, (("sp", 2),), 1)

    def run_segment(air_job, sea_job):
        air_current = None
        sea_current = None
        margin = 0
        if air_job is not None:
            air_current = jnp.concatenate(air_job, axis=1)
        if sea_job is not None:
            sea_current = jnp.concatenate(sea_job, axis=1)
        for layer_index in range(3):
            air_ready = None
            sea_ready = None
            if air_current is not None:
                air_ready, margin = air_extend(air_current, layer_index, margin)
            if sea_current is not None and layer_index < 2:
                sea_ready = sea_extend(sea_current)
            if air_ready is None and sea_ready is None:
                continue

            def on_sea(ready):
                air_given, sea_given = ready
                air_made = None if air_given is None else air_blank(air_given, layer_index)
                sea_made = None if sea_given is None else sea_layer(sea_given, layer_index)
                return (air_made, sea_made)

            def on_air(ready):
                air_given, sea_given = ready
                air_made = None if air_given is None else air_layer(air_given, layer_index)
                sea_made = None if sea_given is None else sea_blank(sea_given, layer_index)
                return (air_made, sea_made)

            air_next, sea_next = lax.cond(is_ocean, on_sea, on_air, (air_ready, sea_ready))
            if air_ready is not None:
                air_current = air_next
            if sea_ready is not None:
                sea_current = sea_next
        air_result = None
        sea_result = None
        if air_job is not None:
            previous = air_job[0]
            renewed = (previous.astype(jnp.float32) + air_current[:, :field_count]).astype(
                jnp.bfloat16
            )
            air_result = (renewed, air_current[:, field_count:].astype(jnp.bfloat16))
        if sea_job is not None:
            previous = sea_job[0]
            sea_result = (
                previous.astype(jnp.float32) + sea_weight[None, None] * sea_current
            ).astype(jnp.bfloat16)
        return (air_result, sea_result)

    air_now, sea_now, flux_now = (atmosphere, ocean_state, fluxes)
    for step_index in range(STEPS):
        sea_now = run_segment(None, (sea_now, flux_now))[1]
        shared = spread_2(sea_now, "sec", sections - 1)
        start_col = jnp.minimum(position, sections - 2) * band_cols
        own_band = lax.dynamic_slice_in_dim(shared, start_col, band_cols, 3)
        own_band = jnp.where(is_ocean, jnp.zeros_like(own_band), own_band)
        sea_now = shared
        air_now, flux_band = run_segment((air_now, own_band), None)[0]
        if step_index + 1 < STEPS:
            collected = lax.all_gather(flux_band, "sec", axis=3, tiled=True)
            flux_now = collected[:, :, :, :ocean_cols]
    return (air_now, sea_now)


LANES = 128
SUBLANES = 8
PACKED = 16


def pad_to(count, unit):
    return -(-count // unit) * unit


def tree_add(terms):
    total = terms[0]
    for term in terms[1:]:
        total = total + term
    return total


def twice_gelu(v):
    inner = v * (0.7978845608028654 + (0.7978845608028654 * 0.044715) * (v * v))
    return v + v * jnp.tanh(inner)


def lane_ids(rows):
    return lax.broadcasted_iota(jnp.int32, (rows, LANES), 1)


def from_left(v, distance, fill=0.0):
    return jnp.where(lane_ids(v.shape[0]) < distance, fill, pltpu.roll(v, distance, 1))


def from_right(v, distance, fill=0.0):
    rolled = pltpu.roll(v, LANES - distance, 1)
    return jnp.where(lane_ids(v.shape[0]) >= LANES - distance, fill, rolled)


def vmem_specs(count):
    return [pl.BlockSpec(memory_space=pltpu.VMEM)] * count


def in_vmem(*values):
    return tuple(pltpu.with_memory_space_constraint(value, pltpu.VMEM) for value in values)


def edge_of(bands):
    lanes = lane_ids(bands[0].shape[0])
    edge = jnp.where(lanes == 0, bands[0], 0.0)
    for row, band in enumerate(bands[1:], 1):
        edge = jnp.where(lanes == row, pltpu.roll(band, row, 1), edge)
    return edge


def pack_own_kernel(air_ref, sea_ref, flux_ref, mask_ref, out_ref, planes):
    fields = air_ref.shape[1]
    surface = sea_ref.shape[1]
    rows = air_ref.shape[2]
    kept = fields + surface + flux_ref.shape[1]
    section = lax.axis_index("sec")
    planes[0:fields] = air_ref[section].astype(jnp.float32)
    planes[fields : fields + surface] = sea_ref[section].astype(jnp.float32)
    planes[fields + surface : kept] = flux_ref[section].astype(jnp.float32)
    bands = []
    for row in range(rows):
        values = planes[:, row, :]
        out_ref[:, row * LANES : (row + 1) * LANES] = values.astype(jnp.bfloat16)
        bands.append(values[0:fields])
    mask = mask_ref[...].astype(jnp.float32)
    rest = jnp.zeros((kept - fields - rows, LANES), jnp.float32)
    tail = jnp.concatenate([edge_of(bands), mask, rest], axis=0)
    out_ref[:, rows * LANES : (rows + 1) * LANES] = tail.astype(jnp.bfloat16)


def pack_got_kernel(own_ref, got_ref, out_ref, planes):
    fields, rows = got_ref.shape[1:3]
    section = lax.axis_index("sec")
    first = section == 0
    planes[...] = got_ref[section].astype(jnp.float32)
    bands = [planes[:, row, :] for row in range(rows)]
    out_ref[fields:, :] = own_ref[fields:, :]

    @pl.when(first)
    def _():
        out_ref[0:fields, 0 : rows * LANES] = own_ref[0:fields, 0 : rows * LANES]
        out_ref[0:fields, rows * LANES :] = edge_of(bands).astype(jnp.bfloat16)

    @pl.when(jnp.logical_not(first))
    def _():
        out_ref[0:fields, rows * LANES :] = own_ref[0:fields, rows * LANES :]
        for row, band in enumerate(bands):
            out_ref[0:fields, row * LANES : (row + 1) * LANES] = band.astype(jnp.bfloat16)


def merge_kernel(made_ref, other_ref, air_ref, air_out, sea_out):
    fields = air_ref.shape[1]
    first = lax.axis_index("sec") == 0

    @pl.when(first)
    def _():
        air_out[0] = made_ref[0:fields]
        air_out[1] = other_ref[0:fields]
        sea_out[0] = made_ref[fields:]
        sea_out[1] = other_ref[fields:]

    @pl.when(jnp.logical_not(first))
    def _():
        air_out[...] = air_ref[...]
        sea_out[0] = other_ref[fields:]
        sea_out[1] = made_ref[fields:]


def weights_kernel(se_ref, sx_ref, ae_ref, am_ref, ax_ref, se_out, sx_out, ae_out, am_out, ax_out):
    for source, target in ((se_ref, se_out), (ae_ref, ae_out)):
        taps = [
            source[a, b].astype(jnp.float32).T for a in range(3) for b in range(3)
        ]
        target[...] = jnp.concatenate(taps, axis=1).astype(jnp.bfloat16)
    for source, target, turned in ((sx_ref, sx_out, True), (am_ref, am_out, False), (ax_ref, ax_out, True)):
        width, depth = source.shape[2:] if turned else source.shape[:1:-1]
        blank = jnp.zeros((width, pad_to(depth, PACKED) - depth), jnp.float32)
        groups = []
        for b in range(3):
            pieces = []
            for a in range(3):
                tap = 0.5 * source[a, b].astype(jnp.float32)
                pieces += [tap if turned else tap.T, blank]
            groups.append(jnp.concatenate(pieces, axis=1))
        target[...] = jnp.concatenate(groups, axis=0).astype(jnp.bfloat16)


def prepare_weights(sea_entry, sea_exit, air_entry, air_middle, air_exit):
    hidden, surface, produced = air_middle.shape[3], sea_exit.shape[3], air_exit.shape[3]
    hidden_rows = pad_to(hidden, PACKED)
    return pl.pallas_call(
        weights_kernel,
        out_shape=(
            pltpu.VMEM((hidden, 9 * sea_entry.shape[2]), jnp.bfloat16),
            pltpu.VMEM((3 * surface, 3 * hidden_rows), jnp.bfloat16),
            pltpu.VMEM((hidden, 9 * air_entry.shape[2]), jnp.bfloat16),
            pltpu.VMEM((3 * hidden, 3 * hidden_rows), jnp.bfloat16),
            pltpu.VMEM((3 * produced, 3 * hidden_rows), jnp.bfloat16),
        ),
        in_specs=vmem_specs(5),
        out_specs=tuple(vmem_specs(5)),
        cost_estimate=pl.CostEstimate(flops=1000000, bytes_accessed=4000000, transcendentals=0),
        name="weights",
    )(sea_entry, jnp.swapaxes(sea_exit, 2, 3), air_entry, air_middle, jnp.swapaxes(air_exit, 2, 3))


def ordered(tasks, ring, lag, stage):
    depends = []
    late = []
    writer, readers = {}, {}
    for index, (_, reads, writes, _) in enumerate(tasks):
        needed = set()
        reads = [(name, row % ring) for name, row in reads]
        writes = [(name, row % ring) for name, row in writes]
        for cell in reads:
            if cell in writer:
                needed.add(writer[cell])
        for cell in writes:
            needed.update(readers.pop(cell, ()))
            if cell in writer:
                needed.add(writer[cell])
        for cell in reads:
            readers.setdefault(cell, set()).add(index)
        for cell in writes:
            writer[cell] = index
        needed.discard(index)
        depends.append(needed)
        late.append(tasks[index][0] == LATE_LOAD or any(late[i] for i in needed))
    chosen_stage = [i for i in range(len(tasks)) if late[i] == bool(stage)]
    placed = {i: -lag for i in range(len(tasks)) if stage and not late[i]}
    order = []
    while len(order) < len(chosen_stage):
        ready = [i for i in chosen_stage if i not in placed and all(j in placed for j in depends[i])]
        rested = [i for i in ready if all(placed[j] + lag <= len(order) for j in depends[i])]
        if rested:
            chosen = max(rested, key=lambda i: (tasks[i][0], -i))
        else:
            chosen = min(ready, key=lambda i: max((placed[j] for j in depends[i]), default=-1))
        placed[chosen] = len(order)
        order.append(chosen)
    return [tasks[i][3] for i in order]


CHUNK = 2
LAG = 20
LOAD = 0
LATE_LOAD = -1
HELD = 9
VMEM_GRANT = 24 * 1024 * 1024
PADS = {"sea_in": 2, "sea_hid": 2, "air_in": 2, "hid1": 2, "hid2": 4}


def forecast_kernel(sizes, stage, *refs):
    fields, surface, flux_count, hidden, blocks, rows = sizes
    loaded = range(1) if stage else range(1, blocks)
    block_refs = dict(zip(loaded, refs, strict=False))
    se_ref, sx_ref, ae_ref, am_ref, ax_ref = refs[len(loaded) : len(loaded) + 5]
    rest = refs[len(loaded) + 5 :]
    if stage:
        out_ref, planes = rest[HELD], rest[-1]
        rest = rest[HELD + 1 : -1]
    held = dict(zip(("sea_in", "sea_hid", "air_in", "hid1", "hid2"), rest, strict=False))
    air_now, sea_now, edge_in, mask_in = rest[5:]
    ring = blocks * rows
    kept = fields + surface + flux_count
    hidden_pad = held["sea_hid"].shape[0] - hidden

    def span(row, count):
        return pl.ds(row * LANES, count * LANES)

    def put(name, row, count, values):
        row %= ring
        pad = PADS[name]
        places = [row]
        if row < pad:
            places.append(row + ring)
        if row + count > ring - pad:
            places.append(row - ring)
        for place in places:
            low, high = max(place, -pad), min(place + count, ring + pad)
            piece = values[:, (low - place) * LANES : (high - place) * LANES]
            held[name][:, span(low + pad, high - low)] = piece

    def gather_rows(name, row, count, spread):
        start = row % ring + PADS[name]
        return jnp.concatenate(
            [held[name][:, span(start + spread * (a - 1), count)] for a in range(3)], axis=0
        )

    def put_sea_in(row, values):
        left, right = from_left(values, 1), from_right(values, 1)
        stacked = jnp.concatenate([left, values, right], axis=0).astype(jnp.bfloat16)
        put("sea_in", row, 1, stacked)

    def put_air_in(row, values, edge):
        fill = jnp.concatenate([edge, jnp.zeros((surface, LANES), jnp.float32)], axis=0)
        left, right = from_left(values, 1), from_right(values, 1, fill)
        stacked = jnp.concatenate([left, values, right], axis=0).astype(jnp.bfloat16)
        put("air_in", row, 1, stacked)

    def product(weight_ref, inputs):
        return jnp.dot(weight_ref[...], inputs, preferred_element_type=jnp.float32)

    def put_hidden(name, row, count, values):
        values = twice_gelu(values)
        if hidden_pad:
            blank = jnp.zeros((hidden_pad, values.shape[1]), jnp.float32)
            values = jnp.concatenate([values, blank], axis=0)
        put(name, row, count, values.astype(jnp.bfloat16))

    def side_sum(made, width, spread, index):
        piece = made[:, index * LANES : (index + 1) * LANES]
        left = from_left(piece[0:width], spread)
        right = from_right(piece[2 * width : 3 * width], spread)
        return piece[width : 2 * width] + left + right

    def sea_entry(row, count):
        put_hidden("sea_hid", row, count, product(se_ref, gather_rows("sea_in", row, count, 1)))

    def sea_exit(row, count):
        made = product(sx_ref, gather_rows("sea_hid", row, count, 1))
        for i in range(count):
            at = (row + i) % ring
            change = side_sum(made, surface, 1, i)
            old = sea_now[:, span(at, 1)]
            new = (old + mask_in[at : at + 1, :] * change).astype(jnp.bfloat16).astype(jnp.float32)
            sea_now[:, span(at, 1)] = new
            values = jnp.concatenate([air_now[:, span(at, 1)], new], axis=0)
            put_air_in(at, values, edge_in[:, span(at, 1)])

    def air_entry(row, count):
        put_hidden("hid1", row, count, product(ae_ref, gather_rows("air_in", row, count, 1)))

    def air_middle(row, count):
        made = product(am_ref, gather_rows("hid1", row, count, 2))
        sums = [side_sum(made, hidden, 2, i) for i in range(count)]
        put_hidden("hid2", row, count, jnp.concatenate(sums, axis=1))

    def air_exit(row, count, last):
        made = product(ax_ref, gather_rows("hid2", row, count, 4))
        for i in range(count):
            at = (row + i) % ring
            change = side_sum(made, fields + flux_count, 4, i)
            old = air_now[:, span(at, 1)]
            new = (old + change[0:fields]).astype(jnp.bfloat16).astype(jnp.float32)
            sea = sea_now[:, span(at, 1)]
            if last:
                planes[:, at - rows, :] = jnp.concatenate([new, sea], axis=0)
            else:
                air_now[:, span(at, 1)] = new
                flux = change[fields:].astype(jnp.bfloat16).astype(jnp.float32)
                put_sea_in(at, jnp.concatenate([sea, flux], axis=0))

    def load_rows(block, row, count):
        source = block_refs[block]
        for i in range(row, row + count):
            values = source[:, i * LANES : (i + 1) * LANES].astype(jnp.float32)
            at = block * rows + i
            air_now[:, span(at, 1)] = values[0:fields]
            sea_now[:, span(at, 1)] = values[fields : fields + surface]
            put_sea_in(at, values[fields:kept])
            tail = source[0:fields, rows * LANES : (rows + 1) * LANES].astype(jnp.float32)
            edge_in[:, span(at, 1)] = jnp.broadcast_to(tail[:, i : i + 1], (fields, LANES))

    for block, source in block_refs.items():
        tail = source[fields : fields + rows, rows * LANES : (rows + 1) * LANES]
        mask_in[block * rows : (block + 1) * rows, :] = tail.astype(jnp.float32)

    tasks = []

    def add(depth, first, last, body, reads, writes, spread):
        for row in range(first, last, CHUNK):
            seen = range(row - spread, row + CHUNK + spread)
            near = range(row, row + CHUNK)
            tasks.append(
                (
                    depth,
                    [(name, r) for name in reads for r in (near if name.endswith("now") else seen)],
                    [(name, r) for name in writes for r in near],
                    functools.partial(body, row, CHUNK),
                )
            )

    for block in range(blocks):
        for row in range(0, rows, CHUNK):
            near = range(block * rows + row, block * rows + row + CHUNK)
            writes = [(name, r) for name in ("sea_in", "air_now", "sea_now") for r in near]
            depth = LATE_LOAD if block == 0 else LOAD
            tasks.append((depth, [], writes, functools.partial(load_rows, block, row, CHUNK)))
    for step in range(STEPS):
        last = step == STEPS - 1
        base = 10 * step

        def reach(halo, last=last):
            return (rows - halo, 2 * rows + halo) if last else (0, ring)

        add(base + 1, *reach(8), sea_entry, ("sea_in",), ("sea_hid",), 1)
        add(base + 2, *reach(7), sea_exit, ("sea_hid", "sea_now", "air_now"), ("sea_now", "air_in"), 1)
        add(base + 3, *reach(6), air_entry, ("air_in",), ("hid1",), 1)
        add(base + 4, *reach(4), air_middle, ("hid1",), ("hid2",), 2)
        low, high = (rows, 2 * rows) if last else (rows - 10, 2 * rows + 10)
        writes = ("planes",) if last else ("air_now", "sea_in")
        body = functools.partial(air_exit, last=last)
        add(base + 5, low, high, body, ("hid2", "air_now", "sea_now"), writes, 4)
    for task in ordered(tasks, ring, LAG, stage):
        task()
    if stage:
        out_ref[...] = planes[...].astype(jnp.bfloat16)


def forecast(sizes, frame, weights):
    fields, surface, flux_count, hidden, blocks, rows = sizes
    ring = blocks * rows
    hidden_rows = pad_to(hidden, PACKED)
    held = []
    for name, depth in (
        ("sea_in", 3 * (surface + flux_count)),
        ("sea_hid", hidden_rows),
        ("air_in", 3 * (fields + surface)),
        ("hid1", hidden_rows),
        ("hid2", hidden_rows),
    ):
        held.append(pltpu.VMEM((depth, (ring + 2 * PADS[name]) * LANES), jnp.bfloat16))
    for depth in (fields, surface, fields):
        held.append(pltpu.VMEM((depth, ring * LANES), jnp.float32))
    held.append(pltpu.VMEM((ring, LANES), jnp.float32))
    cost = pl.CostEstimate(flops=2000000000, bytes_accessed=3000000, transcendentals=1000000)
    state = pl.pallas_call(
        functools.partial(forecast_kernel, sizes, 0),
        out_shape=tuple(held),
        in_specs=vmem_specs(blocks - 1 + 5),
        out_specs=tuple(vmem_specs(HELD)),
        cost_estimate=pl.CostEstimate(flops=1000, bytes_accessed=1000, transcendentals=0),
        compiler_params=pltpu.CompilerParams(vmem_limit_bytes=VMEM_GRANT),
        name="forecast_early",
    )(*in_vmem(*frame[1:], *weights))
    return pl.pallas_call(
        functools.partial(forecast_kernel, sizes, 1),
        out_shape=(pltpu.VMEM((fields + surface, rows, LANES), jnp.bfloat16), *held),
        in_specs=vmem_specs(1 + 5 + HELD),
        out_specs=tuple(vmem_specs(1 + HELD)),
        scratch_shapes=[pltpu.VMEM((fields + surface, rows, LANES), jnp.float32)],
        input_output_aliases={1 + 5 + i: 1 + i for i in range(HELD)},
        cost_estimate=cost,
        compiler_params=pltpu.CompilerParams(vmem_limit_bytes=VMEM_GRANT),
        name="forecast_late",
    )(*in_vmem(frame[0], *weights, *state))[0]


def belt_shards(
    atmosphere, ocean_state, fluxes, sea_mask, air_entry, air_middle, air_exit, sea_entry, sea_exit
):
    blocks = lax.axis_size("sp")
    fields, rows = atmosphere.shape[1:3]
    surface, flux_count = ocean_state.shape[1], fluxes.shape[1]
    hidden = air_middle.shape[3]
    kept = fields + surface + flux_count
    swap = [(0, 1), (1, 0)]
    bf16, f32 = jnp.bfloat16, jnp.float32

    got = lax.ppermute(atmosphere, "sec", swap)
    packed_shape = pltpu.VMEM((kept, (rows + 1) * LANES), bf16)
    small = pl.CostEstimate(flops=1000000, bytes_accessed=1000000, transcendentals=0)
    own = pl.pallas_call(
        pack_own_kernel,
        out_shape=packed_shape,
        in_specs=vmem_specs(4),
        out_specs=vmem_specs(1)[0],
        scratch_shapes=[pltpu.VMEM((kept, rows, LANES), f32)],
        cost_estimate=small,
        name="pack_own",
    )(atmosphere, ocean_state, fluxes, sea_mask)
    packed = pl.pallas_call(
        pack_got_kernel,
        out_shape=packed_shape,
        in_specs=vmem_specs(2),
        out_specs=vmem_specs(1)[0],
        scratch_shapes=[pltpu.VMEM((fields, rows, LANES), f32)],
        cost_estimate=small,
        name="pack_got",
    )(*in_vmem(own, got))

    weights = prepare_weights(sea_entry, sea_exit, air_entry, air_middle, air_exit)

    frame = [None] * blocks
    for index in range(blocks):
        shift = (1 - index) % blocks
        if shift == 0:
            frame[index] = packed
        else:
            pairs = [(i, (i + shift) % blocks) for i in range(blocks)]
            frame[index] = lax.ppermute(packed, "sp", pairs)

    sizes = (fields, surface, flux_count, hidden, blocks, rows)
    made = forecast(sizes, frame, weights)
    other = lax.ppermute(made, "sec", swap)
    return pl.pallas_call(
        merge_kernel,
        out_shape=(
            jax.ShapeDtypeStruct(atmosphere.shape, bf16),
            jax.ShapeDtypeStruct(ocean_state.shape, bf16),
        ),
        in_specs=vmem_specs(3),
        out_specs=tuple(vmem_specs(2)),
        cost_estimate=small,
        name="merge",
    )(*in_vmem(made, other, atmosphere))


def belt_fits(mesh, atmosphere, ocean_state, fluxes, sea_entry, sea_exit):
    sections, blocks = mesh.shape["sec"], mesh.shape["sp"]
    members = atmosphere.shape[0] // (mesh.shape["grp"] * mesh.shape["mb"])
    rows = atmosphere.shape[2] // blocks
    band = atmosphere.shape[3] // sections
    fields, surface, flux_count = atmosphere.shape[1], ocean_state.shape[1], fluxes.shape[1]
    return (
        sections == 2
        and members == 2
        and band == LANES
        and ocean_state.shape[3] == band
        and rows % SUBLANES == 0
        and rows <= LANES
        and rows >= 8
        and 2 * rows + 10 <= blocks * rows
        and blocks * rows <= 64
        and rows <= surface + flux_count
        and all(c % SUBLANES == 0 for c in (fields, surface, flux_count, sea_entry.shape[3]))
        and (surface + flux_count) % PACKED == 0
        and (fields + surface) % PACKED == 0
    )


def solution(mesh):
    placed = (
        P(("grp", "mb"), None, "sp", "sec"),
        P(("grp", "mb"), None, "sp", None),
        P(("grp", "mb"), None, "sp", None),
        P("sp", None),
        P(),
        P(),
        P(),
        P(),
        P(),
    )

    def run(atmosphere, ocean_state, fluxes, sea_mask, air_entry, air_middle, air_exit, sea_entry, sea_exit):
        fits = belt_fits(mesh, atmosphere, ocean_state, fluxes, sea_entry, sea_exit)
        return jax.shard_map(
            belt_shards if fits else shards,
            mesh=mesh,
            in_specs=placed,
            out_specs=(P(("grp", "mb"), None, "sp", "sec"), P(("grp", "mb"), None, "sp", None)),
            check_vma=False,
        )(
            atmosphere, ocean_state, fluxes, sea_mask, air_entry, air_middle, air_exit, sea_entry, sea_exit
        )

    return run
```

```python
import functools

import jax
import jax.numpy as jnp
from jax import lax
from jax.experimental import pallas as pl
from jax.experimental.pallas import tpu as pltpu
from jax.sharding import PartitionSpec as P

STEPS = 2


dilations = (1, 2, 4)


def with_halo(block, sides, width):
    for axis, dim in sides:
        count = lax.axis_size(axis)
        forward = [(i, i + 1) for i in range(count - 1)]
        forward.append((count - 1, 0))
        backward = [(target, source) for source, target in forward]
        low = lax.ppermute(
            lax.slice_in_dim(block, block.shape[dim] - width, None, axis=dim), axis, forward
        )
        high = lax.ppermute(lax.slice_in_dim(block, 0, width, axis=dim), axis, backward)
        block = jnp.concatenate([low, block, high], axis=dim)
    return block


def spread_2(value, axis, source):
    kept = jnp.where(lax.axis_index(axis) == source, value, 0).astype(value.dtype)
    return lax.psum(kept, axis)


def tap_sum(source, weight, dilation):
    out_rows = source.shape[2] - 2 * dilation
    out_cols = source.shape[3] - 2 * dilation
    pieces = []
    for tap_row in range(3):
        for tap_col in range(3):
            sliced = lax.slice_in_dim(
                source, tap_row * dilation, tap_row * dilation + out_rows, axis=2
            )
            sliced = lax.slice_in_dim(
                sliced, tap_col * dilation, tap_col * dilation + out_cols, axis=3
            )
            pieces.append(sliced)
    stacked = jnp.concatenate(pieces, axis=1)
    flat_weight = weight.reshape(-1, weight.shape[3])
    return jnp.einsum("mkrc,ko->morc", stacked, flat_weight, preferred_element_type=jnp.float32)


def gelu_round(values):
    return jax.nn.gelu(values, approximate=True).astype(jnp.bfloat16)


def keep_columns(block, first_column, limit):
    columns = lax.iota(jnp.int32, block.shape[3]) + first_column
    inside = (columns >= 0) & (columns < limit)
    return jnp.where(inside[None, None, None, :], block, jnp.zeros_like(block))


def shards(
    atmosphere, ocean_state, fluxes, sea_mask, air_entry, air_middle, air_exit, sea_entry, sea_exit
):
    sections = lax.axis_size("sec")
    position = lax.axis_index("sec")
    is_ocean = position == sections - 1
    band_cols = atmosphere.shape[3]
    ocean_cols = ocean_state.shape[3]
    field_count = atmosphere.shape[1]
    sea_weight = sea_mask.astype(jnp.float32)
    air_weights = (air_entry, air_middle, air_exit)
    sea_weights = (sea_entry, sea_exit)

    def air_layer(extended, layer_index):
        produced = tap_sum(extended, air_weights[layer_index], dilations[layer_index])
        if layer_index < 2:
            return gelu_round(produced)
        return produced

    def air_blank(extended, layer_index):
        spread = dilations[layer_index]
        out_shape = (
            extended.shape[0],
            air_weights[layer_index].shape[3],
            extended.shape[2] - 2 * spread,
            extended.shape[3] - 2 * spread,
        )
        return jnp.zeros(out_shape, jnp.bfloat16 if layer_index < 2 else jnp.float32)

    def sea_layer(extended, layer_index):
        padded = jnp.pad(extended, ((0, 0), (0, 0), (0, 0), (1, 1)))
        produced = tap_sum(padded, sea_weights[layer_index], 1)
        if layer_index < 1:
            return gelu_round(produced)
        return produced

    def sea_blank(extended, layer_index):
        out_shape = (
            extended.shape[0],
            sea_weights[layer_index].shape[3],
            extended.shape[2] - 2,
            ocean_cols,
        )
        return jnp.zeros(out_shape, jnp.bfloat16 if layer_index < 1 else jnp.float32)

    def air_extend(current, layer_index, margin):
        extended = with_halo(current, (("sp", 2), ("sec", 3)), dilations[layer_index])
        margin = dilations[layer_index]
        limit = band_cols * sections if layer_index == 0 else ocean_cols
        extended = keep_columns(extended, position * band_cols - margin, limit)
        return (extended, margin - dilations[layer_index])

    def sea_extend(current):
        return with_halo(current, (("sp", 2),), 1)

    def run_segment(air_job, sea_job):
        air_current = None
        sea_current = None
        margin = 0
        if air_job is not None:
            air_current = jnp.concatenate(air_job, axis=1)
        if sea_job is not None:
            sea_current = jnp.concatenate(sea_job, axis=1)
        for layer_index in range(3):
            air_ready = None
            sea_ready = None
            if air_current is not None:
                air_ready, margin = air_extend(air_current, layer_index, margin)
            if sea_current is not None and layer_index < 2:
                sea_ready = sea_extend(sea_current)
            if air_ready is None and sea_ready is None:
                continue

            def on_sea(ready):
                air_given, sea_given = ready
                air_made = None if air_given is None else air_blank(air_given, layer_index)
                sea_made = None if sea_given is None else sea_layer(sea_given, layer_index)
                return (air_made, sea_made)

            def on_air(ready):
                air_given, sea_given = ready
                air_made = None if air_given is None else air_layer(air_given, layer_index)
                sea_made = None if sea_given is None else sea_blank(sea_given, layer_index)
                return (air_made, sea_made)

            air_next, sea_next = lax.cond(is_ocean, on_sea, on_air, (air_ready, sea_ready))
            if air_ready is not None:
                air_current = air_next
            if sea_ready is not None:
                sea_current = sea_next
        air_result = None
        sea_result = None
        if air_job is not None:
            previous = air_job[0]
            renewed = (previous.astype(jnp.float32) + air_current[:, :field_count]).astype(
                jnp.bfloat16
            )
            air_result = (renewed, air_current[:, field_count:].astype(jnp.bfloat16))
        if sea_job is not None:
            previous = sea_job[0]
            sea_result = (
                previous.astype(jnp.float32) + sea_weight[None, None] * sea_current
            ).astype(jnp.bfloat16)
        return (air_result, sea_result)

    air_now, sea_now, flux_now = (atmosphere, ocean_state, fluxes)
    for step_index in range(STEPS):
        sea_now = run_segment(None, (sea_now, flux_now))[1]
        shared = spread_2(sea_now, "sec", sections - 1)
        start_col = jnp.minimum(position, sections - 2) * band_cols
        own_band = lax.dynamic_slice_in_dim(shared, start_col, band_cols, 3)
        own_band = jnp.where(is_ocean, jnp.zeros_like(own_band), own_band)
        sea_now = shared
        air_now, flux_band = run_segment((air_now, own_band), None)[0]
        if step_index + 1 < STEPS:
            collected = lax.all_gather(flux_band, "sec", axis=3, tiled=True)
            flux_now = collected[:, :, :, :ocean_cols]
    return (air_now, sea_now)


LANES = 128
SUBLANES = 8
PACKED = 16


def pad_to(count, unit):
    return -(-count // unit) * unit


def tree_add(terms):
    total = terms[0]
    for term in terms[1:]:
        total = total + term
    return total


def twice_gelu(v):
    inner = v * (0.7978845608028654 + (0.7978845608028654 * 0.044715) * (v * v))
    return v + v * jnp.tanh(inner)


def lane_ids(rows):
    return lax.broadcasted_iota(jnp.int32, (rows, LANES), 1)


def from_left(v, distance, fill=0.0):
    return jnp.where(lane_ids(v.shape[0]) < distance, fill, pltpu.roll(v, distance, 1))


def from_right(v, distance, fill=0.0):
    rolled = pltpu.roll(v, LANES - distance, 1)
    return jnp.where(lane_ids(v.shape[0]) >= LANES - distance, fill, rolled)


def vmem_specs(count):
    return [pl.BlockSpec(memory_space=pltpu.VMEM)] * count


def in_vmem(*values):
    return tuple(pltpu.with_memory_space_constraint(value, pltpu.VMEM) for value in values)


def pick_kernel(air_ref, out_ref, done):
    copy = pltpu.make_async_copy(air_ref.at[1 - lax.axis_index("sec")], out_ref, done)
    copy.start()
    copy.wait()


def tile(group, rows, row):
    return pl.ds((group * rows + row) * LANES, LANES)


def edge_of(bands):
    groups = bands[0].shape[0] // SUBLANES
    lanes = lane_ids(SUBLANES)
    edge = jnp.zeros((SUBLANES, LANES), jnp.float32)
    for row, band in enumerate(bands):
        for group in range(groups):
            place = group * len(bands) + row
            part = band[group * SUBLANES : (group + 1) * SUBLANES]
            edge = jnp.where(lanes == place, pltpu.roll(part, place, 1) if place else part, edge)
    return edge


def pack_own_kernel(air_ref, sea_ref, flux_ref, mask_ref, out_ref, planes):
    fields = air_ref.shape[1]
    surface = sea_ref.shape[1]
    rows = air_ref.shape[2]
    kept = fields + surface + flux_ref.shape[1]
    groups = kept // SUBLANES
    section = lax.axis_index("sec")
    planes[0:fields] = air_ref[section].astype(jnp.float32)
    planes[fields : fields + surface] = sea_ref[section].astype(jnp.float32)
    planes[fields + surface : kept] = flux_ref[section].astype(jnp.float32)
    bands = []
    for row in range(rows):
        values = planes[:, row, :]
        for group in range(groups):
            part = values[group * SUBLANES : (group + 1) * SUBLANES]
            out_ref[:, tile(group, rows, row)] = part.astype(jnp.bfloat16)
        bands.append(values[0:fields])
    out_ref[:, tile(groups, rows, 0)] = mask_ref[...].astype(jnp.bfloat16)
    out_ref[:, tile(groups, rows, 1)] = edge_of(bands).astype(jnp.bfloat16)


def pack_got_kernel(own_ref, got_ref, out_ref, planes):
    fields, rows = got_ref.shape[:2]
    groups = fields // SUBLANES
    last = own_ref.shape[1] - LANES
    first = lax.axis_index("sec") == 0
    planes[...] = got_ref[...].astype(jnp.float32)
    bands = [planes[:, row, :] for row in range(rows)]
    air = groups * rows * LANES
    out_ref[:, air:last] = own_ref[:, air:last]

    @pl.when(first)
    def _():
        out_ref[:, 0:air] = own_ref[:, 0:air]
        out_ref[:, last:] = edge_of(bands).astype(jnp.bfloat16)

    @pl.when(jnp.logical_not(first))
    def _():
        out_ref[:, last:] = own_ref[:, last:]
        for row, band in enumerate(bands):
            for group in range(groups):
                part = band[group * SUBLANES : (group + 1) * SUBLANES]
                out_ref[:, tile(group, rows, row)] = part.astype(jnp.bfloat16)


def merge_kernel(made_ref, other_ref, air_ref, air_out, sea_out):
    fields = air_ref.shape[1]
    first = lax.axis_index("sec") == 0

    @pl.when(first)
    def _():
        air_out[0] = made_ref[0:fields]
        air_out[1] = other_ref[0:fields]
        sea_out[0] = made_ref[fields:]
        sea_out[1] = other_ref[fields:]

    @pl.when(jnp.logical_not(first))
    def _():
        air_out[...] = air_ref[...]
        sea_out[0] = other_ref[fields:]
        sea_out[1] = made_ref[fields:]


def weights_kernel(se_ref, sx_ref, ae_ref, am_ref, ax_ref, se_out, sx_out, ae_out, am_out, ax_out):
    for source, target in ((se_ref, se_out), (ae_ref, ae_out)):
        taps = [
            source[a, b].astype(jnp.float32).T for a in range(3) for b in range(3)
        ]
        target[...] = jnp.concatenate(taps, axis=1).astype(jnp.bfloat16)
    for source, target, turned in ((sx_ref, sx_out, True), (am_ref, am_out, False), (ax_ref, ax_out, True)):
        width, depth = source.shape[2:] if turned else source.shape[:1:-1]
        blank = jnp.zeros((width, pad_to(depth, PACKED) - depth), jnp.float32)
        groups = []
        for b in range(3):
            pieces = []
            for a in range(3):
                tap = 0.5 * source[a, b].astype(jnp.float32)
                pieces += [tap if turned else tap.T, blank]
            groups.append(jnp.concatenate(pieces, axis=1))
        target[...] = jnp.concatenate(groups, axis=0).astype(jnp.bfloat16)


def prepare_weights(sea_entry, sea_exit, air_entry, air_middle, air_exit):
    hidden, surface, produced = air_middle.shape[3], sea_exit.shape[3], air_exit.shape[3]
    hidden_rows = pad_to(hidden, PACKED)
    return pl.pallas_call(
        weights_kernel,
        out_shape=(
            pltpu.VMEM((hidden, 9 * sea_entry.shape[2]), jnp.bfloat16),
            pltpu.VMEM((3 * surface, 3 * hidden_rows), jnp.bfloat16),
            pltpu.VMEM((hidden, 9 * air_entry.shape[2]), jnp.bfloat16),
            pltpu.VMEM((3 * hidden, 3 * hidden_rows), jnp.bfloat16),
            pltpu.VMEM((3 * produced, 3 * hidden_rows), jnp.bfloat16),
        ),
        in_specs=vmem_specs(5),
        out_specs=tuple(vmem_specs(5)),
        cost_estimate=pl.CostEstimate(flops=1000000, bytes_accessed=4000000, transcendentals=0),
        name="weights",
    )(sea_entry, jnp.swapaxes(sea_exit, 2, 3), air_entry, air_middle, jnp.swapaxes(air_exit, 2, 3))


def ordered(tasks, ring, lag, stage):
    depends = []
    late = []
    writer, readers = {}, {}
    for index, (_, reads, writes, _) in enumerate(tasks):
        needed = set()
        reads = [(name, row % ring) for name, row in reads]
        writes = [(name, row % ring) for name, row in writes]
        for cell in reads:
            if cell in writer:
                needed.add(writer[cell])
        for cell in writes:
            needed.update(readers.pop(cell, ()))
            if cell in writer:
                needed.add(writer[cell])
        for cell in reads:
            readers.setdefault(cell, set()).add(index)
        for cell in writes:
            writer[cell] = index
        needed.discard(index)
        depends.append(needed)
        late.append(tasks[index][0] == LATE_LOAD or any(late[i] for i in needed))
    chosen_stage = [i for i in range(len(tasks)) if late[i] == bool(stage)]
    placed = {i: -lag for i in range(len(tasks)) if stage and not late[i]}
    order = []
    while len(order) < len(chosen_stage):
        ready = [i for i in chosen_stage if i not in placed and all(j in placed for j in depends[i])]
        rested = [i for i in ready if all(placed[j] + lag <= len(order) for j in depends[i])]
        if rested:
            chosen = max(rested, key=lambda i: (tasks[i][0], -i))
        else:
            chosen = min(ready, key=lambda i: max((placed[j] for j in depends[i]), default=-1))
        placed[chosen] = len(order)
        order.append(chosen)
    return [tasks[i][3] for i in order]


CHUNK = 2
LAG = 20
LOAD = 0
LATE_LOAD = -1
HELD = 9
VMEM_GRANT = 24 * 1024 * 1024
PADS = {"sea_in": 2, "sea_hid": 2, "air_in": 2, "hid1": 2, "hid2": 4}


def forecast_kernel(sizes, stage, *refs):
    fields, surface, flux_count, hidden, blocks, rows = sizes
    loaded = range(1) if stage else range(1, blocks)
    block_refs = dict(zip(loaded, refs, strict=False))
    se_ref, sx_ref, ae_ref, am_ref, ax_ref = refs[len(loaded) : len(loaded) + 5]
    rest = refs[len(loaded) + 5 :]
    if stage:
        out_ref, planes = rest[HELD], rest[-1]
        rest = rest[HELD + 1 : -1]
    held = dict(zip(("sea_in", "sea_hid", "air_in", "hid1", "hid2"), rest, strict=False))
    air_now, sea_now, edge_in, mask_in = rest[5:]
    ring = blocks * rows
    kept = fields + surface + flux_count
    hidden_pad = held["sea_hid"].shape[0] - hidden

    def span(row, count):
        return pl.ds(row * LANES, count * LANES)

    def put(name, row, count, values):
        row %= ring
        pad = PADS[name]
        places = [row]
        if row < pad:
            places.append(row + ring)
        if row + count > ring - pad:
            places.append(row - ring)
        for place in places:
            low, high = max(place, -pad), min(place + count, ring + pad)
            piece = values[:, (low - place) * LANES : (high - place) * LANES]
            held[name][:, span(low + pad, high - low)] = piece

    def gather_rows(name, row, count, spread):
        start = row % ring + PADS[name]
        return jnp.concatenate(
            [held[name][:, span(start + spread * (a - 1), count)] for a in range(3)], axis=0
        )

    def put_sea_in(row, values):
        left, right = from_left(values, 1), from_right(values, 1)
        stacked = jnp.concatenate([left, values, right], axis=0).astype(jnp.bfloat16)
        put("sea_in", row, 1, stacked)

    def put_air_in(row, values, edge):
        fill = jnp.concatenate([edge, jnp.zeros((surface, LANES), jnp.float32)], axis=0)
        left, right = from_left(values, 1), from_right(values, 1, fill)
        stacked = jnp.concatenate([left, values, right], axis=0).astype(jnp.bfloat16)
        put("air_in", row, 1, stacked)

    def product(weight_ref, inputs):
        return jnp.dot(weight_ref[...], inputs, preferred_element_type=jnp.float32)

    def put_hidden(name, row, count, values):
        values = twice_gelu(values)
        if hidden_pad:
            blank = jnp.zeros((hidden_pad, values.shape[1]), jnp.float32)
            values = jnp.concatenate([values, blank], axis=0)
        put(name, row, count, values.astype(jnp.bfloat16))

    def side_sum(made, width, spread, index):
        piece = made[:, index * LANES : (index + 1) * LANES]
        left = from_left(piece[0:width], spread)
        right = from_right(piece[2 * width : 3 * width], spread)
        return piece[width : 2 * width] + left + right

    def sea_entry(row, count):
        put_hidden("sea_hid", row, count, product(se_ref, gather_rows("sea_in", row, count, 1)))

    def sea_exit(row, count):
        made = product(sx_ref, gather_rows("sea_hid", row, count, 1))
        for i in range(count):
            at = (row + i) % ring
            change = side_sum(made, surface, 1, i)
            old = sea_now[:, span(at, 1)]
            new = (old + mask_in[at : at + 1, :] * change).astype(jnp.bfloat16).astype(jnp.float32)
            sea_now[:, span(at, 1)] = new
            values = jnp.concatenate([air_now[:, span(at, 1)], new], axis=0)
            put_air_in(at, values, edge_in[:, span(at, 1)])

    def air_entry(row, count):
        put_hidden("hid1", row, count, product(ae_ref, gather_rows("air_in", row, count, 1)))

    def air_middle(row, count):
        made = product(am_ref, gather_rows("hid1", row, count, 2))
        sums = [side_sum(made, hidden, 2, i) for i in range(count)]
        put_hidden("hid2", row, count, jnp.concatenate(sums, axis=1))

    def air_exit(row, count, last):
        made = product(ax_ref, gather_rows("hid2", row, count, 4))
        for i in range(count):
            at = (row + i) % ring
            change = side_sum(made, fields + flux_count, 4, i)
            old = air_now[:, span(at, 1)]
            new = (old + change[0:fields]).astype(jnp.bfloat16).astype(jnp.float32)
            sea = sea_now[:, span(at, 1)]
            if last:
                planes[:, at - rows, :] = jnp.concatenate([new, sea], axis=0)
            else:
                air_now[:, span(at, 1)] = new
                flux = change[fields:].astype(jnp.bfloat16).astype(jnp.float32)
                put_sea_in(at, jnp.concatenate([sea, flux], axis=0))

    groups = kept // SUBLANES
    tail = groups * rows * LANES

    def load_rows(block, row, count):
        source = block_refs[block]
        for i in range(row, row + count):
            parts = [source[:, tile(group, rows, i)] for group in range(groups)]
            values = jnp.concatenate([part.astype(jnp.float32) for part in parts], axis=0)
            at = block * rows + i
            air_now[:, span(at, 1)] = values[0:fields]
            sea_now[:, span(at, 1)] = values[fields : fields + surface]
            put_sea_in(at, values[fields:kept])
            edge = source[:, tail + LANES : tail + 2 * LANES].astype(jnp.float32)
            places = [group * rows + i for group in range(fields // SUBLANES)]
            columns = [edge[:, place : place + 1] for place in places]
            columns = [jnp.broadcast_to(column, (SUBLANES, LANES)) for column in columns]
            edge_in[:, span(at, 1)] = jnp.concatenate(columns, axis=0)

    for block, source in block_refs.items():
        mask = source[:, tail : tail + LANES].astype(jnp.float32)
        mask_in[block * rows : (block + 1) * rows, :] = mask

    tasks = []

    def add(depth, first, last, body, reads, writes, spread):
        for row in range(first, last, CHUNK):
            seen = range(row - spread, row + CHUNK + spread)
            near = range(row, row + CHUNK)
            tasks.append(
                (
                    depth,
                    [(name, r) for name in reads for r in (near if name.endswith("now") else seen)],
                    [(name, r) for name in writes for r in near],
                    functools.partial(body, row, CHUNK),
                )
            )

    for block in range(blocks):
        for row in range(0, rows, CHUNK):
            near = range(block * rows + row, block * rows + row + CHUNK)
            writes = [(name, r) for name in ("sea_in", "air_now", "sea_now") for r in near]
            depth = LATE_LOAD if block == 0 else LOAD
            tasks.append((depth, [], writes, functools.partial(load_rows, block, row, CHUNK)))
    for step in range(STEPS):
        last = step == STEPS - 1
        base = 10 * step

        def reach(halo, last=last):
            return (rows - halo, 2 * rows + halo) if last else (0, ring)

        add(base + 1, *reach(8), sea_entry, ("sea_in",), ("sea_hid",), 1)
        add(base + 2, *reach(7), sea_exit, ("sea_hid", "sea_now", "air_now"), ("sea_now", "air_in"), 1)
        add(base + 3, *reach(6), air_entry, ("air_in",), ("hid1",), 1)
        add(base + 4, *reach(4), air_middle, ("hid1",), ("hid2",), 2)
        low, high = (rows, 2 * rows) if last else (rows - 10, 2 * rows + 10)
        writes = ("planes",) if last else ("air_now", "sea_in")
        body = functools.partial(air_exit, last=last)
        add(base + 5, low, high, body, ("hid2", "air_now", "sea_now"), writes, 4)
    for task in ordered(tasks, ring, LAG, stage):
        task()
    if stage:
        out_ref[...] = planes[...].astype(jnp.bfloat16)


def forecast(sizes, frame, weights):
    fields, surface, flux_count, hidden, blocks, rows = sizes
    ring = blocks * rows
    hidden_rows = pad_to(hidden, PACKED)
    held = []
    for name, depth in (
        ("sea_in", 3 * (surface + flux_count)),
        ("sea_hid", hidden_rows),
        ("air_in", 3 * (fields + surface)),
        ("hid1", hidden_rows),
        ("hid2", hidden_rows),
    ):
        held.append(pltpu.VMEM((depth, (ring + 2 * PADS[name]) * LANES), jnp.bfloat16))
    for depth in (fields, surface, fields):
        held.append(pltpu.VMEM((depth, ring * LANES), jnp.float32))
    held.append(pltpu.VMEM((ring, LANES), jnp.float32))
    cost = pl.CostEstimate(flops=2000000000, bytes_accessed=3000000, transcendentals=1000000)
    state = pl.pallas_call(
        functools.partial(forecast_kernel, sizes, 0),
        out_shape=tuple(held),
        in_specs=vmem_specs(blocks - 1 + 5),
        out_specs=tuple(vmem_specs(HELD)),
        cost_estimate=pl.CostEstimate(flops=1000, bytes_accessed=1000, transcendentals=0),
        compiler_params=pltpu.CompilerParams(vmem_limit_bytes=VMEM_GRANT),
        name="forecast_early",
    )(*in_vmem(*frame[1:], *weights))
    return pl.pallas_call(
        functools.partial(forecast_kernel, sizes, 1),
        out_shape=(pltpu.VMEM((fields + surface, rows, LANES), jnp.bfloat16), *held),
        in_specs=vmem_specs(1 + 5 + HELD),
        out_specs=tuple(vmem_specs(1 + HELD)),
        scratch_shapes=[pltpu.VMEM((fields + surface, rows, LANES), jnp.float32)],
        input_output_aliases={1 + 5 + i: 1 + i for i in range(HELD)},
        cost_estimate=cost,
        compiler_params=pltpu.CompilerParams(vmem_limit_bytes=VMEM_GRANT),
        name="forecast_late",
    )(*in_vmem(frame[0], *weights, *state))[0]


def belt_shards(
    atmosphere, ocean_state, fluxes, sea_mask, air_entry, air_middle, air_exit, sea_entry, sea_exit
):
    blocks = lax.axis_size("sp")
    fields, rows = atmosphere.shape[1:3]
    surface, flux_count = ocean_state.shape[1], fluxes.shape[1]
    hidden = air_middle.shape[3]
    kept = fields + surface + flux_count
    swap = [(0, 1), (1, 0)]
    bf16, f32 = jnp.bfloat16, jnp.float32

    sent = pl.pallas_call(
        pick_kernel,
        out_shape=pltpu.VMEM(atmosphere.shape[1:], bf16),
        in_specs=[pl.BlockSpec(memory_space=pl.ANY)],
        out_specs=vmem_specs(1)[0],
        scratch_shapes=[pltpu.SemaphoreType.DMA(())],
        name="pick",
    )(atmosphere)
    got = lax.ppermute(sent, "sec", swap)
    packed_shape = pltpu.VMEM((SUBLANES, (kept // SUBLANES * rows + 2) * LANES), bf16)
    small = pl.CostEstimate(flops=1000000, bytes_accessed=1000000, transcendentals=0)
    own = pl.pallas_call(
        pack_own_kernel,
        out_shape=packed_shape,
        in_specs=vmem_specs(4),
        out_specs=vmem_specs(1)[0],
        scratch_shapes=[pltpu.VMEM((kept, rows, LANES), f32)],
        cost_estimate=small,
        name="pack_own",
    )(atmosphere, ocean_state, fluxes, sea_mask)
    packed = pl.pallas_call(
        pack_got_kernel,
        out_shape=packed_shape,
        in_specs=vmem_specs(2),
        out_specs=vmem_specs(1)[0],
        scratch_shapes=[pltpu.VMEM((fields, rows, LANES), f32)],
        cost_estimate=small,
        name="pack_got",
    )(*in_vmem(own, got))

    weights = prepare_weights(sea_entry, sea_exit, air_entry, air_middle, air_exit)

    frame = [None] * blocks
    for index in range(blocks):
        shift = (1 - index) % blocks
        if shift == 0:
            frame[index] = packed
        else:
            pairs = [(i, (i + shift) % blocks) for i in range(blocks)]
            frame[index] = lax.ppermute(packed, "sp", pairs)

    sizes = (fields, surface, flux_count, hidden, blocks, rows)
    made = forecast(sizes, frame, weights)
    other = lax.ppermute(made, "sec", swap)
    return pl.pallas_call(
        merge_kernel,
        out_shape=(
            jax.ShapeDtypeStruct(atmosphere.shape, bf16),
            jax.ShapeDtypeStruct(ocean_state.shape, bf16),
        ),
        in_specs=vmem_specs(3),
        out_specs=tuple(vmem_specs(2)),
        cost_estimate=small,
        name="merge",
    )(*in_vmem(made, other, atmosphere))


def belt_fits(mesh, atmosphere, ocean_state, fluxes, sea_entry, sea_exit):
    sections, blocks = mesh.shape["sec"], mesh.shape["sp"]
    members = atmosphere.shape[0] // (mesh.shape["grp"] * mesh.shape["mb"])
    rows = atmosphere.shape[2] // blocks
    band = atmosphere.shape[3] // sections
    fields, surface, flux_count = atmosphere.shape[1], ocean_state.shape[1], fluxes.shape[1]
    return (
        sections == 2
        and members == 2
        and band == LANES
        and ocean_state.shape[3] == band
        and rows == SUBLANES
        and atmosphere.shape[1] <= LANES
        and 2 * rows + 10 <= blocks * rows
        and blocks * rows <= 64
        and all(c % SUBLANES == 0 for c in (fields, surface, flux_count, sea_entry.shape[3]))
        and (surface + flux_count) % PACKED == 0
        and (fields + surface) % PACKED == 0
    )


def solution(mesh):
    placed = (
        P(("grp", "mb"), None, "sp", "sec"),
        P(("grp", "mb"), None, "sp", None),
        P(("grp", "mb"), None, "sp", None),
        P("sp", None),
        P(),
        P(),
        P(),
        P(),
        P(),
    )

    def run(atmosphere, ocean_state, fluxes, sea_mask, air_entry, air_middle, air_exit, sea_entry, sea_exit):
        fits = belt_fits(mesh, atmosphere, ocean_state, fluxes, sea_entry, sea_exit)
        return jax.shard_map(
            belt_shards if fits else shards,
            mesh=mesh,
            in_specs=placed,
            out_specs=(P(("grp", "mb"), None, "sp", "sec"), P(("grp", "mb"), None, "sp", None)),
            check_vma=False,
        )(
            atmosphere, ocean_state, fluxes, sea_mask, air_entry, air_middle, air_exit, sea_entry, sea_exit
        )

    return run
```

```python
import functools

import jax
import jax.numpy as jnp
from jax import lax
from jax.experimental import pallas as pl
from jax.experimental.pallas import tpu as pltpu
from jax.sharding import PartitionSpec as P

STEPS = 2


dilations = (1, 2, 4)


def with_halo(block, sides, width):
    for axis, dim in sides:
        count = lax.axis_size(axis)
        forward = [(i, i + 1) for i in range(count - 1)]
        forward.append((count - 1, 0))
        backward = [(target, source) for source, target in forward]
        low = lax.ppermute(
            lax.slice_in_dim(block, block.shape[dim] - width, None, axis=dim), axis, forward
        )
        high = lax.ppermute(lax.slice_in_dim(block, 0, width, axis=dim), axis, backward)
        block = jnp.concatenate([low, block, high], axis=dim)
    return block


def spread_2(value, axis, source):
    kept = jnp.where(lax.axis_index(axis) == source, value, 0).astype(value.dtype)
    return lax.psum(kept, axis)


def tap_sum(source, weight, dilation):
    out_rows = source.shape[2] - 2 * dilation
    out_cols = source.shape[3] - 2 * dilation
    pieces = []
    for tap_row in range(3):
        for tap_col in range(3):
            sliced = lax.slice_in_dim(
                source, tap_row * dilation, tap_row * dilation + out_rows, axis=2
            )
            sliced = lax.slice_in_dim(
                sliced, tap_col * dilation, tap_col * dilation + out_cols, axis=3
            )
            pieces.append(sliced)
    stacked = jnp.concatenate(pieces, axis=1)
    flat_weight = weight.reshape(-1, weight.shape[3])
    return jnp.einsum("mkrc,ko->morc", stacked, flat_weight, preferred_element_type=jnp.float32)


def gelu_round(values):
    return jax.nn.gelu(values, approximate=True).astype(jnp.bfloat16)


def keep_columns(block, first_column, limit):
    columns = lax.iota(jnp.int32, block.shape[3]) + first_column
    inside = (columns >= 0) & (columns < limit)
    return jnp.where(inside[None, None, None, :], block, jnp.zeros_like(block))


def shards(
    atmosphere, ocean_state, fluxes, sea_mask, air_entry, air_middle, air_exit, sea_entry, sea_exit
):
    sections = lax.axis_size("sec")
    position = lax.axis_index("sec")
    is_ocean = position == sections - 1
    band_cols = atmosphere.shape[3]
    ocean_cols = ocean_state.shape[3]
    field_count = atmosphere.shape[1]
    sea_weight = sea_mask.astype(jnp.float32)
    air_weights = (air_entry, air_middle, air_exit)
    sea_weights = (sea_entry, sea_exit)

    def air_layer(extended, layer_index):
        produced = tap_sum(extended, air_weights[layer_index], dilations[layer_index])
        if layer_index < 2:
            return gelu_round(produced)
        return produced

    def air_blank(extended, layer_index):
        spread = dilations[layer_index]
        out_shape = (
            extended.shape[0],
            air_weights[layer_index].shape[3],
            extended.shape[2] - 2 * spread,
            extended.shape[3] - 2 * spread,
        )
        return jnp.zeros(out_shape, jnp.bfloat16 if layer_index < 2 else jnp.float32)

    def sea_layer(extended, layer_index):
        padded = jnp.pad(extended, ((0, 0), (0, 0), (0, 0), (1, 1)))
        produced = tap_sum(padded, sea_weights[layer_index], 1)
        if layer_index < 1:
            return gelu_round(produced)
        return produced

    def sea_blank(extended, layer_index):
        out_shape = (
            extended.shape[0],
            sea_weights[layer_index].shape[3],
            extended.shape[2] - 2,
            ocean_cols,
        )
        return jnp.zeros(out_shape, jnp.bfloat16 if layer_index < 1 else jnp.float32)

    def air_extend(current, layer_index, margin):
        extended = with_halo(current, (("sp", 2), ("sec", 3)), dilations[layer_index])
        margin = dilations[layer_index]
        limit = band_cols * sections if layer_index == 0 else ocean_cols
        extended = keep_columns(extended, position * band_cols - margin, limit)
        return (extended, margin - dilations[layer_index])

    def sea_extend(current):
        return with_halo(current, (("sp", 2),), 1)

    def run_segment(air_job, sea_job):
        air_current = None
        sea_current = None
        margin = 0
        if air_job is not None:
            air_current = jnp.concatenate(air_job, axis=1)
        if sea_job is not None:
            sea_current = jnp.concatenate(sea_job, axis=1)
        for layer_index in range(3):
            air_ready = None
            sea_ready = None
            if air_current is not None:
                air_ready, margin = air_extend(air_current, layer_index, margin)
            if sea_current is not None and layer_index < 2:
                sea_ready = sea_extend(sea_current)
            if air_ready is None and sea_ready is None:
                continue

            def on_sea(ready):
                air_given, sea_given = ready
                air_made = None if air_given is None else air_blank(air_given, layer_index)
                sea_made = None if sea_given is None else sea_layer(sea_given, layer_index)
                return (air_made, sea_made)

            def on_air(ready):
                air_given, sea_given = ready
                air_made = None if air_given is None else air_layer(air_given, layer_index)
                sea_made = None if sea_given is None else sea_blank(sea_given, layer_index)
                return (air_made, sea_made)

            air_next, sea_next = lax.cond(is_ocean, on_sea, on_air, (air_ready, sea_ready))
            if air_ready is not None:
                air_current = air_next
            if sea_ready is not None:
                sea_current = sea_next
        air_result = None
        sea_result = None
        if air_job is not None:
            previous = air_job[0]
            renewed = (previous.astype(jnp.float32) + air_current[:, :field_count]).astype(
                jnp.bfloat16
            )
            air_result = (renewed, air_current[:, field_count:].astype(jnp.bfloat16))
        if sea_job is not None:
            previous = sea_job[0]
            sea_result = (
                previous.astype(jnp.float32) + sea_weight[None, None] * sea_current
            ).astype(jnp.bfloat16)
        return (air_result, sea_result)

    air_now, sea_now, flux_now = (atmosphere, ocean_state, fluxes)
    for step_index in range(STEPS):
        sea_now = run_segment(None, (sea_now, flux_now))[1]
        shared = spread_2(sea_now, "sec", sections - 1)
        start_col = jnp.minimum(position, sections - 2) * band_cols
        own_band = lax.dynamic_slice_in_dim(shared, start_col, band_cols, 3)
        own_band = jnp.where(is_ocean, jnp.zeros_like(own_band), own_band)
        sea_now = shared
        air_now, flux_band = run_segment((air_now, own_band), None)[0]
        if step_index + 1 < STEPS:
            collected = lax.all_gather(flux_band, "sec", axis=3, tiled=True)
            flux_now = collected[:, :, :, :ocean_cols]
    return (air_now, sea_now)


LANES = 128
SUBLANES = 8
PACKED = 16


def pad_to(count, unit):
    return -(-count // unit) * unit


def tree_add(terms):
    total = terms[0]
    for term in terms[1:]:
        total = total + term
    return total


def twice_gelu(v):
    inner = v * (0.7978845608028654 + (0.7978845608028654 * 0.044715) * (v * v))
    return v + v * jnp.tanh(inner)


def lane_ids(rows):
    return lax.broadcasted_iota(jnp.int32, (rows, LANES), 1)


def from_left(v, distance, fill=0.0):
    return jnp.where(lane_ids(v.shape[0]) < distance, fill, pltpu.roll(v, distance, 1))


def from_right(v, distance, fill=0.0):
    rolled = pltpu.roll(v, LANES - distance, 1)
    return jnp.where(lane_ids(v.shape[0]) >= LANES - distance, fill, rolled)


def vmem_specs(count):
    return [pl.BlockSpec(memory_space=pltpu.VMEM)] * count


def in_vmem(*values):
    return tuple(pltpu.with_memory_space_constraint(value, pltpu.VMEM) for value in values)


def tile(group, rows, row):
    return pl.ds((group * rows + row) * LANES, LANES)


def edge_of(bands):
    groups = bands[0].shape[0] // SUBLANES
    lanes = lane_ids(SUBLANES)
    edge = jnp.zeros((SUBLANES, LANES), jnp.float32)
    for row, band in enumerate(bands):
        for group in range(groups):
            place = group * len(bands) + row
            part = band[group * SUBLANES : (group + 1) * SUBLANES]
            edge = jnp.where(lanes == place, pltpu.roll(part, place, 1) if place else part, edge)
    return edge


def pack_own_kernel(air_ref, sea_ref, flux_ref, mask_ref, out_ref, planes):
    fields = air_ref.shape[1]
    surface = sea_ref.shape[1]
    rows = air_ref.shape[2]
    kept = fields + surface + flux_ref.shape[1]
    groups = kept // SUBLANES
    section = lax.axis_index("sec")
    planes[0:fields] = air_ref[section].astype(jnp.float32)
    planes[fields : fields + surface] = sea_ref[section].astype(jnp.float32)
    planes[fields + surface : kept] = flux_ref[section].astype(jnp.float32)
    bands = []
    for row in range(rows):
        values = planes[:, row, :]
        for group in range(groups):
            part = values[group * SUBLANES : (group + 1) * SUBLANES]
            out_ref[:, tile(group, rows, row)] = part.astype(jnp.bfloat16)
        bands.append(values[0:fields])
    out_ref[:, tile(groups, rows, 0)] = mask_ref[...].astype(jnp.bfloat16)
    out_ref[:, tile(groups, rows, 1)] = edge_of(bands).astype(jnp.bfloat16)


def pack_got_kernel(own_ref, got_ref, out_ref, planes):
    fields, rows = got_ref.shape[1:3]
    groups = fields // SUBLANES
    last = own_ref.shape[1] - LANES
    section = lax.axis_index("sec")
    first = section == 0
    planes[...] = got_ref[section].astype(jnp.float32)
    bands = [planes[:, row, :] for row in range(rows)]
    air = groups * rows * LANES
    out_ref[:, air:last] = own_ref[:, air:last]

    @pl.when(first)
    def _():
        out_ref[:, 0:air] = own_ref[:, 0:air]
        out_ref[:, last:] = edge_of(bands).astype(jnp.bfloat16)

    @pl.when(jnp.logical_not(first))
    def _():
        out_ref[:, last:] = own_ref[:, last:]
        for row, band in enumerate(bands):
            for group in range(groups):
                part = band[group * SUBLANES : (group + 1) * SUBLANES]
                out_ref[:, tile(group, rows, row)] = part.astype(jnp.bfloat16)


def merge_kernel(made_ref, other_ref, air_ref, air_out, sea_out):
    fields = air_ref.shape[1]
    first = lax.axis_index("sec") == 0

    @pl.when(first)
    def _():
        air_out[0] = made_ref[0:fields]
        air_out[1] = other_ref[0:fields]
        sea_out[0] = made_ref[fields:]
        sea_out[1] = other_ref[fields:]

    @pl.when(jnp.logical_not(first))
    def _():
        air_out[...] = air_ref[...]
        sea_out[0] = other_ref[fields:]
        sea_out[1] = made_ref[fields:]


def weights_kernel(se_ref, sx_ref, ae_ref, am_ref, ax_ref, se_out, sx_out, ae_out, am_out, ax_out):
    for source, target in ((se_ref, se_out), (ae_ref, ae_out)):
        taps = [
            source[a, b].astype(jnp.float32).T for a in range(3) for b in range(3)
        ]
        target[...] = jnp.concatenate(taps, axis=1).astype(jnp.bfloat16)
    for source, target, turned in ((sx_ref, sx_out, True), (am_ref, am_out, False), (ax_ref, ax_out, True)):
        width, depth = source.shape[2:] if turned else source.shape[:1:-1]
        blank = jnp.zeros((width, pad_to(depth, PACKED) - depth), jnp.float32)
        groups = []
        for b in range(3):
            pieces = []
            for a in range(3):
                tap = 0.5 * source[a, b].astype(jnp.float32)
                pieces += [tap if turned else tap.T, blank]
            groups.append(jnp.concatenate(pieces, axis=1))
        target[...] = jnp.concatenate(groups, axis=0).astype(jnp.bfloat16)


def prepare_weights(sea_entry, sea_exit, air_entry, air_middle, air_exit):
    hidden, surface, produced = air_middle.shape[3], sea_exit.shape[3], air_exit.shape[3]
    hidden_rows = pad_to(hidden, PACKED)
    return pl.pallas_call(
        weights_kernel,
        out_shape=(
            pltpu.VMEM((hidden, 9 * sea_entry.shape[2]), jnp.bfloat16),
            pltpu.VMEM((3 * surface, 3 * hidden_rows), jnp.bfloat16),
            pltpu.VMEM((hidden, 9 * air_entry.shape[2]), jnp.bfloat16),
            pltpu.VMEM((3 * hidden, 3 * hidden_rows), jnp.bfloat16),
            pltpu.VMEM((3 * produced, 3 * hidden_rows), jnp.bfloat16),
        ),
        in_specs=vmem_specs(5),
        out_specs=tuple(vmem_specs(5)),
        cost_estimate=pl.CostEstimate(flops=1000000, bytes_accessed=4000000, transcendentals=0),
        name="weights",
    )(sea_entry, jnp.swapaxes(sea_exit, 2, 3), air_entry, air_middle, jnp.swapaxes(air_exit, 2, 3))


def ordered(tasks, ring, lag, stage):
    depends = []
    late = []
    writer, readers = {}, {}
    for index, (_, reads, writes, _) in enumerate(tasks):
        needed = set()
        reads = [(name, row % ring) for name, row in reads]
        writes = [(name, row % ring) for name, row in writes]
        for cell in reads:
            if cell in writer:
                needed.add(writer[cell])
        for cell in writes:
            needed.update(readers.pop(cell, ()))
            if cell in writer:
                needed.add(writer[cell])
        for cell in reads:
            readers.setdefault(cell, set()).add(index)
        for cell in writes:
            writer[cell] = index
        needed.discard(index)
        depends.append(needed)
        late.append(tasks[index][0] == LATE_LOAD or any(late[i] for i in needed))
    chosen_stage = [i for i in range(len(tasks)) if late[i] == bool(stage)]
    placed = {i: -lag for i in range(len(tasks)) if stage and not late[i]}
    order = []
    while len(order) < len(chosen_stage):
        ready = [i for i in chosen_stage if i not in placed and all(j in placed for j in depends[i])]
        rested = [i for i in ready if all(placed[j] + lag <= len(order) for j in depends[i])]
        if rested:
            chosen = max(rested, key=lambda i: (tasks[i][0], -i))
        else:
            chosen = min(ready, key=lambda i: max((placed[j] for j in depends[i]), default=-1))
        placed[chosen] = len(order)
        order.append(chosen)
    return [tasks[i][3] for i in order]


CHUNK = 2
LAG = 20
LOAD = 0
LATE_LOAD = -1
HELD = 9
VMEM_GRANT = 24 * 1024 * 1024
PADS = {"sea_in": 2, "sea_hid": 2, "air_in": 2, "hid1": 2, "hid2": 6}


def forecast_kernel(sizes, stage, *refs):
    fields, surface, flux_count, hidden, blocks, rows = sizes
    loaded = range(1) if stage else range(1, blocks)
    block_refs = dict(zip(loaded, refs, strict=False))
    se_ref, sx_ref, ae_ref, am_ref, ax_ref = refs[len(loaded) : len(loaded) + 5]
    rest = refs[len(loaded) + 5 :]
    if stage:
        out_ref, planes = rest[HELD], rest[-1]
        rest = rest[HELD + 1 : -1]
    held = dict(zip(("sea_in", "sea_hid", "air_in", "hid1", "hid2"), rest, strict=False))
    air_now, sea_now, edge_in, mask_in = rest[5:]
    ring = blocks * rows
    kept = fields + surface + flux_count
    hidden_pad = held["sea_hid"].shape[0] - hidden

    def span(row, count):
        return pl.ds(row * LANES, count * LANES)

    def put(name, row, count, values):
        row %= ring
        pad = PADS[name]
        places = [row]
        if row < pad:
            places.append(row + ring)
        if row + count > ring - pad:
            places.append(row - ring)
        for place in places:
            low, high = max(place, -pad), min(place + count, ring + pad)
            piece = values[:, (low - place) * LANES : (high - place) * LANES]
            held[name][:, span(low + pad, high - low)] = piece

    def gather_rows(name, row, count, spread):
        start = row % ring + PADS[name]
        return jnp.concatenate(
            [held[name][:, span(start + spread * (a - 1), count)] for a in range(3)], axis=0
        )

    def put_sea_in(row, values):
        left, right = from_left(values, 1), from_right(values, 1)
        stacked = jnp.concatenate([left, values, right], axis=0).astype(jnp.bfloat16)
        put("sea_in", row, 1, stacked)

    def put_air_in(row, values, edge):
        fill = jnp.concatenate([edge, jnp.zeros((surface, LANES), jnp.float32)], axis=0)
        left, right = from_left(values, 1), from_right(values, 1, fill)
        stacked = jnp.concatenate([left, values, right], axis=0).astype(jnp.bfloat16)
        put("air_in", row, 1, stacked)

    def product(weight_ref, inputs):
        return jnp.dot(weight_ref[...], inputs, preferred_element_type=jnp.float32)

    def put_hidden(name, row, count, values):
        values = twice_gelu(values)
        if hidden_pad:
            blank = jnp.zeros((hidden_pad, values.shape[1]), jnp.float32)
            values = jnp.concatenate([values, blank], axis=0)
        put(name, row, count, values.astype(jnp.bfloat16))

    def side_sum(made, width, spread, index):
        piece = made[:, index * LANES : (index + 1) * LANES]
        left = from_left(piece[0:width], spread)
        right = from_right(piece[2 * width : 3 * width], spread)
        return piece[width : 2 * width] + left + right

    def sea_entry(row, count):
        put_hidden("sea_hid", row, count, product(se_ref, gather_rows("sea_in", row, count, 1)))

    def sea_exit(row, count):
        made = product(sx_ref, gather_rows("sea_hid", row, count, 1))
        for i in range(count):
            at = (row + i) % ring
            change = side_sum(made, surface, 1, i)
            old = sea_now[:, span(at, 1)]
            new = (old + mask_in[at : at + 1, :] * change).astype(jnp.bfloat16).astype(jnp.float32)
            sea_now[:, span(at, 1)] = new
            values = jnp.concatenate([air_now[:, span(at, 1)], new], axis=0)
            put_air_in(at, values, edge_in[:, span(at, 1)])

    def air_entry(row, count):
        put_hidden("hid1", row, count, product(ae_ref, gather_rows("air_in", row, count, 1)))

    def air_middle(row, count):
        made = product(am_ref, gather_rows("hid1", row, count, 2))
        sums = [side_sum(made, hidden, 2, i) for i in range(count)]
        put_hidden("hid2", row, count, jnp.concatenate(sums, axis=1))

    def air_exit(row, count, last):
        made = product(ax_ref, gather_rows("hid2", row, count, 4))
        for i in range(count):
            at = (row + i) % ring
            change = side_sum(made, fields + flux_count, 4, i)
            old = air_now[:, span(at, 1)]
            new = (old + change[0:fields]).astype(jnp.bfloat16).astype(jnp.float32)
            sea = sea_now[:, span(at, 1)]
            if last:
                planes[:, at - rows, :] = jnp.concatenate([new, sea], axis=0)
            else:
                air_now[:, span(at, 1)] = new
                flux = change[fields:].astype(jnp.bfloat16).astype(jnp.float32)
                put_sea_in(at, jnp.concatenate([sea, flux], axis=0))

    groups = kept // SUBLANES
    tail = groups * rows * LANES

    def load_rows(block, row, count):
        source = block_refs[block]
        for i in range(row, row + count):
            parts = [source[:, tile(group, rows, i)] for group in range(groups)]
            values = jnp.concatenate([part.astype(jnp.float32) for part in parts], axis=0)
            at = block * rows + i
            air_now[:, span(at, 1)] = values[0:fields]
            sea_now[:, span(at, 1)] = values[fields : fields + surface]
            put_sea_in(at, values[fields:kept])
            edge = source[:, tail + LANES : tail + 2 * LANES].astype(jnp.float32)
            places = [group * rows + i for group in range(fields // SUBLANES)]
            columns = [edge[:, place : place + 1] for place in places]
            columns = [jnp.broadcast_to(column, (SUBLANES, LANES)) for column in columns]
            edge_in[:, span(at, 1)] = jnp.concatenate(columns, axis=0)

    for block, source in block_refs.items():
        mask = source[:, tail : tail + LANES].astype(jnp.float32)
        mask_in[block * rows : (block + 1) * rows, :] = mask

    tasks = []

    def add(depth, first, last, body, reads, writes, spread):
        for row in range(first, last, CHUNK):
            seen = range(row - spread, row + CHUNK + spread)
            near = range(row, row + CHUNK)
            tasks.append(
                (
                    depth,
                    [(name, r) for name in reads for r in (near if name.endswith("now") else seen)],
                    [(name, r) for name in writes for r in near],
                    functools.partial(body, row, CHUNK),
                )
            )

    for block in range(blocks):
        for row in range(0, rows, CHUNK):
            near = range(block * rows + row, block * rows + row + CHUNK)
            writes = [(name, r) for name in ("sea_in", "air_now", "sea_now") for r in near]
            depth = LATE_LOAD if block == 0 else LOAD
            tasks.append((depth, [], writes, functools.partial(load_rows, block, row, CHUNK)))
    for step in range(STEPS):
        last = step == STEPS - 1
        base = 10 * step

        def reach(halo, last=last):
            return (rows - halo, 2 * rows + halo) if last else (0, ring)

        add(base + 1, *reach(8), sea_entry, ("sea_in",), ("sea_hid",), 1)
        add(base + 2, *reach(7), sea_exit, ("sea_hid", "sea_now", "air_now"), ("sea_now", "air_in"), 1)
        add(base + 3, *reach(6), air_entry, ("air_in",), ("hid1",), 1)
        add(base + 4, *reach(4), air_middle, ("hid1",), ("hid2",), 2)
        low, high = (rows, 2 * rows) if last else (rows - 9, 2 * rows + 9)
        writes = ("planes",) if last else ("air_now", "sea_in")
        body = functools.partial(air_exit, last=last)
        add(base + 5, low, high, body, ("hid2", "air_now", "sea_now"), writes, 4)
    for task in ordered(tasks, ring, LAG, stage):
        task()
    if stage:
        out_ref[...] = planes[...].astype(jnp.bfloat16)


def forecast(sizes, frame, weights):
    fields, surface, flux_count, hidden, blocks, rows = sizes
    ring = blocks * rows
    hidden_rows = pad_to(hidden, PACKED)
    held = []
    for name, depth in (
        ("sea_in", 3 * (surface + flux_count)),
        ("sea_hid", hidden_rows),
        ("air_in", 3 * (fields + surface)),
        ("hid1", hidden_rows),
        ("hid2", hidden_rows),
    ):
        held.append(pltpu.VMEM((depth, (ring + 2 * PADS[name]) * LANES), jnp.bfloat16))
    for depth in (fields, surface, fields):
        held.append(pltpu.VMEM((depth, ring * LANES), jnp.float32))
    held.append(pltpu.VMEM((ring, LANES), jnp.float32))
    cost = pl.CostEstimate(flops=2000000000, bytes_accessed=3000000, transcendentals=1000000)
    state = pl.pallas_call(
        functools.partial(forecast_kernel, sizes, 0),
        out_shape=tuple(held),
        in_specs=vmem_specs(blocks - 1 + 5),
        out_specs=tuple(vmem_specs(HELD)),
        cost_estimate=pl.CostEstimate(flops=1000, bytes_accessed=1000, transcendentals=0),
        compiler_params=pltpu.CompilerParams(vmem_limit_bytes=VMEM_GRANT),
        name="forecast_early",
    )(*in_vmem(*frame[1:], *weights))
    return pl.pallas_call(
        functools.partial(forecast_kernel, sizes, 1),
        out_shape=(pltpu.VMEM((fields + surface, rows, LANES), jnp.bfloat16), *held),
        in_specs=vmem_specs(1 + 5 + HELD),
        out_specs=tuple(vmem_specs(1 + HELD)),
        scratch_shapes=[pltpu.VMEM((fields + surface, rows, LANES), jnp.float32)],
        input_output_aliases={1 + 5 + i: 1 + i for i in range(HELD)},
        cost_estimate=cost,
        compiler_params=pltpu.CompilerParams(vmem_limit_bytes=VMEM_GRANT),
        name="forecast_late",
    )(*in_vmem(frame[0], *weights, *state))[0]


def belt_shards(
    atmosphere, ocean_state, fluxes, sea_mask, air_entry, air_middle, air_exit, sea_entry, sea_exit
):
    blocks = lax.axis_size("sp")
    fields, rows = atmosphere.shape[1:3]
    surface, flux_count = ocean_state.shape[1], fluxes.shape[1]
    hidden = air_middle.shape[3]
    kept = fields + surface + flux_count
    swap = [(0, 1), (1, 0)]
    bf16, f32 = jnp.bfloat16, jnp.float32

    got = lax.ppermute(atmosphere, "sec", swap)
    packed_shape = pltpu.VMEM((SUBLANES, (kept // SUBLANES * rows + 2) * LANES), bf16)
    small = pl.CostEstimate(flops=1000000, bytes_accessed=1000000, transcendentals=0)
    own = pl.pallas_call(
        pack_own_kernel,
        out_shape=packed_shape,
        in_specs=vmem_specs(4),
        out_specs=vmem_specs(1)[0],
        scratch_shapes=[pltpu.VMEM((kept, rows, LANES), f32)],
        cost_estimate=small,
        name="pack_own",
    )(atmosphere, ocean_state, fluxes, sea_mask)
    packed = pl.pallas_call(
        pack_got_kernel,
        out_shape=packed_shape,
        in_specs=vmem_specs(2),
        out_specs=vmem_specs(1)[0],
        scratch_shapes=[pltpu.VMEM((fields, rows, LANES), f32)],
        cost_estimate=small,
        name="pack_got",
    )(*in_vmem(own, got))

    weights = prepare_weights(sea_entry, sea_exit, air_entry, air_middle, air_exit)

    frame = [None] * blocks
    for index in range(blocks):
        shift = (1 - index) % blocks
        if shift == 0:
            frame[index] = packed
        else:
            pairs = [(i, (i + shift) % blocks) for i in range(blocks)]
            frame[index] = lax.ppermute(packed, "sp", pairs)

    sizes = (fields, surface, flux_count, hidden, blocks, rows)
    made = forecast(sizes, frame, weights)
    other = lax.ppermute(made, "sec", swap)
    return pl.pallas_call(
        merge_kernel,
        out_shape=(
            jax.ShapeDtypeStruct(atmosphere.shape, bf16),
            jax.ShapeDtypeStruct(ocean_state.shape, bf16),
        ),
        in_specs=vmem_specs(3),
        out_specs=tuple(vmem_specs(2)),
        cost_estimate=small,
        name="merge",
    )(*in_vmem(made, other, atmosphere))


def belt_fits(mesh, atmosphere, ocean_state, fluxes, sea_entry, sea_exit):
    sections, blocks = mesh.shape["sec"], mesh.shape["sp"]
    members = atmosphere.shape[0] // (mesh.shape["grp"] * mesh.shape["mb"])
    rows = atmosphere.shape[2] // blocks
    band = atmosphere.shape[3] // sections
    fields, surface, flux_count = atmosphere.shape[1], ocean_state.shape[1], fluxes.shape[1]
    return (
        sections == 2
        and members == 2
        and band == LANES
        and ocean_state.shape[3] == band
        and rows == SUBLANES
        and atmosphere.shape[1] <= LANES
        and 2 * rows + 9 <= blocks * rows
        and blocks * rows <= 64
        and all(c % SUBLANES == 0 for c in (fields, surface, flux_count, sea_entry.shape[3]))
        and (surface + flux_count) % PACKED == 0
        and (fields + surface) % PACKED == 0
    )


def solution(mesh):
    placed = (
        P(("grp", "mb"), None, "sp", "sec"),
        P(("grp", "mb"), None, "sp", None),
        P(("grp", "mb"), None, "sp", None),
        P("sp", None),
        P(),
        P(),
        P(),
        P(),
        P(),
    )

    def run(atmosphere, ocean_state, fluxes, sea_mask, air_entry, air_middle, air_exit, sea_entry, sea_exit):
        fits = belt_fits(mesh, atmosphere, ocean_state, fluxes, sea_entry, sea_exit)
        return jax.shard_map(
            belt_shards if fits else shards,
            mesh=mesh,
            in_specs=placed,
            out_specs=(P(("grp", "mb"), None, "sp", "sec"), P(("grp", "mb"), None, "sp", None)),
            check_vma=False,
        )(
            atmosphere, ocean_state, fluxes, sea_mask, air_entry, air_middle, air_exit, sea_entry, sea_exit
        )

    return run
```

```python
import functools

import jax
import jax.numpy as jnp
from jax import lax
from jax.experimental import pallas as pl
from jax.experimental.pallas import tpu as pltpu
from jax.sharding import PartitionSpec as P

STEPS = 2


dilations = (1, 2, 4)


def with_halo(block, sides, width):
    for axis, dim in sides:
        count = lax.axis_size(axis)
        forward = [(i, i + 1) for i in range(count - 1)]
        forward.append((count - 1, 0))
        backward = [(target, source) for source, target in forward]
        low = lax.ppermute(
            lax.slice_in_dim(block, block.shape[dim] - width, None, axis=dim), axis, forward
        )
        high = lax.ppermute(lax.slice_in_dim(block, 0, width, axis=dim), axis, backward)
        block = jnp.concatenate([low, block, high], axis=dim)
    return block


def spread_2(value, axis, source):
    kept = jnp.where(lax.axis_index(axis) == source, value, 0).astype(value.dtype)
    return lax.psum(kept, axis)


def tap_sum(source, weight, dilation):
    out_rows = source.shape[2] - 2 * dilation
    out_cols = source.shape[3] - 2 * dilation
    pieces = []
    for tap_row in range(3):
        for tap_col in range(3):
            sliced = lax.slice_in_dim(
                source, tap_row * dilation, tap_row * dilation + out_rows, axis=2
            )
            sliced = lax.slice_in_dim(
                sliced, tap_col * dilation, tap_col * dilation + out_cols, axis=3
            )
            pieces.append(sliced)
    stacked = jnp.concatenate(pieces, axis=1)
    flat_weight = weight.reshape(-1, weight.shape[3])
    return jnp.einsum("mkrc,ko->morc", stacked, flat_weight, preferred_element_type=jnp.float32)


def gelu_round(values):
    return jax.nn.gelu(values, approximate=True).astype(jnp.bfloat16)


def keep_columns(block, first_column, limit):
    columns = lax.iota(jnp.int32, block.shape[3]) + first_column
    inside = (columns >= 0) & (columns < limit)
    return jnp.where(inside[None, None, None, :], block, jnp.zeros_like(block))


def shards(
    atmosphere, ocean_state, fluxes, sea_mask, air_entry, air_middle, air_exit, sea_entry, sea_exit
):
    sections = lax.axis_size("sec")
    position = lax.axis_index("sec")
    is_ocean = position == sections - 1
    band_cols = atmosphere.shape[3]
    ocean_cols = ocean_state.shape[3]
    field_count = atmosphere.shape[1]
    sea_weight = sea_mask.astype(jnp.float32)
    air_weights = (air_entry, air_middle, air_exit)
    sea_weights = (sea_entry, sea_exit)

    def air_layer(extended, layer_index):
        produced = tap_sum(extended, air_weights[layer_index], dilations[layer_index])
        if layer_index < 2:
            return gelu_round(produced)
        return produced

    def air_blank(extended, layer_index):
        spread = dilations[layer_index]
        out_shape = (
            extended.shape[0],
            air_weights[layer_index].shape[3],
            extended.shape[2] - 2 * spread,
            extended.shape[3] - 2 * spread,
        )
        return jnp.zeros(out_shape, jnp.bfloat16 if layer_index < 2 else jnp.float32)

    def sea_layer(extended, layer_index):
        padded = jnp.pad(extended, ((0, 0), (0, 0), (0, 0), (1, 1)))
        produced = tap_sum(padded, sea_weights[layer_index], 1)
        if layer_index < 1:
            return gelu_round(produced)
        return produced

    def sea_blank(extended, layer_index):
        out_shape = (
            extended.shape[0],
            sea_weights[layer_index].shape[3],
            extended.shape[2] - 2,
            ocean_cols,
        )
        return jnp.zeros(out_shape, jnp.bfloat16 if layer_index < 1 else jnp.float32)

    def air_extend(current, layer_index, margin):
        extended = with_halo(current, (("sp", 2), ("sec", 3)), dilations[layer_index])
        margin = dilations[layer_index]
        limit = band_cols * sections if layer_index == 0 else ocean_cols
        extended = keep_columns(extended, position * band_cols - margin, limit)
        return (extended, margin - dilations[layer_index])

    def sea_extend(current):
        return with_halo(current, (("sp", 2),), 1)

    def run_segment(air_job, sea_job):
        air_current = None
        sea_current = None
        margin = 0
        if air_job is not None:
            air_current = jnp.concatenate(air_job, axis=1)
        if sea_job is not None:
            sea_current = jnp.concatenate(sea_job, axis=1)
        for layer_index in range(3):
            air_ready = None
            sea_ready = None
            if air_current is not None:
                air_ready, margin = air_extend(air_current, layer_index, margin)
            if sea_current is not None and layer_index < 2:
                sea_ready = sea_extend(sea_current)
            if air_ready is None and sea_ready is None:
                continue

            def on_sea(ready):
                air_given, sea_given = ready
                air_made = None if air_given is None else air_blank(air_given, layer_index)
                sea_made = None if sea_given is None else sea_layer(sea_given, layer_index)
                return (air_made, sea_made)

            def on_air(ready):
                air_given, sea_given = ready
                air_made = None if air_given is None else air_layer(air_given, layer_index)
                sea_made = None if sea_given is None else sea_blank(sea_given, layer_index)
                return (air_made, sea_made)

            air_next, sea_next = lax.cond(is_ocean, on_sea, on_air, (air_ready, sea_ready))
            if air_ready is not None:
                air_current = air_next
            if sea_ready is not None:
                sea_current = sea_next
        air_result = None
        sea_result = None
        if air_job is not None:
            previous = air_job[0]
            renewed = (previous.astype(jnp.float32) + air_current[:, :field_count]).astype(
                jnp.bfloat16
            )
            air_result = (renewed, air_current[:, field_count:].astype(jnp.bfloat16))
        if sea_job is not None:
            previous = sea_job[0]
            sea_result = (
                previous.astype(jnp.float32) + sea_weight[None, None] * sea_current
            ).astype(jnp.bfloat16)
        return (air_result, sea_result)

    air_now, sea_now, flux_now = (atmosphere, ocean_state, fluxes)
    for step_index in range(STEPS):
        sea_now = run_segment(None, (sea_now, flux_now))[1]
        shared = spread_2(sea_now, "sec", sections - 1)
        start_col = jnp.minimum(position, sections - 2) * band_cols
        own_band = lax.dynamic_slice_in_dim(shared, start_col, band_cols, 3)
        own_band = jnp.where(is_ocean, jnp.zeros_like(own_band), own_band)
        sea_now = shared
        air_now, flux_band = run_segment((air_now, own_band), None)[0]
        if step_index + 1 < STEPS:
            collected = lax.all_gather(flux_band, "sec", axis=3, tiled=True)
            flux_now = collected[:, :, :, :ocean_cols]
    return (air_now, sea_now)


LANES = 128
SUBLANES = 8
PACKED = 16


def pad_to(count, unit):
    return -(-count // unit) * unit


def tree_add(terms):
    total = terms[0]
    for term in terms[1:]:
        total = total + term
    return total


def twice_gelu(v):
    inner = v * (0.7978845608028654 + (0.7978845608028654 * 0.044715) * (v * v))
    return v + v * jnp.tanh(inner)


def lane_ids(rows):
    return lax.broadcasted_iota(jnp.int32, (rows, LANES), 1)


def from_left(v, distance, fill=0.0):
    return jnp.where(lane_ids(v.shape[0]) < distance, fill, pltpu.roll(v, distance, 1))


def from_right(v, distance, fill=0.0):
    rolled = pltpu.roll(v, LANES - distance, 1)
    return jnp.where(lane_ids(v.shape[0]) >= LANES - distance, fill, rolled)


def vmem_specs(count):
    return [pl.BlockSpec(memory_space=pltpu.VMEM)] * count


def in_vmem(*values):
    return tuple(pltpu.with_memory_space_constraint(value, pltpu.VMEM) for value in values)


def tile(group, rows, row):
    return pl.ds((group * rows + row) * LANES, LANES)


def edge_of(bands):
    groups = bands[0].shape[0] // SUBLANES
    lanes = lane_ids(SUBLANES)
    edge = jnp.zeros((SUBLANES, LANES), jnp.float32)
    for row, band in enumerate(bands):
        for group in range(groups):
            place = group * len(bands) + row
            part = band[group * SUBLANES : (group + 1) * SUBLANES]
            edge = jnp.where(lanes == place, pltpu.roll(part, place, 1) if place else part, edge)
    return edge


def pack_own_kernel(air_ref, sea_ref, flux_ref, mask_ref, out_ref, planes):
    fields = air_ref.shape[1]
    surface = sea_ref.shape[1]
    rows = air_ref.shape[2]
    kept = fields + surface + flux_ref.shape[1]
    groups = kept // SUBLANES
    section = lax.axis_index("sec")
    planes[0:fields] = air_ref[section].astype(jnp.float32)
    planes[fields : fields + surface] = sea_ref[section].astype(jnp.float32)
    planes[fields + surface : kept] = flux_ref[section].astype(jnp.float32)
    bands = []
    for row in range(rows):
        values = planes[:, row, :]
        for group in range(groups):
            part = values[group * SUBLANES : (group + 1) * SUBLANES]
            out_ref[:, tile(group, rows, row)] = part.astype(jnp.bfloat16)
        bands.append(values[0:fields])
    out_ref[:, tile(groups, rows, 0)] = mask_ref[...].astype(jnp.bfloat16)
    out_ref[:, tile(groups, rows, 1)] = edge_of(bands).astype(jnp.bfloat16)


def pack_got_kernel(own_ref, got_ref, out_ref, planes):
    fields, rows = got_ref.shape[1:3]
    groups = fields // SUBLANES
    last = own_ref.shape[1] - LANES
    section = lax.axis_index("sec")
    first = section == 0
    planes[...] = got_ref[section].astype(jnp.float32)
    bands = [planes[:, row, :] for row in range(rows)]
    air = groups * rows * LANES
    out_ref[:, air:last] = own_ref[:, air:last]

    @pl.when(first)
    def _():
        out_ref[:, 0:air] = own_ref[:, 0:air]
        out_ref[:, last:] = edge_of(bands).astype(jnp.bfloat16)

    @pl.when(jnp.logical_not(first))
    def _():
        out_ref[:, last:] = own_ref[:, last:]
        for row, band in enumerate(bands):
            for group in range(groups):
                part = band[group * SUBLANES : (group + 1) * SUBLANES]
                out_ref[:, tile(group, rows, row)] = part.astype(jnp.bfloat16)


def merge_kernel(made_ref, other_ref, air_ref, air_out, sea_out):
    fields = air_ref.shape[1]
    first = lax.axis_index("sec") == 0

    @pl.when(first)
    def _():
        air_out[0] = made_ref[0:fields]
        air_out[1] = other_ref[0:fields]
        sea_out[0] = made_ref[fields:]
        sea_out[1] = other_ref[fields:]

    @pl.when(jnp.logical_not(first))
    def _():
        air_out[...] = air_ref[...]
        sea_out[0] = other_ref[fields:]
        sea_out[1] = made_ref[fields:]


def weights_kernel(se_ref, sx_ref, ae_ref, am_ref, ax_ref, se_out, sx_out, ae_out, am_out, ax_out):
    for source, target in ((se_ref, se_out), (ae_ref, ae_out)):
        taps = [
            source[a, b].astype(jnp.float32).T for a in range(3) for b in range(3)
        ]
        target[...] = jnp.concatenate(taps, axis=1).astype(jnp.bfloat16)
    surface, depth = sx_ref.shape[2:]
    blank = jnp.zeros((surface, sx_out.shape[1] - depth), jnp.float32)
    rows = []
    for a in range(3):
        for b in range(3):
            tap = 0.5 * sx_ref[a, b].astype(jnp.float32)
            rows.append(jnp.concatenate([tap, blank], axis=1) if blank.shape[1] else tap)
    sx_out[...] = jnp.concatenate(rows, axis=0).astype(jnp.bfloat16)
    for source, target, turned in ((am_ref, am_out, False), (ax_ref, ax_out, True)):
        width, depth = source.shape[2:] if turned else source.shape[:1:-1]
        blank = jnp.zeros((width, pad_to(depth, PACKED) - depth), jnp.float32)
        groups = []
        for b in range(3):
            pieces = []
            for a in range(3):
                tap = 0.5 * source[a, b].astype(jnp.float32)
                pieces += [tap if turned else tap.T, blank]
            groups.append(jnp.concatenate(pieces, axis=1))
        target[...] = jnp.concatenate(groups, axis=0).astype(jnp.bfloat16)


def prepare_weights(sea_entry, sea_exit, air_entry, air_middle, air_exit):
    hidden, surface, produced = air_middle.shape[3], sea_exit.shape[3], air_exit.shape[3]
    hidden_rows = pad_to(hidden, PACKED)
    return pl.pallas_call(
        weights_kernel,
        out_shape=(
            pltpu.VMEM((hidden, 9 * sea_entry.shape[2]), jnp.bfloat16),
            pltpu.VMEM((9 * surface, hidden_rows), jnp.bfloat16),
            pltpu.VMEM((hidden, 9 * air_entry.shape[2]), jnp.bfloat16),
            pltpu.VMEM((3 * hidden, 3 * hidden_rows), jnp.bfloat16),
            pltpu.VMEM((3 * produced, 3 * hidden_rows), jnp.bfloat16),
        ),
        in_specs=vmem_specs(5),
        out_specs=tuple(vmem_specs(5)),
        cost_estimate=pl.CostEstimate(flops=1000000, bytes_accessed=4000000, transcendentals=0),
        name="weights",
    )(sea_entry, jnp.swapaxes(sea_exit, 2, 3), air_entry, air_middle, jnp.swapaxes(air_exit, 2, 3))


def ordered(tasks, ring, lag, stage):
    depends = []
    late = []
    writer, readers = {}, {}
    for index, (_, reads, writes, _) in enumerate(tasks):
        needed = set()
        reads = [(name, row % ring) for name, row in reads]
        writes = [(name, row % ring) for name, row in writes]
        for cell in reads:
            if cell in writer:
                needed.add(writer[cell])
        for cell in writes:
            needed.update(readers.pop(cell, ()))
            if cell in writer:
                needed.add(writer[cell])
        for cell in reads:
            readers.setdefault(cell, set()).add(index)
        for cell in writes:
            writer[cell] = index
        needed.discard(index)
        depends.append(needed)
        late.append(tasks[index][0] == LATE_LOAD or any(late[i] for i in needed))
    chosen_stage = [i for i in range(len(tasks)) if late[i] == bool(stage)]
    placed = {i: -lag for i in range(len(tasks)) if stage and not late[i]}
    order = []
    while len(order) < len(chosen_stage):
        ready = [i for i in chosen_stage if i not in placed and all(j in placed for j in depends[i])]
        rested = [i for i in ready if all(placed[j] + lag <= len(order) for j in depends[i])]
        if rested:
            chosen = max(rested, key=lambda i: (tasks[i][0], -i))
        else:
            chosen = min(ready, key=lambda i: max((placed[j] for j in depends[i]), default=-1))
        placed[chosen] = len(order)
        order.append(chosen)
    return [tasks[i][3] for i in order]


CHUNK = 2
LAG = 28
LOAD = 0
LATE_LOAD = -1
HELD = 10
VMEM_GRANT = 24 * 1024 * 1024
PADS = {"sea_in": 2, "sea_hid": 2, "air_in": 2, "hid1": 2, "hid2": 6, "sea_taps": 2}


def forecast_kernel(sizes, stage, *refs):
    fields, surface, flux_count, hidden, blocks, rows = sizes
    loaded = range(1) if stage else range(1, blocks)
    block_refs = dict(zip(loaded, refs, strict=False))
    se_ref, sx_ref, ae_ref, am_ref, ax_ref = refs[len(loaded) : len(loaded) + 5]
    rest = refs[len(loaded) + 5 :]
    if stage:
        out_ref, planes = rest[HELD], rest[-1]
        rest = rest[HELD + 1 : -1]
    held = dict(zip(("sea_in", "sea_hid", "air_in", "hid1", "hid2", "sea_taps"), rest, strict=False))
    air_now, sea_now, edge_in, mask_in = rest[6:]
    ring = blocks * rows
    kept = fields + surface + flux_count
    hidden_pad = held["sea_hid"].shape[0] - hidden

    def span(row, count):
        return pl.ds(row * LANES, count * LANES)

    def put(name, row, count, values):
        row %= ring
        pad = PADS[name]
        places = [row]
        if row < pad:
            places.append(row + ring)
        if row + count > ring - pad:
            places.append(row - ring)
        for place in places:
            low, high = max(place, -pad), min(place + count, ring + pad)
            piece = values[:, (low - place) * LANES : (high - place) * LANES]
            held[name][:, span(low + pad, high - low)] = piece

    def gather_rows(name, row, count, spread):
        start = row % ring + PADS[name]
        return jnp.concatenate(
            [held[name][:, span(start + spread * (a - 1), count)] for a in range(3)], axis=0
        )

    def put_sea_in(row, values):
        left, right = from_left(values, 1), from_right(values, 1)
        stacked = jnp.concatenate([left, values, right], axis=0).astype(jnp.bfloat16)
        put("sea_in", row, 1, stacked)

    def put_air_in(row, values, edge):
        fill = jnp.concatenate([edge, jnp.zeros((surface, LANES), jnp.float32)], axis=0)
        left, right = from_left(values, 1), from_right(values, 1, fill)
        stacked = jnp.concatenate([left, values, right], axis=0).astype(jnp.bfloat16)
        put("air_in", row, 1, stacked)

    def product(weight_ref, inputs):
        return jnp.dot(weight_ref[...], inputs, preferred_element_type=jnp.float32)

    def put_hidden(name, row, count, values):
        values = twice_gelu(values)
        if hidden_pad:
            blank = jnp.zeros((hidden_pad, values.shape[1]), jnp.float32)
            values = jnp.concatenate([values, blank], axis=0)
        put(name, row, count, values.astype(jnp.bfloat16))

    def side_sum(made, width, spread, index):
        piece = made[:, index * LANES : (index + 1) * LANES]
        left = from_left(piece[0:width], spread)
        right = from_right(piece[2 * width : 3 * width], spread)
        return piece[width : 2 * width] + left + right

    def sea_entry(row, count):
        put_hidden("sea_hid", row, count, product(se_ref, gather_rows("sea_in", row, count, 1)))

    def sea_taps(row, count):
        hidden_rows = held["sea_hid"][:, span(row % ring + PADS["sea_hid"], count)]
        put("sea_taps", row, count, product(sx_ref, hidden_rows))

    def sea_exit(row, count):
        for i in range(count):
            at = (row + i) % ring
            sides = []
            for b in range(3):
                parts = []
                for a in range(3):
                    low = (3 * a + b) * surface
                    place = span(at + a - 1 + PADS["sea_taps"], 1)
                    parts.append(held["sea_taps"][low : low + surface, place])
                sides.append(parts[0] + parts[1] + parts[2])
            change = sides[1] + from_left(sides[0], 1) + from_right(sides[2], 1)
            old = sea_now[:, span(at, 1)]
            new = (old + mask_in[at : at + 1, :] * change).astype(jnp.bfloat16).astype(jnp.float32)
            sea_now[:, span(at, 1)] = new
            values = jnp.concatenate([air_now[:, span(at, 1)], new], axis=0)
            put_air_in(at, values, edge_in[:, span(at, 1)])

    def air_entry(row, count):
        put_hidden("hid1", row, count, product(ae_ref, gather_rows("air_in", row, count, 1)))

    def air_middle(row, count):
        made = product(am_ref, gather_rows("hid1", row, count, 2))
        sums = [side_sum(made, hidden, 2, i) for i in range(count)]
        put_hidden("hid2", row, count, jnp.concatenate(sums, axis=1))

    def air_exit(row, count, last):
        made = product(ax_ref, gather_rows("hid2", row, count, 4))
        for i in range(count):
            at = (row + i) % ring
            change = side_sum(made, fields + flux_count, 4, i)
            old = air_now[:, span(at, 1)]
            new = (old + change[0:fields]).astype(jnp.bfloat16).astype(jnp.float32)
            sea = sea_now[:, span(at, 1)]
            if last:
                planes[:, at - rows, :] = jnp.concatenate([new, sea], axis=0)
            else:
                air_now[:, span(at, 1)] = new
                flux = change[fields:].astype(jnp.bfloat16).astype(jnp.float32)
                put_sea_in(at, jnp.concatenate([sea, flux], axis=0))

    groups = kept // SUBLANES
    tail = groups * rows * LANES

    def load_rows(block, row, count):
        source = block_refs[block]
        for i in range(row, row + count):
            parts = [source[:, tile(group, rows, i)] for group in range(groups)]
            values = jnp.concatenate([part.astype(jnp.float32) for part in parts], axis=0)
            at = block * rows + i
            air_now[:, span(at, 1)] = values[0:fields]
            sea_now[:, span(at, 1)] = values[fields : fields + surface]
            put_sea_in(at, values[fields:kept])
            edge = source[:, tail + LANES : tail + 2 * LANES].astype(jnp.float32)
            places = [group * rows + i for group in range(fields // SUBLANES)]
            columns = [edge[:, place : place + 1] for place in places]
            columns = [jnp.broadcast_to(column, (SUBLANES, LANES)) for column in columns]
            edge_in[:, span(at, 1)] = jnp.concatenate(columns, axis=0)

    for block, source in block_refs.items():
        mask = source[:, tail : tail + LANES].astype(jnp.float32)
        mask_in[block * rows : (block + 1) * rows, :] = mask

    tasks = []

    def add(depth, first, last, body, reads, writes, spread):
        for row in range(first, last, CHUNK):
            seen = range(row - spread, row + CHUNK + spread)
            near = range(row, row + CHUNK)
            tasks.append(
                (
                    depth,
                    [(name, r) for name in reads for r in (near if name.endswith("now") else seen)],
                    [(name, r) for name in writes for r in near],
                    functools.partial(body, row, CHUNK),
                )
            )

    for block in range(blocks):
        for row in range(0, rows, CHUNK):
            near = range(block * rows + row, block * rows + row + CHUNK)
            writes = [(name, r) for name in ("sea_in", "air_now", "sea_now") for r in near]
            depth = LATE_LOAD if block == 0 else LOAD
            tasks.append((depth, [], writes, functools.partial(load_rows, block, row, CHUNK)))
    for step in range(STEPS):
        last = step == STEPS - 1
        base = 10 * step

        def reach(halo, last=last):
            return (rows - halo, 2 * rows + halo) if last else (0, ring)

        add(base + 1, *reach(8), sea_entry, ("sea_in",), ("sea_hid",), 1)
        add(base + 1, *reach(8), sea_taps, ("sea_hid",), ("sea_taps",), 0)
        add(base + 2, *reach(7), sea_exit, ("sea_taps", "sea_now", "air_now"), ("sea_now", "air_in"), 1)
        add(base + 3, *reach(6), air_entry, ("air_in",), ("hid1",), 1)
        add(base + 4, *reach(4), air_middle, ("hid1",), ("hid2",), 2)
        low, high = (rows, 2 * rows) if last else (rows - 9, 2 * rows + 9)
        writes = ("planes",) if last else ("air_now", "sea_in")
        body = functools.partial(air_exit, last=last)
        add(base + 5, low, high, body, ("hid2", "air_now", "sea_now"), writes, 4)
    for task in ordered(tasks, ring, LAG, stage):
        task()
    if stage:
        out_ref[...] = planes[...].astype(jnp.bfloat16)


def forecast(sizes, frame, weights):
    fields, surface, flux_count, hidden, blocks, rows = sizes
    ring = blocks * rows
    hidden_rows = pad_to(hidden, PACKED)
    held = []
    for name, depth in (
        ("sea_in", 3 * (surface + flux_count)),
        ("sea_hid", hidden_rows),
        ("air_in", 3 * (fields + surface)),
        ("hid1", hidden_rows),
        ("hid2", hidden_rows),
    ):
        held.append(pltpu.VMEM((depth, (ring + 2 * PADS[name]) * LANES), jnp.bfloat16))
    wide = (ring + 2 * PADS["sea_taps"]) * LANES
    held.append(pltpu.VMEM((9 * surface, wide), jnp.float32))
    for depth in (fields, surface, fields):
        held.append(pltpu.VMEM((depth, ring * LANES), jnp.float32))
    held.append(pltpu.VMEM((ring, LANES), jnp.float32))
    cost = pl.CostEstimate(flops=2000000000, bytes_accessed=3000000, transcendentals=1000000)
    state = pl.pallas_call(
        functools.partial(forecast_kernel, sizes, 0),
        out_shape=tuple(held),
        in_specs=vmem_specs(blocks - 1 + 5),
        out_specs=tuple(vmem_specs(HELD)),
        cost_estimate=pl.CostEstimate(flops=1000, bytes_accessed=1000, transcendentals=0),
        compiler_params=pltpu.CompilerParams(vmem_limit_bytes=VMEM_GRANT),
        name="forecast_early",
    )(*in_vmem(*frame[1:], *weights))
    return pl.pallas_call(
        functools.partial(forecast_kernel, sizes, 1),
        out_shape=(pltpu.VMEM((fields + surface, rows, LANES), jnp.bfloat16), *held),
        in_specs=vmem_specs(1 + 5 + HELD),
        out_specs=tuple(vmem_specs(1 + HELD)),
        scratch_shapes=[pltpu.VMEM((fields + surface, rows, LANES), jnp.float32)],
        input_output_aliases={1 + 5 + i: 1 + i for i in range(HELD)},
        cost_estimate=cost,
        compiler_params=pltpu.CompilerParams(vmem_limit_bytes=VMEM_GRANT),
        name="forecast_late",
    )(*in_vmem(frame[0], *weights, *state))[0]


def belt_shards(
    atmosphere, ocean_state, fluxes, sea_mask, air_entry, air_middle, air_exit, sea_entry, sea_exit
):
    blocks = lax.axis_size("sp")
    fields, rows = atmosphere.shape[1:3]
    surface, flux_count = ocean_state.shape[1], fluxes.shape[1]
    hidden = air_middle.shape[3]
    kept = fields + surface + flux_count
    swap = [(0, 1), (1, 0)]
    bf16, f32 = jnp.bfloat16, jnp.float32

    got = lax.ppermute(atmosphere, "sec", swap)
    packed_shape = pltpu.VMEM((SUBLANES, (kept // SUBLANES * rows + 2) * LANES), bf16)
    small = pl.CostEstimate(flops=1000000, bytes_accessed=1000000, transcendentals=0)
    own = pl.pallas_call(
        pack_own_kernel,
        out_shape=packed_shape,
        in_specs=vmem_specs(4),
        out_specs=vmem_specs(1)[0],
        scratch_shapes=[pltpu.VMEM((kept, rows, LANES), f32)],
        cost_estimate=small,
        name="pack_own",
    )(atmosphere, ocean_state, fluxes, sea_mask)
    packed = pl.pallas_call(
        pack_got_kernel,
        out_shape=packed_shape,
        in_specs=vmem_specs(2),
        out_specs=vmem_specs(1)[0],
        scratch_shapes=[pltpu.VMEM((fields, rows, LANES), f32)],
        cost_estimate=small,
        name="pack_got",
    )(*in_vmem(own, got))

    weights = prepare_weights(sea_entry, sea_exit, air_entry, air_middle, air_exit)

    frame = [None] * blocks
    for index in range(blocks):
        shift = (1 - index) % blocks
        if shift == 0:
            frame[index] = packed
        else:
            pairs = [(i, (i + shift) % blocks) for i in range(blocks)]
            frame[index] = lax.ppermute(packed, "sp", pairs)

    sizes = (fields, surface, flux_count, hidden, blocks, rows)
    made = forecast(sizes, frame, weights)
    other = lax.ppermute(made, "sec", swap)
    return pl.pallas_call(
        merge_kernel,
        out_shape=(
            jax.ShapeDtypeStruct(atmosphere.shape, bf16),
            jax.ShapeDtypeStruct(ocean_state.shape, bf16),
        ),
        in_specs=vmem_specs(3),
        out_specs=tuple(vmem_specs(2)),
        cost_estimate=small,
        name="merge",
    )(*in_vmem(made, other, atmosphere))


def belt_fits(mesh, atmosphere, ocean_state, fluxes, sea_entry, sea_exit):
    sections, blocks = mesh.shape["sec"], mesh.shape["sp"]
    members = atmosphere.shape[0] // (mesh.shape["grp"] * mesh.shape["mb"])
    rows = atmosphere.shape[2] // blocks
    band = atmosphere.shape[3] // sections
    fields, surface, flux_count = atmosphere.shape[1], ocean_state.shape[1], fluxes.shape[1]
    return (
        sections == 2
        and members == 2
        and band == LANES
        and ocean_state.shape[3] == band
        and rows == SUBLANES
        and atmosphere.shape[1] <= LANES
        and 2 * rows + 9 <= blocks * rows
        and blocks * rows <= 64
        and all(c % SUBLANES == 0 for c in (fields, surface, flux_count, sea_entry.shape[3]))
        and (surface + flux_count) % PACKED == 0
        and (fields + surface) % PACKED == 0
    )


def solution(mesh):
    placed = (
        P(("grp", "mb"), None, "sp", "sec"),
        P(("grp", "mb"), None, "sp", None),
        P(("grp", "mb"), None, "sp", None),
        P("sp", None),
        P(),
        P(),
        P(),
        P(),
        P(),
    )

    def run(atmosphere, ocean_state, fluxes, sea_mask, air_entry, air_middle, air_exit, sea_entry, sea_exit):
        fits = belt_fits(mesh, atmosphere, ocean_state, fluxes, sea_entry, sea_exit)
        return jax.shard_map(
            belt_shards if fits else shards,
            mesh=mesh,
            in_specs=placed,
            out_specs=(P(("grp", "mb"), None, "sp", "sec"), P(("grp", "mb"), None, "sp", None)),
            check_vma=False,
        )(
            atmosphere, ocean_state, fluxes, sea_mask, air_entry, air_middle, air_exit, sea_entry, sea_exit
        )

    return run
```

```python
import functools

import jax
import jax.numpy as jnp
from jax import lax
from jax.experimental import pallas as pl
from jax.experimental.pallas import tpu as pltpu
from jax.sharding import PartitionSpec as P

STEPS = 2


dilations = (1, 2, 4)


def with_halo(block, sides, width):
    for axis, dim in sides:
        count = lax.axis_size(axis)
        forward = [(i, i + 1) for i in range(count - 1)]
        forward.append((count - 1, 0))
        backward = [(target, source) for source, target in forward]
        low = lax.ppermute(
            lax.slice_in_dim(block, block.shape[dim] - width, None, axis=dim), axis, forward
        )
        high = lax.ppermute(lax.slice_in_dim(block, 0, width, axis=dim), axis, backward)
        block = jnp.concatenate([low, block, high], axis=dim)
    return block


def spread_2(value, axis, source):
    kept = jnp.where(lax.axis_index(axis) == source, value, 0).astype(value.dtype)
    return lax.psum(kept, axis)


def tap_sum(source, weight, dilation):
    out_rows = source.shape[2] - 2 * dilation
    out_cols = source.shape[3] - 2 * dilation
    pieces = []
    for tap_row in range(3):
        for tap_col in range(3):
            sliced = lax.slice_in_dim(
                source, tap_row * dilation, tap_row * dilation + out_rows, axis=2
            )
            sliced = lax.slice_in_dim(
                sliced, tap_col * dilation, tap_col * dilation + out_cols, axis=3
            )
            pieces.append(sliced)
    stacked = jnp.concatenate(pieces, axis=1)
    flat_weight = weight.reshape(-1, weight.shape[3])
    return jnp.einsum("mkrc,ko->morc", stacked, flat_weight, preferred_element_type=jnp.float32)


def gelu_round(values):
    return jax.nn.gelu(values, approximate=True).astype(jnp.bfloat16)


def keep_columns(block, first_column, limit):
    columns = lax.iota(jnp.int32, block.shape[3]) + first_column
    inside = (columns >= 0) & (columns < limit)
    return jnp.where(inside[None, None, None, :], block, jnp.zeros_like(block))


def shards(
    atmosphere, ocean_state, fluxes, sea_mask, air_entry, air_middle, air_exit, sea_entry, sea_exit
):
    sections = lax.axis_size("sec")
    position = lax.axis_index("sec")
    is_ocean = position == sections - 1
    band_cols = atmosphere.shape[3]
    ocean_cols = ocean_state.shape[3]
    field_count = atmosphere.shape[1]
    sea_weight = sea_mask.astype(jnp.float32)
    air_weights = (air_entry, air_middle, air_exit)
    sea_weights = (sea_entry, sea_exit)

    def air_layer(extended, layer_index):
        produced = tap_sum(extended, air_weights[layer_index], dilations[layer_index])
        if layer_index < 2:
            return gelu_round(produced)
        return produced

    def air_blank(extended, layer_index):
        spread = dilations[layer_index]
        out_shape = (
            extended.shape[0],
            air_weights[layer_index].shape[3],
            extended.shape[2] - 2 * spread,
            extended.shape[3] - 2 * spread,
        )
        return jnp.zeros(out_shape, jnp.bfloat16 if layer_index < 2 else jnp.float32)

    def sea_layer(extended, layer_index):
        padded = jnp.pad(extended, ((0, 0), (0, 0), (0, 0), (1, 1)))
        produced = tap_sum(padded, sea_weights[layer_index], 1)
        if layer_index < 1:
            return gelu_round(produced)
        return produced

    def sea_blank(extended, layer_index):
        out_shape = (
            extended.shape[0],
            sea_weights[layer_index].shape[3],
            extended.shape[2] - 2,
            ocean_cols,
        )
        return jnp.zeros(out_shape, jnp.bfloat16 if layer_index < 1 else jnp.float32)

    def air_extend(current, layer_index, margin):
        extended = with_halo(current, (("sp", 2), ("sec", 3)), dilations[layer_index])
        margin = dilations[layer_index]
        limit = band_cols * sections if layer_index == 0 else ocean_cols
        extended = keep_columns(extended, position * band_cols - margin, limit)
        return (extended, margin - dilations[layer_index])

    def sea_extend(current):
        return with_halo(current, (("sp", 2),), 1)

    def run_segment(air_job, sea_job):
        air_current = None
        sea_current = None
        margin = 0
        if air_job is not None:
            air_current = jnp.concatenate(air_job, axis=1)
        if sea_job is not None:
            sea_current = jnp.concatenate(sea_job, axis=1)
        for layer_index in range(3):
            air_ready = None
            sea_ready = None
            if air_current is not None:
                air_ready, margin = air_extend(air_current, layer_index, margin)
            if sea_current is not None and layer_index < 2:
                sea_ready = sea_extend(sea_current)
            if air_ready is None and sea_ready is None:
                continue

            def on_sea(ready):
                air_given, sea_given = ready
                air_made = None if air_given is None else air_blank(air_given, layer_index)
                sea_made = None if sea_given is None else sea_layer(sea_given, layer_index)
                return (air_made, sea_made)

            def on_air(ready):
                air_given, sea_given = ready
                air_made = None if air_given is None else air_layer(air_given, layer_index)
                sea_made = None if sea_given is None else sea_blank(sea_given, layer_index)
                return (air_made, sea_made)

            air_next, sea_next = lax.cond(is_ocean, on_sea, on_air, (air_ready, sea_ready))
            if air_ready is not None:
                air_current = air_next
            if sea_ready is not None:
                sea_current = sea_next
        air_result = None
        sea_result = None
        if air_job is not None:
            previous = air_job[0]
            renewed = (previous.astype(jnp.float32) + air_current[:, :field_count]).astype(
                jnp.bfloat16
            )
            air_result = (renewed, air_current[:, field_count:].astype(jnp.bfloat16))
        if sea_job is not None:
            previous = sea_job[0]
            sea_result = (
                previous.astype(jnp.float32) + sea_weight[None, None] * sea_current
            ).astype(jnp.bfloat16)
        return (air_result, sea_result)

    air_now, sea_now, flux_now = (atmosphere, ocean_state, fluxes)
    for step_index in range(STEPS):
        sea_now = run_segment(None, (sea_now, flux_now))[1]
        shared = spread_2(sea_now, "sec", sections - 1)
        start_col = jnp.minimum(position, sections - 2) * band_cols
        own_band = lax.dynamic_slice_in_dim(shared, start_col, band_cols, 3)
        own_band = jnp.where(is_ocean, jnp.zeros_like(own_band), own_band)
        sea_now = shared
        air_now, flux_band = run_segment((air_now, own_band), None)[0]
        if step_index + 1 < STEPS:
            collected = lax.all_gather(flux_band, "sec", axis=3, tiled=True)
            flux_now = collected[:, :, :, :ocean_cols]
    return (air_now, sea_now)


LANES = 128
SUBLANES = 8
PACKED = 16


def pad_to(count, unit):
    return -(-count // unit) * unit


def tree_add(terms):
    total = terms[0]
    for term in terms[1:]:
        total = total + term
    return total


def twice_gelu(v):
    inner = v * (0.7978845608028654 + (0.7978845608028654 * 0.044715) * (v * v))
    return v + v * jnp.tanh(inner)


def lane_ids(rows):
    return lax.broadcasted_iota(jnp.int32, (rows, LANES), 1)


def from_left(v, distance, fill=0.0):
    return jnp.where(lane_ids(v.shape[0]) < distance, fill, pltpu.roll(v, distance, 1))


def from_right(v, distance, fill=0.0):
    rolled = pltpu.roll(v, LANES - distance, 1)
    return jnp.where(lane_ids(v.shape[0]) >= LANES - distance, fill, rolled)


def vmem_specs(count):
    return [pl.BlockSpec(memory_space=pltpu.VMEM)] * count


def in_vmem(*values):
    return tuple(pltpu.with_memory_space_constraint(value, pltpu.VMEM) for value in values)


def tile(group, rows, row):
    return pl.ds((group * rows + row) * LANES, LANES)


def edge_of(bands):
    groups = bands[0].shape[0] // SUBLANES
    lanes = lane_ids(SUBLANES)
    edge = jnp.zeros((SUBLANES, LANES), jnp.float32)
    for row, band in enumerate(bands):
        for group in range(groups):
            place = group * len(bands) + row
            part = band[group * SUBLANES : (group + 1) * SUBLANES]
            edge = jnp.where(lanes == place, pltpu.roll(part, place, 1) if place else part, edge)
    return edge


def pack_own_kernel(air_ref, sea_ref, flux_ref, mask_ref, out_ref, planes):
    fields = air_ref.shape[1]
    surface = sea_ref.shape[1]
    rows = air_ref.shape[2]
    kept = fields + surface + flux_ref.shape[1]
    groups = kept // SUBLANES
    section = lax.axis_index("sec")
    planes[0:fields] = air_ref[section].astype(jnp.float32)
    planes[fields : fields + surface] = sea_ref[section].astype(jnp.float32)
    planes[fields + surface : kept] = flux_ref[section].astype(jnp.float32)
    bands = []
    for row in range(rows):
        values = planes[:, row, :]
        for group in range(groups):
            part = values[group * SUBLANES : (group + 1) * SUBLANES]
            out_ref[:, tile(group, rows, row)] = part.astype(jnp.bfloat16)
        bands.append(values[0:fields])
    out_ref[:, tile(groups, rows, 0)] = mask_ref[...].astype(jnp.bfloat16)
    out_ref[:, tile(groups, rows, 1)] = edge_of(bands).astype(jnp.bfloat16)


def pack_got_kernel(own_ref, got_ref, out_ref, planes):
    fields, rows = got_ref.shape[1:3]
    groups = fields // SUBLANES
    last = own_ref.shape[1] - LANES
    section = lax.axis_index("sec")
    first = section == 0
    planes[...] = got_ref[section].astype(jnp.float32)
    bands = [planes[:, row, :] for row in range(rows)]
    air = groups * rows * LANES
    out_ref[:, air:last] = own_ref[:, air:last]

    @pl.when(first)
    def _():
        out_ref[:, 0:air] = own_ref[:, 0:air]
        out_ref[:, last:] = edge_of(bands).astype(jnp.bfloat16)

    @pl.when(jnp.logical_not(first))
    def _():
        out_ref[:, last:] = own_ref[:, last:]
        for row, band in enumerate(bands):
            for group in range(groups):
                part = band[group * SUBLANES : (group + 1) * SUBLANES]
                out_ref[:, tile(group, rows, row)] = part.astype(jnp.bfloat16)


def merge_kernel(made_ref, other_ref, air_ref, air_out, sea_out):
    fields = air_ref.shape[1]
    first = lax.axis_index("sec") == 0

    @pl.when(first)
    def _():
        air_out[0] = made_ref[0:fields]
        air_out[1] = other_ref[0:fields]
        sea_out[0] = made_ref[fields:]
        sea_out[1] = other_ref[fields:]

    @pl.when(jnp.logical_not(first))
    def _():
        air_out[...] = air_ref[...]
        sea_out[0] = other_ref[fields:]
        sea_out[1] = made_ref[fields:]


def weights_kernel(se_ref, sx_ref, ae_ref, am_ref, ax_ref, se_out, sx_out, ae_out, am_out, ax_out):
    for source, target in ((se_ref, se_out), (ae_ref, ae_out)):
        taps = [
            source[a, b].astype(jnp.float32).T for a in range(3) for b in range(3)
        ]
        target[...] = jnp.concatenate(taps, axis=1).astype(jnp.bfloat16)
    for source, target, turned in ((sx_ref, sx_out, True), (am_ref, am_out, False), (ax_ref, ax_out, True)):
        width, depth = source.shape[2:] if turned else source.shape[:1:-1]
        blank = jnp.zeros((width, pad_to(depth, PACKED) - depth), jnp.float32)
        groups = []
        for b in range(3):
            pieces = []
            for a in range(3):
                tap = 0.5 * source[a, b].astype(jnp.float32)
                pieces += [tap if turned else tap.T, blank]
            groups.append(jnp.concatenate(pieces, axis=1))
        target[...] = jnp.concatenate(groups, axis=0).astype(jnp.bfloat16)


def prepare_weights(sea_entry, sea_exit, air_entry, air_middle, air_exit):
    hidden, surface, produced = air_middle.shape[3], sea_exit.shape[3], air_exit.shape[3]
    hidden_rows = pad_to(hidden, PACKED)
    return pl.pallas_call(
        weights_kernel,
        out_shape=(
            pltpu.VMEM((hidden, 9 * sea_entry.shape[2]), jnp.bfloat16),
            pltpu.VMEM((3 * surface, 3 * hidden_rows), jnp.bfloat16),
            pltpu.VMEM((hidden, 9 * air_entry.shape[2]), jnp.bfloat16),
            pltpu.VMEM((3 * hidden, 3 * hidden_rows), jnp.bfloat16),
            pltpu.VMEM((3 * produced, 3 * hidden_rows), jnp.bfloat16),
        ),
        in_specs=vmem_specs(5),
        out_specs=tuple(vmem_specs(5)),
        cost_estimate=pl.CostEstimate(flops=1000000, bytes_accessed=4000000, transcendentals=0),
        name="weights",
    )(sea_entry, jnp.swapaxes(sea_exit, 2, 3), air_entry, air_middle, jnp.swapaxes(air_exit, 2, 3))


def ordered(tasks, ring, lag, stage):
    depends = []
    late = []
    writer, readers = {}, {}
    for index, (_, reads, writes, _) in enumerate(tasks):
        needed = set()
        reads = [(name, row % ring) for name, row in reads]
        writes = [(name, row % ring) for name, row in writes]
        for cell in reads:
            if cell in writer:
                needed.add(writer[cell])
        for cell in writes:
            needed.update(readers.pop(cell, ()))
            if cell in writer:
                needed.add(writer[cell])
        for cell in reads:
            readers.setdefault(cell, set()).add(index)
        for cell in writes:
            writer[cell] = index
        needed.discard(index)
        depends.append(needed)
        late.append(tasks[index][0] == LATE_LOAD or any(late[i] for i in needed))
    chosen_stage = [i for i in range(len(tasks)) if late[i] == bool(stage)]
    placed = {i: -lag for i in range(len(tasks)) if stage and not late[i]}
    order = []
    while len(order) < len(chosen_stage):
        ready = [i for i in chosen_stage if i not in placed and all(j in placed for j in depends[i])]
        rested = [i for i in ready if all(placed[j] + lag <= len(order) for j in depends[i])]
        if rested:
            chosen = max(rested, key=lambda i: (tasks[i][0], -i))
        else:
            chosen = min(ready, key=lambda i: max((placed[j] for j in depends[i]), default=-1))
        placed[chosen] = len(order)
        order.append(chosen)
    return [tasks[i][3] for i in order]


CHUNK = 2
LAG = 14
LOAD = 0
LATE_LOAD = -1
HELD = 9
VMEM_GRANT = 24 * 1024 * 1024
PADS = {"sea_in": 2, "sea_hid": 2, "air_in": 2, "hid1": 2, "hid2": 6}


def forecast_kernel(sizes, stage, *refs):
    fields, surface, flux_count, hidden, blocks, rows = sizes
    loaded = range(1) if stage else range(1, blocks)
    block_refs = dict(zip(loaded, refs, strict=False))
    se_ref, sx_ref, ae_ref, am_ref, ax_ref = refs[len(loaded) : len(loaded) + 5]
    rest = refs[len(loaded) + 5 :]
    if stage:
        out_ref, planes = rest[HELD], rest[-1]
        rest = rest[HELD + 1 : -1]
    held = dict(zip(("sea_in", "sea_hid", "air_in", "hid1", "hid2"), rest, strict=False))
    air_now, sea_now, edge_in, mask_in = rest[5:]
    ring = blocks * rows
    kept = fields + surface + flux_count
    hidden_pad = held["sea_hid"].shape[0] - hidden

    def span(row, count):
        return pl.ds(row * LANES, count * LANES)

    def put(name, row, count, values):
        row %= ring
        pad = PADS[name]
        places = [row]
        if row < pad:
            places.append(row + ring)
        if row + count > ring - pad:
            places.append(row - ring)
        for place in places:
            low, high = max(place, -pad), min(place + count, ring + pad)
            piece = values[:, (low - place) * LANES : (high - place) * LANES]
            held[name][:, span(low + pad, high - low)] = piece

    def gather_rows(name, row, count, spread):
        start = row % ring + PADS[name]
        return jnp.concatenate(
            [held[name][:, span(start + spread * (a - 1), count)] for a in range(3)], axis=0
        )

    def put_sea_in(row, values):
        left, right = from_left(values, 1), from_right(values, 1)
        stacked = jnp.concatenate([left, values, right], axis=0).astype(jnp.bfloat16)
        put("sea_in", row, 1, stacked)

    def put_air_in(row, values, edge):
        fill = jnp.concatenate([edge, jnp.zeros((surface, LANES), jnp.float32)], axis=0)
        left, right = from_left(values, 1), from_right(values, 1, fill)
        stacked = jnp.concatenate([left, values, right], axis=0).astype(jnp.bfloat16)
        put("air_in", row, 1, stacked)

    def product(weight_ref, inputs):
        return jnp.dot(weight_ref[...], inputs, preferred_element_type=jnp.float32)

    def put_hidden(name, row, count, values):
        values = twice_gelu(values)
        if hidden_pad:
            blank = jnp.zeros((hidden_pad, values.shape[1]), jnp.float32)
            values = jnp.concatenate([values, blank], axis=0)
        put(name, row, count, values.astype(jnp.bfloat16))

    def side_sum(made, width, spread, index):
        piece = made[:, index * LANES : (index + 1) * LANES]
        left = from_left(piece[0:width], spread)
        right = from_right(piece[2 * width : 3 * width], spread)
        return piece[width : 2 * width] + left + right

    def sea_entry(row, count):
        put_hidden("sea_hid", row, count, product(se_ref, gather_rows("sea_in", row, count, 1)))

    def sea_exit(row, count):
        made = product(sx_ref, gather_rows("sea_hid", row, count, 1))
        for i in range(count):
            at = (row + i) % ring
            change = side_sum(made, surface, 1, i)
            old = sea_now[:, span(at, 1)]
            new = (old + mask_in[at : at + 1, :] * change).astype(jnp.bfloat16).astype(jnp.float32)
            sea_now[:, span(at, 1)] = new
            values = jnp.concatenate([air_now[:, span(at, 1)], new], axis=0)
            put_air_in(at, values, edge_in[:, span(at, 1)])

    def air_entry(row, count):
        put_hidden("hid1", row, count, product(ae_ref, gather_rows("air_in", row, count, 1)))

    def air_middle(row, count):
        made = product(am_ref, gather_rows("hid1", row, count, 2))
        sums = [side_sum(made, hidden, 2, i) for i in range(count)]
        put_hidden("hid2", row, count, jnp.concatenate(sums, axis=1))

    def air_exit(row, count, last):
        made = product(ax_ref, gather_rows("hid2", row, count, 4))
        for i in range(count):
            at = (row + i) % ring
            change = side_sum(made, fields + flux_count, 4, i)
            old = air_now[:, span(at, 1)]
            new = (old + change[0:fields]).astype(jnp.bfloat16).astype(jnp.float32)
            sea = sea_now[:, span(at, 1)]
            if last:
                planes[:, at - rows, :] = jnp.concatenate([new, sea], axis=0)
            else:
                air_now[:, span(at, 1)] = new
                flux = change[fields:].astype(jnp.bfloat16).astype(jnp.float32)
                put_sea_in(at, jnp.concatenate([sea, flux], axis=0))

    groups = kept // SUBLANES
    tail = groups * rows * LANES

    def load_rows(block, row, count):
        source = block_refs[block]
        for i in range(row, row + count):
            parts = [source[:, tile(group, rows, i)] for group in range(groups)]
            values = jnp.concatenate([part.astype(jnp.float32) for part in parts], axis=0)
            at = block * rows + i
            air_now[:, span(at, 1)] = values[0:fields]
            sea_now[:, span(at, 1)] = values[fields : fields + surface]
            put_sea_in(at, values[fields:kept])
            edge = source[:, tail + LANES : tail + 2 * LANES].astype(jnp.float32)
            places = [group * rows + i for group in range(fields // SUBLANES)]
            columns = [edge[:, place : place + 1] for place in places]
            columns = [jnp.broadcast_to(column, (SUBLANES, LANES)) for column in columns]
            edge_in[:, span(at, 1)] = jnp.concatenate(columns, axis=0)

    for block, source in block_refs.items():
        mask = source[:, tail : tail + LANES].astype(jnp.float32)
        mask_in[block * rows : (block + 1) * rows, :] = mask

    tasks = []

    def add(depth, first, last, body, reads, writes, spread):
        for row in range(first, last, CHUNK):
            seen = range(row - spread, row + CHUNK + spread)
            near = range(row, row + CHUNK)
            tasks.append(
                (
                    depth,
                    [(name, r) for name in reads for r in (near if name.endswith("now") else seen)],
                    [(name, r) for name in writes for r in near],
                    functools.partial(body, row, CHUNK),
                )
            )

    for block in range(blocks):
        for row in range(0, rows, CHUNK):
            near = range(block * rows + row, block * rows + row + CHUNK)
            writes = [(name, r) for name in ("sea_in", "air_now", "sea_now") for r in near]
            depth = LATE_LOAD if block == 0 else LOAD
            tasks.append((depth, [], writes, functools.partial(load_rows, block, row, CHUNK)))
    for step in range(STEPS):
        last = step == STEPS - 1
        base = 10 * step

        def reach(halo, last=last):
            return (rows - halo, 2 * rows + halo) if last else (0, ring)

        add(base + 1, *reach(8), sea_entry, ("sea_in",), ("sea_hid",), 1)
        add(base + 2, *reach(7), sea_exit, ("sea_hid", "sea_now", "air_now"), ("sea_now", "air_in"), 1)
        add(base + 3, *reach(6), air_entry, ("air_in",), ("hid1",), 1)
        add(base + 4, *reach(4), air_middle, ("hid1",), ("hid2",), 2)
        low, high = (rows, 2 * rows) if last else (rows - 9, 2 * rows + 9)
        writes = ("planes",) if last else ("air_now", "sea_in")
        body = functools.partial(air_exit, last=last)
        add(base + 5, low, high, body, ("hid2", "air_now", "sea_now"), writes, 4)
    for task in ordered(tasks, ring, LAG, stage):
        task()
    if stage:
        out_ref[...] = planes[...].astype(jnp.bfloat16)


def forecast(sizes, frame, weights):
    fields, surface, flux_count, hidden, blocks, rows = sizes
    ring = blocks * rows
    hidden_rows = pad_to(hidden, PACKED)
    held = []
    for name, depth in (
        ("sea_in", 3 * (surface + flux_count)),
        ("sea_hid", hidden_rows),
        ("air_in", 3 * (fields + surface)),
        ("hid1", hidden_rows),
        ("hid2", hidden_rows),
    ):
        held.append(pltpu.VMEM((depth, (ring + 2 * PADS[name]) * LANES), jnp.bfloat16))
    for depth in (fields, surface, fields):
        held.append(pltpu.VMEM((depth, ring * LANES), jnp.float32))
    held.append(pltpu.VMEM((ring, LANES), jnp.float32))
    cost = pl.CostEstimate(flops=2000000000, bytes_accessed=3000000, transcendentals=1000000)
    state = pl.pallas_call(
        functools.partial(forecast_kernel, sizes, 0),
        out_shape=tuple(held),
        in_specs=vmem_specs(blocks - 1 + 5),
        out_specs=tuple(vmem_specs(HELD)),
        cost_estimate=pl.CostEstimate(flops=1000, bytes_accessed=1000, transcendentals=0),
        compiler_params=pltpu.CompilerParams(vmem_limit_bytes=VMEM_GRANT),
        name="forecast_early",
    )(*in_vmem(*frame[1:], *weights))
    return pl.pallas_call(
        functools.partial(forecast_kernel, sizes, 1),
        out_shape=(pltpu.VMEM((fields + surface, rows, LANES), jnp.bfloat16), *held),
        in_specs=vmem_specs(1 + 5 + HELD),
        out_specs=tuple(vmem_specs(1 + HELD)),
        scratch_shapes=[pltpu.VMEM((fields + surface, rows, LANES), jnp.float32)],
        input_output_aliases={1 + 5 + i: 1 + i for i in range(HELD)},
        cost_estimate=cost,
        compiler_params=pltpu.CompilerParams(vmem_limit_bytes=VMEM_GRANT),
        name="forecast_late",
    )(*in_vmem(frame[0], *weights, *state))[0]


def belt_shards(
    atmosphere, ocean_state, fluxes, sea_mask, air_entry, air_middle, air_exit, sea_entry, sea_exit
):
    blocks = lax.axis_size("sp")
    fields, rows = atmosphere.shape[1:3]
    surface, flux_count = ocean_state.shape[1], fluxes.shape[1]
    hidden = air_middle.shape[3]
    kept = fields + surface + flux_count
    swap = [(0, 1), (1, 0)]
    bf16, f32 = jnp.bfloat16, jnp.float32

    got = lax.ppermute(atmosphere, "sec", swap)
    packed_shape = pltpu.VMEM((SUBLANES, (kept // SUBLANES * rows + 2) * LANES), bf16)
    small = pl.CostEstimate(flops=1000000, bytes_accessed=1000000, transcendentals=0)
    own = pl.pallas_call(
        pack_own_kernel,
        out_shape=packed_shape,
        in_specs=vmem_specs(4),
        out_specs=vmem_specs(1)[0],
        scratch_shapes=[pltpu.VMEM((kept, rows, LANES), f32)],
        cost_estimate=small,
        name="pack_own",
    )(atmosphere, ocean_state, fluxes, sea_mask)
    packed = pl.pallas_call(
        pack_got_kernel,
        out_shape=packed_shape,
        in_specs=vmem_specs(2),
        out_specs=vmem_specs(1)[0],
        scratch_shapes=[pltpu.VMEM((fields, rows, LANES), f32)],
        cost_estimate=small,
        name="pack_got",
    )(*in_vmem(own, got))

    weights = prepare_weights(sea_entry, sea_exit, air_entry, air_middle, air_exit)

    frame = [None] * blocks
    for index in range(blocks):
        shift = (1 - index) % blocks
        if shift == 0:
            frame[index] = packed
        else:
            pairs = [(i, (i + shift) % blocks) for i in range(blocks)]
            frame[index] = lax.ppermute(packed, "sp", pairs)

    sizes = (fields, surface, flux_count, hidden, blocks, rows)
    made = forecast(sizes, frame, weights)
    other = lax.ppermute(made, "sec", swap)
    return pl.pallas_call(
        merge_kernel,
        out_shape=(
            jax.ShapeDtypeStruct(atmosphere.shape, bf16),
            jax.ShapeDtypeStruct(ocean_state.shape, bf16),
        ),
        in_specs=vmem_specs(3),
        out_specs=tuple(vmem_specs(2)),
        cost_estimate=small,
        name="merge",
    )(*in_vmem(made, other, atmosphere))


def belt_fits(mesh, atmosphere, ocean_state, fluxes, sea_entry, sea_exit):
    sections, blocks = mesh.shape["sec"], mesh.shape["sp"]
    members = atmosphere.shape[0] // (mesh.shape["grp"] * mesh.shape["mb"])
    rows = atmosphere.shape[2] // blocks
    band = atmosphere.shape[3] // sections
    fields, surface, flux_count = atmosphere.shape[1], ocean_state.shape[1], fluxes.shape[1]
    return (
        sections == 2
        and members == 2
        and band == LANES
        and ocean_state.shape[3] == band
        and rows == SUBLANES
        and atmosphere.shape[1] <= LANES
        and 2 * rows + 9 <= blocks * rows
        and blocks * rows <= 64
        and all(c % SUBLANES == 0 for c in (fields, surface, flux_count, sea_entry.shape[3]))
        and (surface + flux_count) % PACKED == 0
        and (fields + surface) % PACKED == 0
    )


def solution(mesh):
    placed = (
        P(("grp", "mb"), None, "sp", "sec"),
        P(("grp", "mb"), None, "sp", None),
        P(("grp", "mb"), None, "sp", None),
        P("sp", None),
        P(),
        P(),
        P(),
        P(),
        P(),
    )

    def run(atmosphere, ocean_state, fluxes, sea_mask, air_entry, air_middle, air_exit, sea_entry, sea_exit):
        fits = belt_fits(mesh, atmosphere, ocean_state, fluxes, sea_entry, sea_exit)
        return jax.shard_map(
            belt_shards if fits else shards,
            mesh=mesh,
            in_specs=placed,
            out_specs=(P(("grp", "mb"), None, "sp", "sec"), P(("grp", "mb"), None, "sp", None)),
            check_vma=False,
        )(
            atmosphere, ocean_state, fluxes, sea_mask, air_entry, air_middle, air_exit, sea_entry, sea_exit
        )

    return run
```
